32 devices in a mesh: wide: 16 (over z, x, core), narrow: 2 (over y).
Axes of the slice: x: 2, y: 2, z: 4, core: 2. Of those that a mesh axis runs over, the one named last changes fastest.
Arguments:
- tokens_short: bfloat16 [32, 128, 768], P(('wide', 'narrow')), may hold values from -6 to 6
- tokens_long: bfloat16 [32, 512, 768], P(('wide', 'narrow')), may hold values from -6 to 6
- in_weight: bfloat16 [768, 2304], P('wide', 'narrow'), may hold values from -0.21875 to 0.21875
- in_bias: bfloat16 [2304], P(('wide', 'narrow')), may hold values from -2 to 2
- short_kernel: bfloat16 [3, 2304], P(None, ('wide', 'narrow')), may hold values from -3 to 3
- cond_kernel: bfloat16 [3, 768], P(None, ('wide', 'narrow')), may hold values from -3 to 3
- fourier_gain: bfloat16 [2, 768], P(None, ('wide', 'narrow')), may hold values from -4 to 4
- out_weight: bfloat16 [768, 768], P('wide', 'narrow'), may hold values from -0.21875 to 0.21875
- out_bias: bfloat16 [768], P(('wide', 'narrow')), may hold values from -2 to 2
- gain_first: bfloat16 [768], P(('wide', 'narrow')), may hold values from 0.099609375 to 1.8984375
- bias_first: bfloat16 [768], P(('wide', 'narrow')), may hold values from -2 to 2
- gain_second: bfloat16 [768], P(('wide', 'narrow')), may hold values from 0.099609375 to 1.8984375
- bias_second: bfloat16 [768], P(('wide', 'narrow')), may hold values from -2 to 2
- gate_weight: bfloat16 [768, 3072], P('wide', 'narrow'), may hold values from -0.21875 to 0.21875
- up_weight: bfloat16 [768, 3072], P('wide', 'narrow'), may hold values from -0.21875 to 0.21875
- glu_bias: bfloat16 [2, 3072], P(None, ('wide', 'narrow')), may hold values from -2 to 2
- down_weight: bfloat16 [3072, 768], P('wide', 'narrow'), may hold values from -0.109375 to 0.109375
- down_bias: bfloat16 [768], P(('wide', 'narrow')), may hold values from -2 to 2
- cotan_short: bfloat16 [32, 128, 768], P(('wide', 'narrow')), may hold values from -6 to 6
- cotan_long: bfloat16 [32, 512, 768], P(('wide', 'narrow')), may hold values from -6 to 6
Outputs:
- output_short: bfloat16 [32, 128, 768], P(('wide', 'narrow'))
- output_long: bfloat16 [32, 512, 768], P(('wide', 'narrow'))
- input_grad_short: float32 [32, 128, 768], P(('wide', 'narrow'))
- input_grad_long: float32 [32, 512, 768], P(('wide', 'narrow'))
- grad_in_weight: float32 [768, 2304], P('wide', 'narrow')
- grad_in_bias: float32 [2304], P(('wide', 'narrow'))
- grad_short_kernel: float32 [3, 2304], P(None, ('wide', 'narrow'))
- grad_cond_kernel: float32 [3, 768], P(None, ('wide', 'narrow'))
- grad_fourier_gain: float32 [2, 768], P(None, ('wide', 'narrow'))
- grad_out_weight: float32 [768, 768], P('wide', 'narrow')
- grad_out_bias: float32 [768], P(('wide', 'narrow'))
- grad_gain_first: float32 [768], P(('wide', 'narrow'))
- grad_bias_first: float32 [768], P(('wide', 'narrow'))
- grad_gain_second: float32 [768], P(('wide', 'narrow'))
- grad_bias_second: float32 [768], P(('wide', 'narrow'))
- grad_gate_weight: float32 [768, 3072], P('wide', 'narrow')
- grad_up_weight: float32 [768, 3072], P('wide', 'narrow')
- grad_glu_bias: float32 [2, 3072], P(None, ('wide', 'narrow'))
- grad_down_weight: float32 [3072, 768], P('wide', 'narrow')
- grad_down_bias: float32 [768], P(('wide', 'narrow'))
The draws below stay inside these ranges and needn't reach their ends.
All inputs are finite; a program needn't handle non-finite values.
Results may differ from the reference program's by a relative error of at most 0.017.
Values may be sent and summed in bfloat16 or wider, within the bound.
A program may use at most 192 MiB of HBM per device.

```python
import math
import jax
import jax.numpy as jnp
from jax import lax

D = 768
FF = 3072
LEN_A = 128
LEN_B = 512
SEQS_A = 32
SEQS_B = 32


def block_scale(key, shape, cuts, least, top_value):
    factor_of = 1.0
    for position, shards_of in cuts:
        heights = jax.random.uniform(jax.random.fold_in(jax.random.fold_in(key, 6), position), (shards_of,), jnp.float32, least / len(cuts), top_value / len(cuts))
        factor_of = factor_of * jnp.repeat(jnp.exp(heights), shape[position] // shards_of).reshape((-1,) + (1,) * (len(shape) - 1 - position))
    return factor_of


def gaussian(own_key, shape, scale, limit, cuts=(), dtype=jnp.bfloat16):
    result = scale * jax.random.normal(own_key, shape, jnp.float32)
    if cuts:
        result = result * block_scale(own_key, shape, cuts, -0.22, 0.18)
    return jnp.clip(result, -limit, limit).astype(dtype)


def setup_inputs(seed: int = 0) -> dict:
    splits = jax.random.split(jax.random.key(seed), 21)
    return {
        "tokens_short": gaussian(splits[0], (SEQS_A, LEN_A, D), 1.0, 6.0, ((0, 32),)),
        "tokens_long": gaussian(splits[1], (SEQS_B, LEN_B, D), 1.0, 6.0, ((0, 32),)),
        "in_weight": gaussian(splits[2], (D, 3 * D), D ** -0.5, 0.21875, ((0, 16), (1, 2))),
        "in_bias": gaussian(splits[3], (3 * D,), 0.3, 2.0, ((0, 32),)),
        "short_kernel": gaussian(splits[4], (3, 3 * D), 0.5, 3.0, ((1, 32),)),
        "cond_kernel": gaussian(splits[5], (3, D), 0.5, 3.0, ((1, 32),)),
        "fourier_gain": gaussian(splits[6], (2, D), 1.0, 4.0, ((1, 32),)),
        "out_weight": gaussian(splits[7], (D, D), D ** -0.5, 0.21875, ((0, 16), (1, 2))),
        "out_bias": gaussian(splits[8], (D,), 0.3, 2.0, ((0, 32),)),
        "gain_first": jnp.clip(1.0 + 0.18 * jax.random.normal(splits[9], (D,), jnp.float32), 0.099609375, 1.8984375).astype(jnp.bfloat16),
        "bias_first": gaussian(splits[10], (D,), 0.3, 2.0, ((0, 32),)),
        "gain_second": jnp.clip(1.0 + 0.18 * jax.random.normal(splits[11], (D,), jnp.float32), 0.099609375, 1.8984375).astype(jnp.bfloat16),
        "bias_second": gaussian(splits[12], (D,), 0.3, 2.0, ((0, 32),)),
        "gate_weight": gaussian(splits[13], (D, FF), D ** -0.5, 0.21875, ((0, 16), (1, 2))),
        "up_weight": gaussian(splits[14], (D, FF), D ** -0.5, 0.21875, ((0, 16), (1, 2))),
        "glu_bias": gaussian(splits[15], (2, FF), 0.3, 2.0, ((1, 32),)),
        "down_weight": gaussian(splits[16], (FF, D), FF ** -0.5, 0.109375, ((0, 16), (1, 2))),
        "down_bias": gaussian(splits[17], (D,), 0.3, 2.0, ((0, 32),)),
        "cotan_short": gaussian(splits[18], (SEQS_A, LEN_A, D), 1.0, 6.0, ((0, 32),)),
        "cotan_long": gaussian(splits[19], (SEQS_B, LEN_B, D), 1.0, 6.0, ((0, 32),)),
    }


eps = 1e-05

@jax.custom_vjp
def low(v):
    return lax.optimization_barrier(v.astype(jnp.bfloat16)).astype(jnp.float32)

@jax.custom_vjp
def low_back(v):
    return v

def low_keep(v):
    return (low(v), None)

def low_pass(kept, grad):
    return (grad,)

def back_keep(v):
    return (v, None)

def back_low(kept, grad):
    return (low(grad),)
low.defvjp(low_keep, low_pass)
low_back.defvjp(back_keep, back_low)

def layer_norm(values, gain_vec, bias_vec):
    centre = lax.optimization_barrier(jnp.mean(values, axis=-1, keepdims=True))
    centred = values - centre
    spread = lax.optimization_barrier(jnp.mean(centred * centred, axis=-1, keepdims=True))
    return centred * lax.rsqrt(spread + eps) * gain_vec + bias_vec

def shift_down(values):
    return jnp.pad(values[:, :-1], ((0, 0), (1, 0), (0, 0)))

def shift_up(values):
    return jnp.pad(values[:, 1:], ((0, 0), (0, 1), (0, 0)))

def short_conv(values, kernel):
    return kernel[0] * shift_down(values) + kernel[1] * values + kernel[2] * shift_up(values)

def product(left_mat, right_mat):
    return jnp.dot(left_mat, right_mat, precision=lax.Precision.HIGHEST)

def mixer(projected, short_kernel, cond_kernel, fourier_gain):
    model_width = cond_kernel.shape[1]
    conv_out = short_conv(projected, short_kernel)
    gate_left = conv_out[:, :, :model_width]
    gate_right = conv_out[:, :, model_width:2 * model_width]
    values = conv_out[:, :, 2 * model_width:]
    conditioned = short_conv(values, cond_kernel)
    spectrum = jnp.fft.fft(conditioned, axis=1, norm='ortho')
    filt_real = jnp.tanh(jnp.real(spectrum) * fourier_gain[0]) * fourier_gain[1]
    filt_imag = jnp.tanh(jnp.imag(spectrum) * fourier_gain[0]) * fourier_gain[1]
    filt = lax.complex(filt_real, filt_imag)
    carried = jnp.fft.fft(gate_right * values, axis=1, norm='ortho')
    long_conv = jnp.real(jnp.fft.ifft(filt * carried, axis=1, norm='ortho'))
    return gate_left * long_conv

def block_forward(params, blocks):
    in_weight, in_bias, short_kernel, cond_kernel, fourier_gain, out_weight, out_bias, gain_first, bias_first, gain_second, bias_second, gate_weight, up_weight, glu_bias, down_weight, down_bias = params
    seq_count, seq_length, model_width = blocks.shape
    flat_rows = blocks.reshape(seq_count * seq_length, model_width)
    normed_one = low(layer_norm(flat_rows, gain_first, bias_first))
    projected = low_back(product(normed_one, in_weight) + in_bias)
    mixed_out = mixer(projected.reshape(seq_count, seq_length, 3 * model_width), short_kernel, cond_kernel, fourier_gain)
    branch_one = low_back(product(low(mixed_out.reshape(-1, model_width)), out_weight) + out_bias)
    hidden_one = flat_rows + branch_one
    normed_two = low(layer_norm(hidden_one, gain_second, bias_second))
    gate_pre = low_back(product(normed_two, gate_weight) + glu_bias[0])
    up_pre = low_back(product(normed_two, up_weight) + glu_bias[1])
    glu_act = low(jax.nn.gelu(gate_pre) * up_pre)
    branch_two = low_back(product(glu_act, down_weight) + down_bias)
    return (hidden_one + branch_two).reshape(seq_count, seq_length, model_width)

def run_group(params, tokens):
    seq_total, seq_length, model_width = tokens.shape
    per_block = math.gcd(seq_total, max(1, 4096 // seq_length))
    blocks = tokens.reshape(seq_total // per_block, per_block, seq_length, model_width)

    def one_block(block_rows):
        return block_forward(params, block_rows)
    results = lax.map(jax.checkpoint(one_block), blocks)
    return results.reshape(seq_total, seq_length, model_width)

def reference(tokens_short, tokens_long, in_weight, in_bias, short_kernel, cond_kernel, fourier_gain, out_weight, out_bias, gain_first, bias_first, gain_second, bias_second, gate_weight, up_weight, glu_bias, down_weight, down_bias, cotan_short, cotan_long):
    params = (in_weight.astype(jnp.float32), in_bias.astype(jnp.float32), short_kernel.astype(jnp.float32), cond_kernel.astype(jnp.float32), fourier_gain.astype(jnp.float32), out_weight.astype(jnp.float32), out_bias.astype(jnp.float32), gain_first.astype(jnp.float32), bias_first.astype(jnp.float32), gain_second.astype(jnp.float32), bias_second.astype(jnp.float32), gate_weight.astype(jnp.float32), up_weight.astype(jnp.float32), glu_bias.astype(jnp.float32), down_weight.astype(jnp.float32), down_bias.astype(jnp.float32))

    def forward(param_set, short_rows, long_rows):
        return (run_group(param_set, short_rows), run_group(param_set, long_rows))
    results, pullback = jax.vjp(forward, params, tokens_short.astype(jnp.float32), tokens_long.astype(jnp.float32))
    grads, grad_short, grad_long = pullback((cotan_short.astype(jnp.float32), cotan_long.astype(jnp.float32)))
    return (results[0].astype(jnp.bfloat16), results[1].astype(jnp.bfloat16), grad_short, grad_long, grads[0], grads[1], grads[2], grads[3], grads[4], grads[5], grads[6], grads[7], grads[8], grads[9], grads[10], grads[11], grads[12], grads[13], grads[14], grads[15])
```

```python
import functools
import math

import jax
import jax.numpy as jnp
import numpy as np
from jax import lax
from jax.experimental import pallas as pl
from jax.experimental.pallas import tpu as pltpu
from jax.sharding import PartitionSpec as P

bf16 = jnp.bfloat16
f32 = jnp.float32
MESH = pl.DeviceIdType.MESH
Z, X, C, Y = 4, 2, 2, 2


def coords():
    w = lax.axis_index("wide")
    y = lax.axis_index("narrow")
    return w // 4, (w // 2) % 2, w % 2, y


def flat(z, x, c):
    return (z * 2 + x) * 2 + c


def gather_kernel(n, *refs):
    shards = refs[:n]
    fulls = refs[n : 2 * n]
    ici_send, ici_recv, core_send, core_recv, own_sem = refs[2 * n :]
    z, x, c, y = coords()
    barrier = pltpu.get_barrier_semaphore()
    peers = [(flat(lax.rem(z + i, Z), x, c), y) for i in (1, 2, 3)]
    peers += [(flat(z, 1 - x, c), y), (flat(z, x, c), 1 - y), (flat(z, x, 1 - c), y)]
    for peer in peers:
        pl.semaphore_signal(barrier, inc=1, device_id=peer, device_id_type=MESH)
    pl.semaphore_wait(barrier, len(peers))
    xpeer, ypeer, cpeer = peers[3], peers[4], peers[5]

    def window(k, i, xf, yf, cf=0):
        zz = lax.rem(z + i, Z)
        xx = 1 - x if xf else x
        yy = 1 - y if yf else y
        cc = 1 - c if cf else c
        wide = shards[k].shape[1]
        return fulls[k].at[flat(zz, xx, cc), :, pl.ds(pl.multiple_of(yy * wide, 128), wide)]

    pending = []
    count = [0] * n

    def send(k, i, xf, yf, dst, slot):
        src = shards[k] if (i, xf, yf) == (0, 0, 0) else window(k, i, xf, yf)
        copy = pltpu.make_async_remote_copy(
            src_ref=src,
            dst_ref=window(k, i, xf, yf),
            send_sem=ici_send.at[k, count[k]],
            recv_sem=ici_recv.at[k, slot],
            device_id=dst,
            device_id_type=MESH,
        )
        count[k] += 1
        copy.start()
        pending.append(copy)

    def to_core(k, i, xf, yf):
        slot = i * 4 + xf * 2 + yf
        src = shards[k] if (i, xf, yf) == (0, 0, 0) else window(k, i, xf, yf)
        copy = pltpu.make_async_remote_copy(
            src_ref=src,
            dst_ref=window(k, i, xf, yf),
            send_sem=core_send.at[k, slot],
            recv_sem=core_recv.at[k, slot],
            device_id=cpeer,
            device_id_type=MESH,
        )
        copy.start()
        pending.append(copy)

    def arrived(k, i, xf, yf):
        slot = i * 4 + xf * 2 + yf
        pltpu.make_async_remote_copy(
            src_ref=shards[k], dst_ref=window(k, i, xf, yf), send_sem=ici_send.at[k, 0],
            recv_sem=ici_recv.at[k, slot], device_id=cpeer, device_id_type=MESH,
        ).wait_recv()

    def core_arrived(k, i, xf, yf):
        slot = i * 4 + xf * 2 + yf
        pltpu.make_async_remote_copy(
            src_ref=shards[k], dst_ref=window(k, i, xf, yf, 1), send_sem=ici_send.at[k, 0],
            recv_sem=core_recv.at[k, slot], device_id=cpeer, device_id_type=MESH,
        ).wait_recv()

    own = []
    for k in range(n):
        copy = pltpu.make_async_copy(shards[k], window(k, 0, 0, 0), own_sem.at[k])
        copy.start()
        own.append(copy)

    def start(k):
        for i in (1, 3, 2):
            send(k, 0, 0, 0, peers[i - 1], ((Z - i) % Z) * 4)
        send(k, 0, 0, 0, xpeer, 2)
        send(k, 0, 0, 0, ypeer, 1)
        to_core(k, 0, 0, 0)

    def zstep(k):
        for i in (1, 3, 2):
            arrived(k, i, 0, 0)
            send(k, i, 0, 0, xpeer, i * 4 + 2)
            send(k, i, 0, 0, ypeer, i * 4 + 1)
            to_core(k, i, 0, 0)

    def xystep(k):
        for i in (0, 1, 3, 2):
            arrived(k, i, 1, 0)
            if i % 2 == 0:
                send(k, i, 1, 0, ypeer, i * 4 + 3)
            to_core(k, i, 1, 0)
            arrived(k, i, 0, 1)
            if i % 2 == 1:
                send(k, i, 0, 1, xpeer, i * 4 + 3)
            to_core(k, i, 0, 1)

    def dstep(k):
        for i in (0, 1, 3, 2):
            arrived(k, i, 1, 1)
            to_core(k, i, 1, 1)

    start(0)
    for k in range(n + 2):
        if k + 1 < n:
            start(k + 1)
        if k < n:
            zstep(k)
        if 0 <= k - 1 < n:
            xystep(k - 1)
        if 0 <= k - 2 < n:
            dstep(k - 2)
    for k in range(n):
        for i in range(4):
            for xf in range(2):
                for yf in range(2):
                    core_arrived(k, i, xf, yf)
    for copy in pending:
        copy.wait_send()
    for copy in own:
        copy.wait()


def gather(shards, cid=0):
    n = len(shards)
    outs = [jax.ShapeDtypeStruct((16, s.shape[0], 2 * s.shape[1]), s.dtype) for s in shards]
    return pl.pallas_call(
        functools.partial(gather_kernel, n),
        out_shape=outs,
        in_specs=[pl.BlockSpec(memory_space=pl.ANY)] * n,
        out_specs=[pl.BlockSpec(memory_space=pl.ANY)] * n,
        scratch_shapes=[
            pltpu.SemaphoreType.DMA((n, 15)),
            pltpu.SemaphoreType.DMA((n, 16)),
            pltpu.SemaphoreType.DMA((n, 16)),
            pltpu.SemaphoreType.DMA((n, 16)),
            pltpu.SemaphoreType.DMA((n,)),
        ],
        compiler_params=pltpu.CompilerParams(collective_id=cid, has_side_effects=True),
    )(*shards)


def reduce_kernel(n, *refs):
    parts = refs[:n]
    outs = refs[n : 2 * n]
    pos = 2 * n
    held = refs[pos : pos + n]; pos += n
    from_core = refs[pos : pos + n]; pos += n
    diag_x = refs[pos : pos + n]; pos += n
    diag_y = refs[pos : pos + n]; pos += n
    near_x = refs[pos : pos + n]; pos += n
    near_y = refs[pos : pos + n]; pos += n
    far_z = refs[pos : pos + n]; pos += n
    own_sem, send_sem, recv_sem = refs[pos:]
    z, x, c, y = coords()
    barrier = pltpu.get_barrier_semaphore()
    zpeers = [(flat(lax.rem(z + i, Z), x, c), y) for i in (1, 2, 3)]
    xpeer, ypeer, cpeer = (flat(z, 1 - x, c), y), (flat(z, x, c), 1 - y), (flat(z, x, 1 - c), y)
    peers = zpeers + [xpeer, ypeer, cpeer]
    for peer in peers:
        pl.semaphore_signal(barrier, inc=1, device_id=peer, device_id_type=MESH)
    pl.semaphore_wait(barrier, len(peers))

    started = [[] for _ in range(n)]
    pending = []

    def post(k, src, dst, peer, slot):
        copy = pltpu.make_async_remote_copy(
            src_ref=src, dst_ref=dst, send_sem=send_sem.at[k, slot], recv_sem=recv_sem.at[k, slot],
            device_id=peer, device_id_type=MESH)
        copy.start()
        pending.append(copy)

    def arrived(k, dst, slot):
        pltpu.make_async_remote_copy(
            src_ref=dst, dst_ref=dst, send_sem=send_sem.at[k, slot], recv_sem=recv_sem.at[k, slot],
            device_id=cpeer, device_id_type=MESH).wait_recv()

    def cols(k, yy):
        wide = outs[k].shape[1]
        return pl.ds(pl.multiple_of(yy * wide, 128), wide)

    def zrow(i, xx):
        return lax.rem(z + i, Z) * 2 + xx

    def stage_core(k):
        for i in range(8):
            pltpu.make_async_copy(parts[k].at[2 * i + c], held[k].at[i], own_sem.at[k, i]).start()
        for i in range(8):
            post(k, parts[k].at[2 * i + 1 - c], from_core[k].at[i], cpeer, i)

    def stage_diag(k):
        for i in range(8):
            pltpu.make_async_copy(parts[k].at[2 * i + c], held[k].at[i], own_sem.at[k, i]).wait()
        for i in range(8):
            arrived(k, from_core[k].at[i], i)
        for i in range(4):
            b = zrow(i, 1 - x)
            held[k][b] = held[k][b] + from_core[k][b]
            src = held[k].at[b, :, cols(k, 1 - y)]
            if i % 2 == 0:
                post(k, src, diag_x[k].at[i // 2], xpeer, 8 + i // 2)
            else:
                post(k, src, diag_y[k].at[i // 2], ypeer, 10 + i // 2)
        for i in range(4):
            b = zrow(i, x)
            held[k][b] = held[k][b] + from_core[k][b]

    def stage_near(k):
        for i in range(4):
            b = zrow(i, x)
            if i % 2 == 0:
                arrived(k, diag_x[k].at[i // 2], 8 + i // 2)
                held[k][b, :, cols(k, 1 - y)] = held[k][b, :, cols(k, 1 - y)] + diag_x[k][i // 2]
            post(k, held[k].at[b, :, cols(k, 1 - y)], near_y[k].at[i], ypeer, 12 + i)
            b = zrow(i, 1 - x)
            if i % 2 == 1:
                arrived(k, diag_y[k].at[i // 2], 10 + i // 2)
                held[k][b, :, cols(k, y)] = held[k][b, :, cols(k, y)] + diag_y[k][i // 2]
            post(k, held[k].at[b, :, cols(k, y)], near_x[k].at[i], xpeer, 16 + i)

    def stage_far(k):
        for i in (1, 2, 3, 0):
            b = zrow(i, x)
            arrived(k, near_x[k].at[i], 16 + i)
            arrived(k, near_y[k].at[i], 12 + i)
            held[k][b, :, cols(k, y)] = (
                held[k][b, :, cols(k, y)].astype(jnp.float32)
                + near_x[k][i].astype(jnp.float32) + near_y[k][i].astype(jnp.float32)
            ).astype(held[k].dtype)
            if i:
                post(k, held[k].at[b, :, cols(k, y)], far_z[k].at[i - 1], zpeers[i - 1], 19 + i)

    def stage_last(k):
        total = held[k][zrow(0, x), :, cols(k, y)].astype(jnp.float32)
        for i in range(3):
            arrived(k, far_z[k].at[i], 20 + i)
            total = total + far_z[k][i].astype(jnp.float32)
        outs[k][...] = total

    for k in range(n):
        stage_core(k)
    for t in range(n + 3):
        if t < n: stage_diag(t)
        if 0 <= t - 1 < n: stage_near(t - 1)
        if 0 <= t - 2 < n: stage_far(t - 2)
        if 0 <= t - 3 < n: stage_last(t - 3)
    for copy in pending:
        copy.wait_send()


def reduce(parts, cid=1):
    n = len(parts)
    rc = [(p.shape[1], p.shape[2] // 2) for p in parts]
    dt = [p.dtype for p in parts]
    V = pltpu.VMEM
    scratch = (
        [V((8, r, 2 * c), d) for (r, c), d in zip(rc, dt)]
        + [V((8, r, 2 * c), d) for (r, c), d in zip(rc, dt)]
        + [V((2, r, c), d) for (r, c), d in zip(rc, dt)]
        + [V((2, r, c), d) for (r, c), d in zip(rc, dt)]
        + [V((4, r, c), d) for (r, c), d in zip(rc, dt)]
        + [V((4, r, c), d) for (r, c), d in zip(rc, dt)]
        + [V((3, r, c), d) for (r, c), d in zip(rc, dt)]
        + [pltpu.SemaphoreType.DMA((n, 8)), pltpu.SemaphoreType.DMA((n, 23)), pltpu.SemaphoreType.DMA((n, 23))]
    )
    return pl.pallas_call(
        functools.partial(reduce_kernel, n),
        out_shape=[jax.ShapeDtypeStruct(s, jnp.float32) for s in rc],
        in_specs=[pl.BlockSpec(memory_space=pl.ANY)] * n,
        out_specs=[pl.BlockSpec(memory_space=pltpu.VMEM)] * n,
        scratch_shapes=scratch,
        compiler_params=pltpu.CompilerParams(collective_id=cid, has_side_effects=True, vmem_limit_bytes=64000 * 1024),
    )(*parts)
def table(length):
    half = length // 2
    t = np.arange(length)
    k = np.arange(half)
    ang = 2.0 * np.pi * (np.outer(k, t) % length) / length
    top = np.cos(ang)
    low = -np.sin(ang)
    low[0] = np.where(t % 2 == 0, 1.0, -1.0)
    return (np.concatenate([top, low]) / math.sqrt(length)).astype(np.float32)

def split(v):
    hi = v.astype(bf16)
    return hi, (v - hi.astype(f32)).astype(bf16)

def dft(form, tab, v, passes):
    th, tl = split(jnp.asarray(tab));
    vh, vl = split(v)
    e = lambda a, b: jnp.einsum(form, a, b, preferred_element_type=f32)
    out = e(th, vh)
    if passes >= 2: out = out + e(th, vl)
    if passes >= 3: out = out + e(tl, vh)
    return out

def down(v): return jnp.pad(v[:, :-1], ((0,0),(1,0),(0,0)))
def up(v): return jnp.pad(v[:, 1:], ((0,0),(0,1),(0,0)))
def conv(v, k): return k[0]*down(v)+k[1]*v+k[2]*up(v)
def conv_back(g, k): return k[0]*up(g)+k[1]*g+k[2]*down(g)
def conv_kernel(g, v):
    return jnp.stack([jnp.sum(g*down(v),(0,1)), jnp.sum(g*v,(0,1)), jnp.sum(g*up(v),(0,1))])

def weights(length):
    half = length//2
    w = np.full((half,1),2.0,np.float32); w[0]=1.0
    return np.concatenate([w,w])

def mixer_fwd(proj, sk, ck, fg):
    D = ck.shape[1]; L = proj.shape[1]; H=L//2
    tab = table(L); w = weights(L)
    co = conv(proj, sk)
    gl, gr, va = co[:,:,:D], co[:,:,D:2*D], co[:,:,2*D:]
    cond = conv(va, ck)
    spec = dft("kt,btc->bkc", tab, cond, 1)
    carr = dft("kt,btc->bkc", tab, gr*va, 1)
    th = jnp.tanh(spec*fg[0]); filt = th*fg[1]
    first = (lax.broadcasted_iota(jnp.int32,(H,1),0)==0)
    fa, fb, ca, cb = filt[:,:H], filt[:,H:], carr[:,:H], carr[:,H:]
    pa = fa*ca - jnp.where(first,0.0,fb*cb)
    pb = jnp.where(first, fb*cb, fa*cb+fb*ca)
    prod = jnp.concatenate([pa,pb],1)*w
    longc = dft("kt,bkc->btc", tab, prod, 1)
    return gl*longc, (co, spec, th, carr, longc)

def mixer_bwd(dmix, proj, res, sk, ck, fg):
    co, spec, th, carr, longc = res
    D = ck.shape[1]; L = proj.shape[1]; H=L//2
    tab = table(L); w = weights(L)
    gl, gr, va = co[:,:,:D], co[:,:,D:2*D], co[:,:,2*D:]
    dgl = dmix*longc
    dlong = dmix*gl
    dp = dft("kt,btc->bkc", tab, dlong, 1)*w
    filt = th*fg[1]
    first = (lax.broadcasted_iota(jnp.int32,(H,1),0)==0)
    fa, fb, ca, cb = filt[:,:H], filt[:,H:], carr[:,:H], carr[:,H:]
    da, db = dp[:,:H], dp[:,H:]
    dfa = da*ca + jnp.where(first,0.0,db*cb)
    dfb = jnp.where(first, db*cb, db*ca-da*cb)
    dca = da*fa + jnp.where(first,0.0,db*fb)
    dcb = jnp.where(first, db*fb, db*fa-da*fb)
    df = jnp.concatenate([dfa,dfb],1); dc = jnp.concatenate([dca,dcb],1)
    dth = df*fg[1]*(1-th*th)
    dfg = jnp.stack([jnp.sum(dth*spec,(0,1)), jnp.sum(df*th,(0,1))])
    dcond = dft("kt,bkc->btc", tab, dth*fg[0], 1)
    dgv = dft("kt,bkc->btc", tab, dc, 1)
    dck = conv_kernel(dcond, va)
    dva = conv_back(dcond, ck) + dgv*gr
    dgr = dgv*va
    dco = jnp.concatenate([dgl,dgr,dva],2)
    dsk = conv_kernel(dco, proj)
    return conv_back(dco, sk), dsk, dck, dfg

def mm(a,b): return jnp.dot(a,b,preferred_element_type=f32)
def tn(a,b): return lax.dot_general(a,b,(((0,),(0,)),((),())),preferred_element_type=f32)
def nt(a,b): return lax.dot_general(a,b,(((1,),(1,)),((),())),preferred_element_type=f32)

def norm(v):
    m = jnp.mean(v,-1,keepdims=True); d = v-m
    r = lax.rsqrt(jnp.mean(d*d,-1,keepdims=True)+1e-5)
    return d*r, r

def norm_back(e, h, r):
    return r*(e-jnp.mean(e,-1,keepdims=True)-h*jnp.mean(e*h,-1,keepdims=True))

C0=math.sqrt(2/math.pi); C1=0.044715
def gelu_parts(g):
    t = jnp.tanh(C0*(g+C1*g*g*g))
    return 0.5*g*(1+t), 0.5*(1+t)+0.5*g*(1-t*t)*C0*(1+3*C1*g*g)

def local(ts, tl, P, cs, cl):
    (iw, ib, sk, ck, fg, ow, ob, g1, b1, g2, b2, gw, uw, gb, dw, db) = [p if i in (0,5,11,12,14) else p.astype(f32) for i,p in enumerate(P)]
    D = ow.shape[0]
    ns = ts.shape[0]*ts.shape[1]
    x = jnp.concatenate([ts.reshape(-1,D),tl.reshape(-1,D)]).astype(f32)
    c = jnp.concatenate([cs.reshape(-1,D),cl.reshape(-1,D)])
    h1, r1 = norm(x)
    n1 = (h1*g1+b1).astype(bf16)
    proj = mm(n1, iw)+ib
    ps, pl_ = proj[:ns].reshape(ts.shape[0],ts.shape[1],3*D), proj[ns:].reshape(tl.shape[0],tl.shape[1],3*D)
    ms, rs = mixer_fwd(ps, sk, ck, fg); ml, rl = mixer_fwd(pl_, sk, ck, fg)
    mixed = jnp.concatenate([ms.reshape(-1,D),ml.reshape(-1,D)]).astype(bf16)
    hid = x + mm(mixed, ow)+ob
    h2, r2 = norm(hid)
    n2 = (h2*g2+b2).astype(bf16)
    gp = mm(n2,gw)+gb[0]; up_ = mm(n2,uw)+gb[1]
    ge, gd = gelu_parts(gp)
    ga = (ge*up_).astype(bf16)
    out = (hid+mm(ga,dw)+db).astype(bf16)
    cf = c.astype(f32)
    d_db = jnp.sum(cf,0); d_dw = tn(ga,c)
    dg = nt(c,dw)
    dgate = (dg*up_*gd).astype(bf16); dup=(dg*ge).astype(bf16)
    d_gb = jnp.stack([jnp.sum(dgate.astype(f32),0),jnp.sum(dup.astype(f32),0)])
    d_gw = tn(n2,dgate); d_uw = tn(n2,dup)
    dn2 = nt(dgate,gw)+nt(dup,uw)
    d_g2 = jnp.sum(dn2*h2,0); d_b2=jnp.sum(dn2,0)
    dh = cf + norm_back(dn2*g2,h2,r2)
    gm = dh.astype(bf16)
    d_ob = jnp.sum(gm.astype(f32),0); d_ow = tn(mixed,gm)
    dm = nt(gm,ow)
    dps, a1,a2,a3 = mixer_bwd(dm[:ns].reshape(ts.shape), ps, rs, sk, ck, fg)
    dpl, e1,e2,e3 = mixer_bwd(dm[ns:].reshape(tl.shape), pl_, rl, sk, ck, fg)
    gpj = jnp.concatenate([dps.reshape(-1,3*D),dpl.reshape(-1,3*D)]).astype(bf16)
    d_ib = jnp.sum(gpj.astype(f32),0); d_iw = tn(n1,gpj)
    dn1 = nt(gpj,iw)
    d_g1=jnp.sum(dn1*h1,0); d_b1=jnp.sum(dn1,0)
    dx = dh + norm_back(dn1*g1,h1,r1)
    return (out[:ns].reshape(ts.shape), out[ns:].reshape(tl.shape), dx[:ns].reshape(ts.shape), dx[ns:].reshape(tl.shape),
        d_iw,d_ib,a1+e1,a2+e2,a3+e3,d_ow,d_ob,d_g1,d_b1,d_g2,d_b2,d_gw,d_uw,d_gb,d_dw,d_db)


SMALL = (1, 2, 3, 4, 6, 7, 8, 9, 10, 13, 15)
LARGE = (0, 5, 11, 12, 14)


def pack_small(shards, rows, lanes, dtype):
    joined = jnp.concatenate([shards[i].reshape(-1).astype(dtype) for i in SMALL])
    return jnp.pad(joined, (0, rows * lanes - joined.size)).reshape(rows, lanes)


def fetch_ring(shards):
    small = pack_small(shards, 16, 128, bf16)
    fulls = gather([small] + [shards[i] for i in LARGE])
    params = [None] * 16
    for i, full in zip(LARGE, fulls[1:]):
        params[i] = full.reshape(-1, full.shape[-1])
    flat_small = fulls[0].reshape(16, 16, 2, 128).transpose(0, 2, 1, 3).reshape(32, 2048)
    start = 0
    for i in SMALL:
        shard = shards[i]
        piece = flat_small[:, start : start + shard.size]
        start += shard.size
        if shard.ndim == 1:
            params[i] = piece.reshape(-1)
        else:
            rows, width = shard.shape
            params[i] = piece.reshape(32, rows, width).transpose(1, 0, 2).reshape(rows, 32 * width)
    return params


def reduce_ring(grads, shards):
    pieces = []
    for i in SMALL:
        grad = grads[i]
        if grad.ndim == 1:
            pieces.append(grad.reshape(32, -1))
        else:
            rows = grad.shape[0]
            pieces.append(grad.reshape(rows, 32, -1).transpose(1, 0, 2).reshape(32, -1))
    joined = jnp.concatenate(pieces, axis=1)
    joined = jnp.pad(joined, ((0, 0), (0, 1024 - joined.shape[1])))
    small = joined.reshape(16, 2, 8, 128).transpose(0, 2, 1, 3).reshape(16, 8, 256)
    parts = [grads[i].reshape(16, -1, grads[i].shape[-1]) for i in (14, 11, 12, 5, 0)]
    sums = reduce([small] + [part.astype(bf16) for part in parts])
    outs = [None] * 16
    for i, total in zip((14, 11, 12, 5, 0), sums[1:]):
        outs[i] = total
    flat_small = sums[0].reshape(-1)
    start = 0
    for i in SMALL:
        shard = shards[i]
        outs[i] = flat_small[start : start + shard.size].reshape(shard.shape)
        start += shard.size
    return outs


def fetch_plain(shards):
    params = []
    for i, shard in enumerate(shards):
        if i in LARGE:
            wide = lax.all_gather(shard, "narrow", axis=1, tiled=True)
            params.append(lax.all_gather(wide, "wide", axis=0, tiled=True))
        else:
            params.append(
                lax.all_gather(shard, ("wide", "narrow"), axis=shard.ndim - 1, tiled=True)
            )
    return params


def reduce_plain(grads, shards):
    outs = []
    for i, grad in enumerate(grads):
        if i in LARGE:
            block = lax.psum_scatter(grad.astype(bf16), "wide", scatter_dimension=0, tiled=True)
            block = lax.psum_scatter(block, "narrow", scatter_dimension=1, tiled=True)
            outs.append(block.astype(f32))
        else:
            outs.append(
                lax.psum_scatter(
                    grad, ("wide", "narrow"), scatter_dimension=grad.ndim - 1, tiled=True
                )
            )
    return outs


def body(ring, ts, tl, *rest):
    shards, cs, cl = rest[:16], rest[16], rest[17]
    params = fetch_ring(shards) if ring else fetch_plain(shards)
    results = local(ts, tl, params, cs, cl)
    grads = reduce_ring(results[4:], shards) if ring else reduce_plain(results[4:], shards)
    return tuple(results[:4]) + tuple(grads)


def solution(mesh):
    ring = mesh.shape["wide"] == 16 and mesh.shape["narrow"] == 2
    seq = P(("wide", "narrow"), None, None)
    mat = P("wide", "narrow")
    vec = P(("wide", "narrow"))
    pair = P(None, ("wide", "narrow"))
    params = (mat, vec, pair, pair, pair, mat, vec, vec, vec, vec, vec, mat, mat, pair, mat, vec)
    return jax.shard_map(
        functools.partial(body, ring),
        mesh=mesh,
        in_specs=(seq, seq) + params + (seq, seq),
        out_specs=(seq, seq, seq, seq) + params,
        check_vma=False,
    )
```

```python
import functools
import math

import jax
import jax.numpy as jnp
import numpy as np
from jax import lax
from jax.experimental import pallas as pl
from jax.experimental.pallas import tpu as pltpu
from jax.sharding import PartitionSpec as P

bf16 = jnp.bfloat16
f32 = jnp.float32
MESH = pl.DeviceIdType.MESH
Z = 4
D = 768
BLK = 256
PAD = 8


def coords():
    w = lax.axis_index("wide")
    return w // 4, (w // 2) % 2, w % 2, lax.axis_index("narrow")


def flat(z, x, c):
    return (z * 2 + x) * 2 + c


def window(ref, rows, cols, w, y):
    return ref.at[
        pl.ds(pl.multiple_of(w * rows, 16), rows), pl.ds(pl.multiple_of(y * cols, 128), cols)
    ]


def greet(peers):
    barrier = pltpu.get_barrier_semaphore()
    for peer in peers:
        pl.semaphore_signal(barrier, inc=1, device_id=peer, device_id_type=MESH)
    pl.semaphore_wait(barrier, len(peers))


def neighbours():
    z, x, c, y = coords()
    zpeers = [(flat(lax.rem(z + i, Z), x, c), y) for i in (1, 2, 3)]
    return zpeers, (flat(z, 1 - x, c), y), (flat(z, x, c), 1 - y), (flat(z, x, 1 - c), y)


class Gather:
    def __init__(self, shards, fulls, ici_send, ici_recv, core_send, core_recv, own_sem):
        self.shards, self.fulls = shards, fulls
        self.ici_send, self.ici_recv = ici_send, ici_recv
        self.core_send, self.core_recv, self.own_sem = core_send, core_recv, own_sem
        self.z, self.x, self.c, self.y = coords()
        self.zpeers, self.xpeer, self.ypeer, self.cpeer = neighbours()
        self.count = [0] * len(shards)
        self.pending = []

    def view(self, k, i, xf, yf, cf=0):
        zz = lax.rem(self.z + i, Z)
        xx = 1 - self.x if xf else self.x
        yy = 1 - self.y if yf else self.y
        cc = 1 - self.c if cf else self.c
        rows, cols = self.shards[k].shape
        return window(self.fulls[k], rows, cols, flat(zz, xx, cc), yy)

    def source(self, k, i, xf, yf):
        return self.shards[k] if (i, xf, yf) == (0, 0, 0) else self.view(k, i, xf, yf)

    def post(self, k, i, xf, yf, peer, send, recv):
        copy = pltpu.make_async_remote_copy(
            src_ref=self.source(k, i, xf, yf),
            dst_ref=self.view(k, i, xf, yf),
            send_sem=send,
            recv_sem=recv,
            device_id=peer,
            device_id_type=MESH,
        )
        copy.start()
        self.pending.append(copy)

    def send(self, k, i, xf, yf, peer, slot):
        self.post(k, i, xf, yf, peer, self.ici_send.at[k, self.count[k]], self.ici_recv.at[k, slot])
        self.count[k] += 1

    def to_core(self, k, i, xf, yf):
        slot = i * 4 + xf * 2 + yf
        self.post(k, i, xf, yf, self.cpeer, self.core_send.at[k, slot], self.core_recv.at[k, slot])

    def arrived(self, k, i, xf, yf, cf=0):
        slot = i * 4 + xf * 2 + yf
        sems = self.core_recv if cf else self.ici_recv
        pltpu.make_async_remote_copy(
            src_ref=self.shards[k],
            dst_ref=self.view(k, i, xf, yf, cf),
            send_sem=self.ici_send.at[k, 0],
            recv_sem=sems.at[k, slot],
            device_id=self.cpeer,
            device_id_type=MESH,
        ).wait_recv()

    def own(self, k):
        return pltpu.make_async_copy(self.shards[k], self.view(k, 0, 0, 0), self.own_sem.at[k])

    def start(self, k):
        self.own(k).start()
        for i in (1, 3, 2):
            self.send(k, 0, 0, 0, self.zpeers[i - 1], ((Z - i) % Z) * 4)
        self.send(k, 0, 0, 0, self.xpeer, 2)
        self.send(k, 0, 0, 0, self.ypeer, 1)
        self.to_core(k, 0, 0, 0)

    def events(self, order):
        out = []
        for kind, k in order:
            if kind == "S":
                out.append(functools.partial(self.start, k))
            elif kind == "z":
                out += [functools.partial(self.zstep, k, i) for i in (1, 3, 2)]
            elif kind == "p":
                out += [functools.partial(self.xystep, k, i, xf) for i in (0, 1, 3, 2) for xf in (1, 0)]
            else:
                out += [functools.partial(self.dstep, k, i) for i in (0, 1, 3, 2)]
        return out

    def zstep(self, k, i):
        self.arrived(k, i, 0, 0)
        self.send(k, i, 0, 0, self.xpeer, i * 4 + 2)
        self.send(k, i, 0, 0, self.ypeer, i * 4 + 1)
        self.to_core(k, i, 0, 0)

    def xystep(self, k, i, xf):
        self.arrived(k, i, xf, 1 - xf)
        if i % 2 == 1 - xf:
            self.send(k, i, xf, 1 - xf, self.ypeer if xf else self.xpeer, i * 4 + 3)
        self.to_core(k, i, xf, 1 - xf)

    def dstep(self, k, i):
        self.arrived(k, i, 1, 1)
        self.to_core(k, i, 1, 1)

    def done(self, k):
        self.own(k).wait()
        for i in range(4):
            for xf in range(2):
                for yf in range(2):
                    self.arrived(k, i, xf, yf, 1)

    def finish(self):
        for copy in self.pending:
            copy.wait_send()


def normal(v):
    centred = v - jnp.mean(v, axis=-1, keepdims=True)
    scale = lax.rsqrt(jnp.mean(centred * centred, axis=-1, keepdims=True) + 1e-5)
    return centred * scale, scale


def dot(a, b):
    return jnp.dot(a, b, preferred_element_type=f32)


def dot_nt(a, b):
    return lax.dot_general(a, b, (((1,), (1,)), ((), ())), preferred_element_type=f32)


def fold(v):
    return jnp.sum(v.reshape(v.shape[0] // 8, 8, v.shape[1]), axis=0)


def loop(count, fn):
    def go(i, carry):
        fn(i)
        return carry

    lax.fori_loop(0, count, go, 0)


def rows_at(i, size):
    return pl.ds(pl.multiple_of(i * size, size), size)


GELU_A = math.sqrt(2.0 / math.pi)
GELU_B = 0.044715


class Rows:
    def __init__(self, short, long):
        self.short, self.long = short, long
        self.total = short + long
        self.padded = self.total + 3 * PAD
        self.segs = ((0, short, PAD), (short, long, 2 * PAD + short))
        self.chunk = short
        self.count = self.total // short
        self.half = short // 2

    def plain(self, i):
        return rows_at(i, self.chunk)

    def place(self, i):
        return pl.multiple_of(i * self.chunk + PAD + PAD * jnp.minimum(i, 1), PAD)

    def halves(self, i):
        low = jnp.where(i == 0, 0, self.short + (i - 1) * self.half)
        high = low + jnp.where(i == 0, self.half, self.long // 2)
        return tuple(pl.ds(pl.multiple_of(v, self.half), self.half) for v in (low, high))


def window3(ref, p, n):
    span = ref[pl.ds(pl.multiple_of(p - PAD, PAD), n + 2 * PAD), :]
    return span[PAD - 1 : PAD - 1 + n], span[PAD : PAD + n], span[PAD + 1 : PAD + 1 + n]


def taps3(views, taps, flip=False):
    a, b, c = views
    return taps[0] * (c if flip else a) + taps[1] * b + taps[2] * (a if flip else c)


def owners(width, q):
    row = lax.broadcasted_iota(jnp.int32, (32, D), 0)
    owner = 2 * (row % 16) + row // 16
    col = lax.broadcasted_iota(jnp.int32, (32, D), 1) + q * D - owner * width
    return jnp.logical_and(col >= 0, col < width)


def one_hot(width, q):
    col = lax.broadcasted_iota(jnp.int32, (8, D), 1) + q * D
    whole = jnp.floor((col.astype(f32) + 0.5) * (1.0 / width)).astype(jnp.int32)
    place = (col - whole * width)[0:1]
    hit = lax.broadcasted_iota(jnp.int32, (128, D), 0) == place
    return jnp.where(hit, 1.0, 0.0).astype(bf16)


def unpack(wide_ref, first, count, width, out_ref):
    parts = []
    for r in range(first, first + count):
        for y in range(2):
            parts.append(wide_ref.at[y][pl.ds(r, 16, stride=32), :])
    parts = jnp.concatenate(parts, axis=0).astype(bf16)
    for q in range(32 * width // D):
        spread = dot(parts, one_hot(width, q))
        mine = owners(width, q)
        for r in range(count):
            piece = jnp.where(mine, spread[32 * r : 32 * r + 32], 0.0)
            out_ref[r : r + 1, q * D : (q + 1) * D] = jnp.sum(piece, axis=0, keepdims=True)


def repack(vec, count, width, first, out_ref):
    out = None
    for q in range(32 * width // D):
        mine = owners(width, q)
        highs, lows = [], []
        for r in range(count):
            v = jnp.where(mine, vec[r : r + 1, q * D : (q + 1) * D], 0.0)
            high = v.astype(bf16)
            highs.append(high)
            lows.append((v - high.astype(f32)).astype(bf16))
        value = dot_nt(jnp.concatenate(highs + lows, axis=0), one_hot(width, q))
        out = value if out is None else out + value
    n = 32 * count
    for r in range(count):
        v = out[32 * r : 32 * r + 32] + out[n + 32 * r : n + 32 * r + 32]
        for y in range(2):
            out_ref.at[y][pl.ds(first + r, 16, stride=24), :] = v[16 * y : 16 * y + 16]


STEP = 16


def angle_parts(length):
    t = np.arange(length)
    coarse = 2.0 * np.pi * (np.outer(STEP * np.arange(length // 2 // STEP), t) % length) / length
    fine = 2.0 * np.pi * (np.outer(np.arange(STEP), t) % length) / length
    scale = 1.0 / math.sqrt(length)
    parts = [np.cos(coarse) * scale, np.sin(coarse) * scale, np.cos(fine), np.sin(fine)]
    return np.concatenate(parts).astype(np.float32)


def build_table(parts_ref, out_ref):
    length = out_ref.shape[0]
    n = length // 2 // STEP
    fine_cos, fine_sin = parts_ref[2 * n : 2 * n + STEP], parts_ref[2 * n + STEP : 2 * n + 2 * STEP]
    row = lax.broadcasted_iota(jnp.int32, (STEP, length), 0)
    sign = 1.0 - 2.0 * (lax.broadcasted_iota(jnp.int32, (STEP, length), 1) % 2).astype(f32)
    for i in range(n):
        cos, sin = parts_ref[i : i + 1], parts_ref[n + i : n + i + 1]
        low = -(sin * fine_cos + cos * fine_sin)
        if i == 0:
            low = jnp.where(row == 0, sign / math.sqrt(length), low)
        out_ref[i * STEP : (i + 1) * STEP] = (cos * fine_cos - sin * fine_sin).astype(bf16)
        out_ref[length // 2 + i * STEP : length // 2 + (i + 1) * STEP] = low.astype(bf16)


def forward_kernel(shape, widths, *refs):
    (pack, w0, w1, w2, w3, w4, ts, tl, cs, cl, ps, pl_) = refs[:12]
    (g_in, g_out, g_gate, g_up, g_down, v72, v24, v96, o_n1, o_proj, o_spec, o_carr, o_long,
     o_mixed, o_hid, o_n2, o_pd, o_ga, o_ap, o_ge, o_fs, o_fst, o_fl, o_flt) = refs[12:36]
    (f_small, f_in, f_out, f_gate, f_up, smallw, x, cot, n1, n1t, proj, spec, carr, longc,
     mixed, mixedt, hid, n2, n2t, ga, ap, ge, pd, pj, gl, vap, rhs, tr, prod, s_ps, s_pl, s_fs, s_fst,
     s_fl, s_flt, ici_send, ici_recv, core_send, core_recv, own_sem, load_sem, save_sem) = refs[36:]
    rows = shape.total
    short = shape.short
    shards = [pack, w0, w1, w2, w3, w4]
    fulls = [f_small, f_in, f_out, f_gate, f_up, g_down]
    zp, xp, yp, cp = neighbours()
    greet(zp + [xp, yp, cp])
    g = Gather(shards, fulls, ici_send, ici_recv, core_send, core_recv, own_sem)
    steps = g.events(GATHER_ORDER)
    marks = {}
    for token in GATHER_ORDER:
        size = {"S": 1, "z": 3, "p": 8, "d": 4}[token[0]]
        marks[token] = size + (max(marks.values()) if marks else 0)
    position = [0]

    def pump(n):
        for step in steps[position[0] : position[0] + n]:
            step()
        position[0] = min(position[0] + n, len(steps))

    def need(k):
        pump(max(0, marks["d", k] - position[0]))
        g.done(k)

    pump(GATHER_FIRST)
    loads = []
    for a, b in [(ps, s_ps), (pl_, s_pl), (ts, x.at[0:short]), (tl, x.at[short:rows]),
                 (cs, cot.at[0:short]), (cl, cot.at[short:rows])]:
        copy = pltpu.make_async_copy(a, b, load_sem.at[len(loads)])
        copy.start()
        loads.append(copy)
    saves = []

    def save(a, b):
        copy = pltpu.make_async_copy(a, b, save_sem.at[len(saves)])
        copy.start()
        saves.append(copy)

    for start, length, place in shape.segs:
        zero = jnp.zeros((PAD, BLK), f32)
        for ref in (pj.at[0], pj.at[1], pj.at[2], vap):
            ref[place - PAD : place] = zero
            ref[place + length : place + length + PAD] = zero
    for copy in loads:
        copy.wait()
    build_table(s_ps, s_fs)
    build_table(s_pl, s_fl)
    pump(6)
    s_fst[...] = s_fs[...].T
    s_flt[...] = s_fl[...].T
    for a, b in ((s_fs, o_fs), (s_fst, o_fst), (s_fl, o_fl), (s_flt, o_flt)):
        save(a, b)
    need(0)
    for y in range(2):
        smallw[y] = f_small[:, y * 128 : (y + 1) * 128].astype(f32)
    unpack(smallw, 0, 4, widths[0], v72)
    pump(2)
    unpack(smallw, 4, 11, widths[1], v24)
    unpack(smallw, 15, 2, widths[2], v96)
    pump(2)

    def norm_one(i):
        r = rows_at(i, 64)
        h, _ = normal(x[r, :].astype(f32))
        n1[r, :] = (h * v24[6:7, :] + v24[7:8, :]).astype(bf16)

    loop(rows // 64, norm_one)
    pump(2)
    n1t[...] = n1[...].T
    save(n1t, o_n1)
    need(1)
    save(f_in, g_in)

    def mix(j, pumps):
        ch = slice(j * BLK, (j + 1) * BLK)
        los = [b * D + j * BLK for b in range(3)]
        tap = [[v72[1 + k : 2 + k, lo : lo + BLK] for k in range(3)] for lo in los]
        ctap = [v24[k : k + 1, ch] for k in range(3)]
        inner, outer = v24[3:4, ch], v24[4:5, ch]
        for b, lo in enumerate(los):
            value = dot(n1[...], f_in[:, lo : lo + BLK]) + v72[0:1, lo : lo + BLK]
            proj[:, lo : lo + BLK] = value.astype(bf16)
            for start, length, place in shape.segs:
                pj[b, place : place + length] = value[start : start + length]
        pump(pumps[0])
        n = shape.chunk

        def convolve(i):
            r, p = shape.plain(i), shape.place(i)
            here = pl.ds(p, n)
            gl[r, :] = taps3(window3(pj.at[0], p, n), tap[0])
            value = taps3(window3(pj.at[2], p, n), tap[2])
            vap[here, :] = value
            rhs[r, BLK:] = (taps3(window3(pj.at[1], p, n), tap[1]) * value).astype(bf16)

        def condition(i):
            rhs[shape.plain(i), :BLK] = taps3(window3(vap, shape.place(i), n), ctap).astype(bf16)

        loop(shape.count, convolve)
        loop(shape.count, condition)
        pump(pumps[1])
        for (start, length, _), table in zip(shape.segs, (s_fs, s_fl)):
            tr[start : start + length] = dot(table[...], rhs[start : start + length])

        def filt(i):
            a, b = shape.halves(i)
            sa, sb = tr[a, :BLK], tr[b, :BLK]
            ca, cb = tr[a, BLK:], tr[b, BLK:]
            spec[a, ch] = sa.astype(bf16)
            spec[b, ch] = sb.astype(bf16)
            carr[a, ch] = ca.astype(bf16)
            carr[b, ch] = cb.astype(bf16)
            fa = jnp.tanh(sa * inner) * outer
            fb = jnp.tanh(sb * inner) * outer
            real, imag = fa * ca, fb * cb
            row = lax.broadcasted_iota(jnp.int32, real.shape, 0)
            first = jnp.logical_and(row == 0, i <= 1)
            prod[a, :] = jnp.where(first, real, 2.0 * (real - imag)).astype(bf16)
            prod[b, :] = jnp.where(first, imag, 2.0 * (fa * cb + fb * ca)).astype(bf16)

        loop(shape.count, filt)
        pump(pumps[2])
        for (start, length, _), table in zip(shape.segs, (s_fst, s_flt)):
            value = dot(table[...], prod[start : start + length])
            longc[start : start + length, ch] = value.astype(bf16)
            mixed[start : start + length, ch] = (value * gl[start : start + length]).astype(bf16)

    for j in range(3):
        mix(j, MIX_PUMPS[j])
    for a, b in ((proj, o_proj), (spec, o_spec), (carr, o_carr), (longc, o_long)):
        save(a, b)
    pump(3)
    mixedt[...] = mixed[...].T
    save(mixedt, o_mixed)
    need(2)
    save(f_out, g_out)

    def branch_one(i):
        r = rows_at(i, 128)
        value = x[r, :].astype(f32) + dot(mixed[r, :], f_out[...]) + v24[5:6, :]
        hid[r, :] = value
        h, _ = normal(value)
        n2[r, :] = (h * v24[8:9, :] + v24[9:10, :]).astype(bf16)

    loop(rows // 128, branch_one)
    save(hid, o_hid)
    n2t[...] = n2[...].T
    save(n2t, o_n2)
    need(3)
    save(f_gate, g_gate)
    need(4)
    save(f_up, g_up)

    def glu(i):
        cols = rows_at(i, BLK)
        for m in range(0, rows, 320):
            gate = dot(n2[m : m + 320, :], f_gate[:, cols]) + v96[0:1, cols]
            up = dot(n2[m : m + 320, :], f_up[:, cols]) + v96[1:2, cols]
            square = gate * gate
            t = jnp.tanh(gate * (GELU_A + GELU_A * GELU_B * square))
            half = 0.5 * (1.0 + t)
            act = gate * half
            slope = half + 0.5 * gate * (1.0 - t * t) * (GELU_A + 3.0 * GELU_A * GELU_B * square)
            ga[m : m + 320, cols] = (act * up).astype(bf16)
            ge[m : m + 320, cols] = act.astype(bf16)
            ap[m : m + 320, cols] = (up * slope).astype(bf16)
        pd[cols, :] = dot(ga[:, cols].T, cot[...]).astype(bf16)

    tiles = ga.shape[1] // BLK
    parts = 6

    def some(first, count):
        lax.fori_loop(first, first + count, lambda i, c: (glu(i), c)[1], 0)

    for q in range(parts):
        some(q * tiles // parts, tiles // parts)
        pump(GLU_PUMPS[q])
        half = pd.shape[0] // 2
        if q == parts // 2:
            save(pd.at[0:half], o_pd.at[0:half])
            first = ga.shape[1] // 2
            for a, b in ((ga, o_ga), (ap, o_ap), (ge, o_ge)):
                save(a.at[:, 0:first], b.at[:, 0:first])
    save(pd.at[half:], o_pd.at[half:])
    for a, b in ((ga, o_ga), (ap, o_ap), (ge, o_ge)):
        save(a.at[:, first:], b.at[:, first:])
    need(5)
    for copy in saves:
        copy.wait()
    g.finish()


GATHER_ORDER = (
    ("S", 0), ("S", 1), ("S", 2), ("z", 0), ("z", 1), ("p", 0), ("S", 3), ("d", 0), ("z", 2), ("p", 1), ("d", 1),
    ("z", 3), ("p", 2), ("S", 4), ("d", 2), ("p", 3), ("z", 4), ("S", 5), ("d", 3), ("p", 4), ("z", 5), ("d", 4),
    ("p", 5), ("d", 5),
)
GATHER_FIRST = 3
MIX_PUMPS = ((2, 3, 2), (3, 3, 2), (3, 3, 2))
GLU_PUMPS = (2, 2, 2, 2, 2, 2)


def place_rows(piece, first):
    rows, width = piece.shape
    return lax.pad(piece, jnp.zeros((), piece.dtype), ((first, 32 - first - rows, 0), (0, 128 - width, 0)))


LARGE = (0, 5, 11, 12, 14)
SMALL = (1, 2, 3, 4, 6, 7, 8, 9, 10, 15, 13)


def pack_small(shards):
    total = None
    first = 0
    for i in SMALL:
        piece = shards[i].reshape(-1, shards[i].shape[-1])
        placed = place_rows(piece, first)
        first += piece.shape[0]
        total = placed if total is None else total + placed
    return total


def forward(ts, tl, cs, cl, shards):
    shape = Rows(ts.shape[1], tl.shape[1])
    short, long, rows = shape.short, shape.long, shape.total
    widths = (shards[1].shape[0], shards[6].shape[0], shards[13].shape[1])
    large = [shards[i] for i in LARGE]
    ff = shards[11].shape[1] * 2
    full = [(16 * s.shape[0], 2 * s.shape[1]) for s in large]
    S = jax.ShapeDtypeStruct
    V = pltpu.VMEM
    angles = [angle_parts(short), angle_parts(long)]
    ins = [pack_small(shards)] + large + [ts.reshape(short, D), tl.reshape(long, D)]
    ins += [cs.reshape(short, D), cl.reshape(long, D)] + [jnp.asarray(a) for a in angles]
    square = [(n, n) for n in (short, short, long, long)]
    vecs = [(8, 32 * widths[0]), (16, 32 * widths[1]), (8, 32 * widths[2])]
    outs = [S(s, bf16) for s in full] + [S(s, f32) for s in vecs]
    outs += [S((D, rows), bf16), S((rows, 3 * D), bf16)] + [S((rows, D), bf16)] * 3
    outs += [S((D, rows), bf16), S((rows, D), f32), S((D, rows), bf16), S((ff, D), bf16)]
    outs += [S((rows, ff), bf16)] * 3 + [S(s, bf16) for s in square]
    any_ = pl.BlockSpec(memory_space=pl.ANY)
    vm = pl.BlockSpec(memory_space=pltpu.VMEM)
    sem = pltpu.SemaphoreType.DMA
    scratch = [V((512, 256), bf16)] + [V(s, bf16) for s in full[:4]]
    scratch += [V((2, 512, 128), f32), V((rows, D), bf16), V((rows, D), bf16), V((rows, D), bf16), V((D, rows), bf16)]
    scratch += [V((rows, 3 * D), bf16)] + [V((rows, D), bf16)] * 4
    scratch += [V((D, rows), bf16), V((rows, D), f32), V((rows, D), bf16), V((D, rows), bf16)]
    scratch += [V((rows, ff), bf16)] * 3 + [V((ff, D), bf16)]
    scratch += [V((3, shape.padded, BLK), f32), V((rows, BLK), f32), V((shape.padded, BLK), f32)]
    scratch += [V((rows, 2 * BLK), bf16), V((rows, 2 * BLK), f32), V((rows, BLK), bf16)]
    scratch += [V(a.shape, f32) for a in angles] + [V(s, bf16) for s in square]
    scratch += [sem((6, 15)), sem((6, 16)), sem((6, 16)), sem((6, 16)), sem((6,)), sem((6,)), sem((28,))]
    return pl.pallas_call(
        functools.partial(forward_kernel, shape, widths),
        out_shape=outs,
        in_specs=[any_] * len(ins),
        out_specs=[any_] * 5 + [vm] * 3 + [any_] * 16,
        scratch_shapes=scratch,
        compiler_params=pltpu.CompilerParams(collective_id=0, has_side_effects=True, vmem_limit_bytes=67043328),
    )(*ins)


class Reduce:
    def __init__(self, items, send_sem, recv_sem, own_sem):
        self.items = items
        self.send_sem, self.recv_sem, self.own_sem = send_sem, recv_sem, own_sem
        self.z, self.x, self.c, self.y = coords()
        self.zpeers, self.xpeer, self.ypeer, self.cpeer = neighbours()
        self.count = [0] * len(items)
        self.pending = []

    def post(self, k, src, dst, peer, slot):
        copy = pltpu.make_async_remote_copy(
            src_ref=src,
            dst_ref=dst,
            send_sem=self.send_sem.at[k, self.count[k]],
            recv_sem=self.recv_sem.at[k, slot],
            device_id=peer,
            device_id_type=MESH,
        )
        self.count[k] += 1
        copy.start()
        self.pending.append(copy)

    def arrived(self, k, dst, slot):
        pltpu.make_async_remote_copy(
            src_ref=dst,
            dst_ref=dst,
            send_sem=self.send_sem.at[k, 0],
            recv_sem=self.recv_sem.at[k, slot],
            device_id=self.cpeer,
            device_id_type=MESH,
        ).wait_recv()

    def part(self, k, b, core, yy):
        item = self.items[k]
        start = (2 * b + core) * item["rows"] + item["base"]
        rows = pl.ds(pl.multiple_of(start, 8), item["rows"])
        if item["flat"]:
            cols = item["cols"]
            return item["source"].at[rows, pl.ds(pl.multiple_of(yy * cols, 128), cols)]
        return item["source"].at[yy, rows, pl.ds(item["first"], item["cols"])]

    def own(self, k, b, yy):
        held = self.items[k]["held"]
        return held.at[b, yy] if held is not None else self.part(k, b, self.c, yy)

    def block(self, i, xx):
        return lax.rem(self.z + i, Z) * 2 + xx

    def order(self):
        for i in (1, 3, 2, 0):
            yield i, self.block(i, 1 - self.x), self.block(i, self.x)

    def core(self, k):
        item = self.items[k]
        for i, across, along in self.order():
            for b in (across, along):
                for yy in range(2):
                    self.post(k, self.part(k, b, 1 - self.c, yy), item["core"].at[b, yy], self.cpeer, b)
        if item["held"] is not None:
            for i, across, along in self.order():
                for b in (across, along):
                    for yy in range(2):
                        pltpu.make_async_copy(
                            self.part(k, b, self.c, yy), item["held"].at[b, yy], self.own_sem.at[b, yy]
                        ).start()

    def merge(self, k, b):
        item = self.items[k]
        if item["held"] is not None:
            for yy in range(2):
                pltpu.make_async_copy(
                    self.part(k, b, self.c, yy), item["held"].at[b, yy], self.own_sem.at[b, yy]
                ).wait()
        self.arrived(k, item["core"].at[b], b)
        for yy in range(2):
            own = self.own(k, b, yy)
            own[...] = own[...] + item["core"][b, yy]

    def diag(self, k):
        item = self.items[k]
        for i, across, along in self.order():
            self.merge(k, across)
            src = self.own(k, across, 1 - self.y)
            if i % 2 == 0:
                self.post(k, src, item["diag_x"].at[i // 2], self.xpeer, 8 + i // 2)
            else:
                self.post(k, src, item["diag_y"].at[i // 2], self.ypeer, 10 + i // 2)
        for i, across, along in self.order():
            self.merge(k, along)

    def near(self, k):
        item = self.items[k]
        for i, across, along in self.order():
            own = self.own(k, along, 1 - self.y)
            if i % 2 == 0:
                self.arrived(k, item["diag_x"].at[i // 2], 8 + i // 2)
                own[...] = own[...] + item["diag_x"][i // 2]
            self.post(k, own, item["near_y"].at[i], self.ypeer, 12 + i)
            own = self.own(k, across, self.y)
            if i % 2 == 1:
                self.arrived(k, item["diag_y"].at[i // 2], 10 + i // 2)
                own[...] = own[...] + item["diag_y"][i // 2]
            self.post(k, own, item["near_x"].at[i], self.xpeer, 16 + i)

    def far(self, k):
        item = self.items[k]
        for i, across, along in self.order():
            self.arrived(k, item["near_x"].at[i], 16 + i)
            self.arrived(k, item["near_y"].at[i], 12 + i)
            own = self.own(k, along, self.y)
            total = own[...].astype(f32) + item["near_x"][i].astype(f32) + item["near_y"][i].astype(f32)
            own[...] = total.astype(own.dtype)
            if i:
                self.post(k, own, item["far"].at[i - 1], self.zpeers[i - 1], 19 + i)

    def last(self, k):
        item = self.items[k]
        total = self.own(k, self.block(0, self.x), self.y)[...].astype(f32)
        for i in range(3):
            self.arrived(k, item["far"].at[i], 20 + i)
            total = total + item["far"][i].astype(f32)
        item["out"][...] = total

    def finish(self):
        for copy in self.pending:
            copy.wait_send()


def backward_kernel(shape, widths, *refs):
    (pd, h_g, h_u, h_d, h_o, h_i, ts, tl, cs, cl, v72, v24, r_n1, r_proj, r_spec, r_carr, r_long,
     r_mixed, r_hid, r_n2, r_ga, r_ap, r_ge, fs, fst, fl, flt) = refs[:27]
    y_s, y_l, o_s, o_l, o_in, o_out, o_gate, o_up, o_down, o_small = refs[27:37]
    nitem = 10
    groups = [refs[37 + q * nitem : 37 + (q + 1) * nitem] for q in range(6)]
    (held, wd, wg, wu, wo, wi, p_small, cot, n2t, apb, geb, acc, big, gm, mixedt, gpj, bspec, bcarr, blong,
     pj, dco, vap, gr, dcp, rhs, tr, s_fs, s_fst, s_fl, s_flt, g72, g24, g96,
     send_sem, recv_sem, own_sem, load_sem, tile_sem, blk_sem, out_sem) = refs[37 + 6 * nitem :]
    rows, short = shape.total, shape.short
    zp, xp, yp, cp = neighbours()
    greet(zp + [xp, yp, cp])

    def item(k, source, out, nrows, cols, first=0, base=0, flat_form=False, held=None):
        names = ("core", "diag_x", "diag_y", "near_x", "near_y", "far")
        made = dict(source=source, out=out, rows=nrows, cols=cols, first=first, base=base, flat=flat_form, held=held)
        made.update({name: group[k] for name, group in zip(names, groups)})
        return made

    half = wg.shape[2] // 2
    span = wi.shape[2] // 3
    n = wi.shape[1]
    r_gate, r_in = o_gate.shape[0], o_in.shape[0]
    items = [
        item(0, pd, o_down, o_down.shape[0], o_down.shape[1], flat_form=True, held=held),
        item(1, wg, o_gate.at[:, 0:half], r_gate, half),
        item(2, wu, o_up.at[:, 0:half], r_gate, half),
        item(3, wg, o_gate.at[:, half : 2 * half], r_gate, half, first=half),
        item(4, wu, o_up.at[:, half : 2 * half], r_gate, half, first=half),
        item(5, wo, o_out, o_out.shape[0], o_out.shape[1]),
    ]
    for t in range(3):
        out = o_in.at[:, t * span : (t + 1) * span]
        items.append(item(6 + t, wd, out, r_in, span, base=t * n, flat_form=True))
    items.append(item(9, p_small, o_small, o_small.shape[0], o_small.shape[1]))
    red = Reduce(items, send_sem, recv_sem, own_sem)
    red.core(0)
    loads = {}

    def load(name, a, b):
        copy = pltpu.make_async_copy(a, b, load_sem.at[len(loads)])
        copy.start()
        loads[name] = copy

    def wait(*names):
        for name in names:
            loads[name].wait()

    def halves(name, a, b, first, size):
        cols = b.shape[2]
        for y in range(2):
            lo = y * cols + first
            load(name + str(y), a.at[:, lo : lo + size], b.at[y, :, first : first + size])

    load("cs", cs, cot.at[0:short])
    load("cl", cl, cot.at[short:rows])
    load("n2t", r_n2, n2t)
    quarter = wd.shape[0] // 4
    for q in (0, 2):
        load("wd%d" % q, h_d.at[q * quarter : (q + 1) * quarter], wd.at[q * quarter : (q + 1) * quarter])
    halves("ga", h_g, wg, 0, half)
    halves("ua", h_u, wu, 0, half)
    per = 2 * (half // BLK)
    total_tiles = 2 * per

    def tile_start(i):
        h, t, y = i // per, lax.rem(i, per) // 2, lax.rem(i, 2)
        return h * half + t * BLK, y

    def tile_copy(i, which):
        first, y = tile_start(i)
        cols = pl.ds(pl.multiple_of(y * 2 * half + first, BLK), BLK)
        slot = lax.rem(i, 2)
        src, dst = ((r_ap, apb), (r_ge, geb))[which]
        return pltpu.make_async_copy(src.at[:, cols], dst.at[slot], tile_sem.at[which, slot])

    for which in range(2):
        tile_copy(0, which).start()
    for q in (1, 3):
        load("wd%d" % q, h_d.at[q * quarter : (q + 1) * quarter], wd.at[q * quarter : (q + 1) * quarter])
    halves("gb", h_g, wg, half, half)
    halves("ub", h_u, wu, half, half)
    load("hid", r_hid, big)
    wide3 = gpj.shape[1]
    load("ga_a", r_ga.at[:, 0:wide3], gpj)
    load("ga_b", r_ga.at[:, wide3:], gm)
    load("mixedt", r_mixed, mixedt)
    halves("wo", h_o, wo, 0, wo.shape[2])
    halves("wi", h_i, wi, 0, wi.shape[2])
    for name, a, b in (("fs", fs, s_fs), ("fst", fst, s_fst), ("fl", fl, s_fl), ("flt", flt, s_flt)):
        load(name, a, b)

    def block_copies(j):
        ch = slice(j * BLK, (j + 1) * BLK)
        return [
            pltpu.make_async_copy(src.at[:, ch], dst, blk_sem.at[k])
            for k, (src, dst) in enumerate(((r_spec, bspec), (r_carr, bcarr), (r_long, blong)))
        ]

    for copy in block_copies(0):
        copy.start()
    acc[...] = jnp.zeros_like(acc)
    zero = jnp.zeros((PAD, BLK), f32)
    for start, length, place in shape.segs:
        for ref in (pj.at[0], pj.at[1], pj.at[2], dco, vap, dcp):
            ref[place - PAD : place] = zero
            ref[place + length : place + length + PAD] = zero
    g24[...] = jnp.zeros_like(g24)
    p_small[...] = jnp.zeros_like(p_small)
    red.diag(0)
    wait("cs", "cl", "n2t", "wd0", "wd2", "ga0", "ga1", "ua0", "ua1")

    def glu_back(i):
        first, y = tile_start(i)
        slot = lax.rem(i, 2)

        @pl.when(i + 1 < total_tiles)
        def _():
            for which in range(2):
                tile_copy(i + 1, which).start()

        for which in range(2):
            tile_copy(i, which).wait()
        cols = pl.ds(pl.multiple_of(first, BLK), BLK)
        every = pl.ds(pl.multiple_of(y * 2 * half + first, BLK), BLK)
        d_act = dot_nt(cot[...], wd[every, :])
        d_gate = (d_act * apb[slot].astype(f32)).astype(bf16)
        d_up = (d_act * geb[slot].astype(f32)).astype(bf16)
        g96[0:1, every] = jnp.sum(fold(d_gate.astype(f32)), axis=0, keepdims=True)
        g96[1:2, every] = jnp.sum(fold(d_up.astype(f32)), axis=0, keepdims=True)
        for m in range(0, rows, 320):
            acc[m : m + 320] += dot_nt(d_gate[m : m + 320], wg[y, :, cols]) + dot_nt(d_up[m : m + 320], wu[y, :, cols])
        wg[y, :, cols] = dot(n2t[...], d_gate).astype(bf16)
        wu[y, :, cols] = dot(n2t[...], d_up).astype(bf16)

    def tile_range(a, b):
        lax.fori_loop(a, b, lambda i, c: (glu_back(i), c)[1], 0)

    tile_range(0, per // 2)
    red.near(0)
    tile_range(per // 2, per)
    red.core(1)
    red.core(2)
    wait("wd1", "wd3", "gb0", "gb1", "ub0", "ub1")
    tile_range(per, per + per // 2)
    red.diag(1)
    red.diag(2)
    tile_range(per + per // 2, 2 * per)
    red.core(3)
    red.core(4)
    red.far(0)
    red.near(1)
    wait("hid", "ga_a", "ga_b")

    def branch_two(i):
        r = rows_at(i, 128)
        value = dot(gpj[r, :], wd[0:wide3, :]) + dot(gm[r, :], wd[wide3:, :])
        gm[r, :] = (big[r, :] + value + v24[10:11, :]).astype(bf16)

    loop(rows // 128, branch_two)
    outs = [
        pltpu.make_async_copy(gm.at[0:short], y_s, out_sem.at[0]),
        pltpu.make_async_copy(gm.at[short:rows], y_l, out_sem.at[1]),
    ]
    for copy in outs:
        copy.start()
    load("proj", r_proj, gpj)
    red.near(2)
    red.diag(3)
    red.diag(4)
    red.last(0)
    for copy in outs:
        copy.wait()

    def norm_two(i):
        r = rows_at(i, 64)
        h, scale = normal(big[r, :])
        d_norm = acc[r, :]
        c = cot[r, :].astype(f32)
        e = d_norm * v24[8:9, :]
        d_hid = c + scale * (e - jnp.mean(e, -1, keepdims=True) - h * jnp.mean(e * h, -1, keepdims=True))
        low = d_hid.astype(bf16)
        acc[r, :] = d_hid
        gm[r, :] = low
        for row, v in ((8, d_norm * h), (9, d_norm), (10, c), (5, low.astype(f32))):
            g24[row : row + 1, :] += jnp.sum(fold(v), axis=0, keepdims=True)

    loop(rows // 64, norm_two)
    red.far(1)
    wait("mixedt", "wo0", "wo1")
    wide = wo.shape[2]

    def out_back(i):
        r = rows_at(i, 128)
        big[r, :] = dot_nt(gm[r, 0:wide], wo[0]) + dot_nt(gm[r, wide : 2 * wide], wo[1])

    loop(rows // 128, out_back)
    for y in range(2):
        wo[y] = dot(mixedt[...], gm[:, y * wide : (y + 1) * wide]).astype(bf16)
    red.core(5)
    load("n1t", r_n1, n2t)
    load("ts", ts, gm.at[0:short])
    load("tl", tl, gm.at[short:rows])
    red.far(2)
    wait("proj", "fs", "fst", "fl", "flt")
    size = shape.chunk

    def mix_back(j, pumps):
        ch = slice(j * BLK, (j + 1) * BLK)
        los = [b * D + j * BLK for b in range(3)]
        tap = [[v72[1 + k : 2 + k, lo : lo + BLK] for k in range(3)] for lo in los]
        ctap = [v24[k : k + 1, ch] for k in range(3)]
        inner, outer = v24[3:4, ch], v24[4:5, ch]
        for copy in block_copies(j):
            copy.wait()

        def spread_out(i):
            here = pl.ds(shape.place(i), size)
            for b in range(3):
                pj[b, here, :] = gpj[shape.plain(i), los[b] : los[b] + BLK].astype(f32)

        def gates(i):
            r, p = shape.plain(i), shape.place(i)
            here = pl.ds(p, size)
            d_mix = big[r, ch]
            rhs[r, :BLK] = (d_mix * taps3(window3(pj.at[0], p, size), tap[0])).astype(bf16)
            dco[here, :] = d_mix * blong[r, :].astype(f32)
            gr[r, :] = taps3(window3(pj.at[1], p, size), tap[1])
            vap[here, :] = taps3(window3(pj.at[2], p, size), tap[2])

        loop(shape.count, spread_out)
        loop(shape.count, gates)

        def conv_down(b):
            def go(i, sums):
                r, p = shape.plain(i), shape.place(i)
                views = window3(dco, p, size)
                low = taps3(views, tap[b], True).astype(bf16)
                gpj[r, los[b] : los[b] + BLK] = low
                parts = [low.astype(f32)] + [views[1] * v for v in window3(pj.at[b], p, size)]
                return tuple(s + fold(v) for s, v in zip(sums, parts))

            sums = lax.fori_loop(0, shape.count, go, (jnp.zeros((8, BLK), f32),) * 4)
            for k in range(4):
                g72[k : k + 1, los[b] : los[b] + BLK] = jnp.sum(sums[k], axis=0, keepdims=True)

        for (start, length, _), table in zip(shape.segs, (s_fs, s_fl)):
            tr[start : start + length] = dot(table[...], rhs[start : start + length, :BLK])
        conv_down(0)
        pumps[0]()

        def filt_back(i, sums):
            a, b = shape.halves(i)
            pa, pb = tr[a, :], tr[b, :]
            sa, sb = bspec[a, :].astype(f32), bspec[b, :].astype(f32)
            ca, cb = bcarr[a, :].astype(f32), bcarr[b, :].astype(f32)
            ta, tb = jnp.tanh(sa * inner), jnp.tanh(sb * inner)
            fa, fb = ta * outer, tb * outer
            first = jnp.logical_and(lax.broadcasted_iota(jnp.int32, pa.shape, 0) == 0, i <= 1)
            pa = jnp.where(first, pa, 2.0 * pa)
            pb = jnp.where(first, pb, 2.0 * pb)
            ra, rb = pa * ca, pb * cb
            ua, ub = pa * fa, pb * fb
            dfa = jnp.where(first, ra, ra + rb)
            dfb = jnp.where(first, rb, pb * ca - pa * cb)
            rhs[a, BLK:] = jnp.where(first, ua, ua + ub).astype(bf16)
            rhs[b, BLK:] = jnp.where(first, ub, pb * fa - pa * fb).astype(bf16)
            dta, dtb = dfa * outer * (1.0 - ta * ta), dfb * outer * (1.0 - tb * tb)
            rhs[a, :BLK] = (dta * inner).astype(bf16)
            rhs[b, :BLK] = (dtb * inner).astype(bf16)
            return sums[0] + fold(dta * sa + dtb * sb), sums[1] + fold(dfa * ta + dfb * tb)

        sums = lax.fori_loop(0, shape.count, filt_back, (jnp.zeros((8, BLK), f32),) * 2)
        for k in range(2):
            g24[3 + k : 4 + k, ch] = jnp.sum(sums[k], axis=0, keepdims=True)
        if j < 2:
            for copy in block_copies(j + 1):
                copy.start()
        for (start, length, place), table in zip(shape.segs, (s_fst, s_flt)):
            dcp[place : place + length] = dot(table[...], rhs[start : start + length, :BLK])
            tr[start : start + length] = dot(table[...], rhs[start : start + length, BLK:])
        pumps[1]()

        def right(i):
            here = pl.ds(shape.place(i), size)
            dco[here, :] = tr[shape.plain(i), :] * vap[here, :]

        loop(shape.count, right)
        conv_down(1)

        def value(i, sums):
            r, p = shape.plain(i), shape.place(i)
            views = window3(dcp, p, size)
            dco[pl.ds(p, size), :] = taps3(views, ctap, True) + tr[r, :] * gr[r, :]
            return tuple(s + fold(views[1] * v) for s, v in zip(sums, window3(vap, p, size)))

        sums = lax.fori_loop(0, shape.count, value, (jnp.zeros((8, BLK), f32),) * 3)
        for k in range(3):
            g24[k : k + 1, ch] = jnp.sum(sums[k], axis=0, keepdims=True)
        conv_down(2)
        pumps[2]()

    none = lambda: None
    mix_back(0, [none, lambda: red.diag(5), none])
    mix_back(1, [lambda: red.near(3), lambda: red.near(4), lambda: red.last(1)])
    mix_back(2, [lambda: red.last(2), none, none])
    wait("n1t", "wi0", "wi1")
    for t in range(3):
        for y in range(2):
            lo = (3 * y + t) * span
            wd[t * n : (t + 1) * n, y * span : (y + 1) * span] = dot(n2t[...], gpj[:, lo : lo + span]).astype(bf16)
        red.core(6 + t)
        if t == 0:
            red.near(5)
        if t == 1:
            red.far(3)
    red.diag(6)
    deep = wi.shape[2]

    def in_back(i):
        r = rows_at(i, 128)
        big[r, :] = dot_nt(gpj[r, 0:deep], wi[0]) + dot_nt(gpj[r, deep : 2 * deep], wi[1])

    lax.fori_loop(0, 2, lambda i, c: (in_back(i), c)[1], 0)
    red.diag(7)
    lax.fori_loop(2, rows // 128, lambda i, c: (in_back(i), c)[1], 0)
    red.diag(8)
    red.far(4)
    wait("ts", "tl")

    def norm_one(i):
        r = rows_at(i, 64)
        h, scale = normal(gm[r, :].astype(f32))
        d_norm = big[r, :]
        e = d_norm * v24[6:7, :]
        acc[r, :] += scale * (e - jnp.mean(e, -1, keepdims=True) - h * jnp.mean(e * h, -1, keepdims=True))
        for row, v in ((6, d_norm * h), (7, d_norm)):
            g24[row : row + 1, :] += jnp.sum(fold(v), axis=0, keepdims=True)

    loop(rows // 64, norm_one)
    outs = [
        pltpu.make_async_copy(acc.at[0:short], o_s, out_sem.at[0]),
        pltpu.make_async_copy(acc.at[short:rows], o_l, out_sem.at[1]),
    ]
    for copy in outs:
        copy.start()
    red.far(5)
    red.near(6)
    red.last(3)
    repack(g72, 4, widths[0], 0, p_small)
    red.near(7)
    repack(g24, 11, widths[1], 4, p_small)
    repack(g96, 2, widths[2], 15, p_small)
    red.core(9)
    red.near(8)
    red.last(4)
    red.diag(9)
    red.far(6)
    red.near(9)
    red.far(7)
    red.far(8)
    red.far(9)
    for k in (5, 6, 7, 8, 9):
        red.last(k)
    for copy in outs:
        copy.wait()
    red.finish()


def backward(ts, tl, cs, cl, shards, weights, vecs, res, tables):
    shape = Rows(ts.shape[1], tl.shape[1])
    short, long, rows = shape.short, shape.long, shape.total
    widths = (shards[1].shape[0], shards[6].shape[0], shards[13].shape[1])
    S = jax.ShapeDtypeStruct
    V = pltpu.VMEM
    w_in, w_out, w_gate, w_up, w_down = weights
    n1t, proj, spec, carr, longc, mixedt, hid, n2t, pd, ga, ap, ge = res
    ins = [pd, w_gate, w_up, w_down, w_out, w_in, ts.reshape(short, D), tl.reshape(long, D), cs.reshape(short, D),
           cl.reshape(long, D), vecs[0], vecs[1], n1t, proj, spec, carr, longc, mixedt, hid, n2t, ga, ap, ge]
    ins += list(tables)
    any_ = pl.BlockSpec(memory_space=pl.ANY)
    vm = pl.BlockSpec(memory_space=pltpu.VMEM)
    in_specs = [any_] * 10 + [vm] * 2 + [any_] * 15
    shard = [shards[i].shape for i in LARGE]
    outs = [S((short, D), bf16), S((long, D), bf16), S((short, D), f32), S((long, D), f32)]
    outs += [S(s, f32) for s in shard] + [S((24, 128), f32)]
    half, span = shard[2][1] // 2, shard[0][1] // 3
    dims = [shard[4]] + [(shard[2][0], half)] * 4 + [shard[1]] + [(shard[0][0], span)] * 3 + [(24, 128)]
    kinds = [bf16] * 9 + [f32]
    scratch = []
    for lead in ((8, 2), (2,), (2,), (4,), (4,), (3,)):
        scratch += [V(lead + d, t) for d, t in zip(dims, kinds)]
    wide = lambda s: (2, 16 * s[0], s[1])
    scratch += [
        V((8, 2) + shard[4], bf16), V((16 * shard[4][0], 2 * shard[4][1]), bf16), V(wide(shard[2]), bf16),
        V(wide(shard[3]), bf16), V(wide(shard[1]), bf16), V(wide(shard[0]), bf16), V((2, 384, 128), f32),
        V((rows, D), bf16), V((D, rows), bf16), V((2, rows, BLK), bf16), V((2, rows, BLK), bf16),
        V((rows, D), f32), V((rows, D), f32), V((rows, D), bf16), V((D, rows), bf16), V((rows, 3 * D), bf16),
        V((rows, BLK), bf16), V((rows, BLK), bf16), V((rows, BLK), bf16),
        V((3, shape.padded, BLK), f32), V((shape.padded, BLK), f32), V((shape.padded, BLK), f32),
        V((rows, BLK), f32), V((shape.padded, BLK), f32), V((rows, 2 * BLK), bf16), V((rows, BLK), f32),
    ]
    scratch += [V((m, m), bf16) for m in (short, short, long, long)]
    scratch += [V((8, 32 * widths[0]), f32), V((16, 32 * widths[1]), f32), V((8, 32 * widths[2]), f32)]
    sem = pltpu.SemaphoreType.DMA
    scratch += [sem((10, 31)), sem((10, 23)), sem((8, 2)), sem((36,)), sem((2, 2)), sem((3,)), sem((2,))]
    return pl.pallas_call(
        functools.partial(backward_kernel, shape, widths),
        out_shape=outs,
        in_specs=in_specs,
        out_specs=[any_] * 4 + [vm] * 6,
        scratch_shapes=scratch,
        compiler_params=pltpu.CompilerParams(collective_id=1, has_side_effects=True, vmem_limit_bytes=67043328),
    )(*ins)


def finish_kernel(spans, *refs):
    n = 9
    small, bulk = refs[0], refs[1 : 1 + n]
    outs = refs[1 + n : 1 + 2 * n]
    smalls = refs[1 + 2 * n : 1 + 2 * n + len(spans)]
    bufs = refs[1 + 2 * n + len(spans) : 1 + 3 * n + len(spans)]
    sem = refs[-1]
    ins = [pltpu.make_async_copy(a, b, sem.at[0, k]) for k, (a, b) in enumerate(zip(bulk, bufs))]
    for copy in ins:
        copy.start()
    for (first, count, width), ref in zip(spans, smalls):
        ref[...] = small[first : first + count, 0:width]
    back = [pltpu.make_async_copy(a, b, sem.at[1, k]) for k, (a, b) in enumerate(zip(bufs, outs))]
    for one, two in zip(ins, back):
        one.wait()
        two.start()
    for copy in back:
        copy.wait()


def finish(small, bulk, shards):
    spans = []
    first = 0
    for i in SMALL:
        s = shards[i].shape
        count = s[0] if len(s) == 2 else 1
        spans.append((first, count, s[-1]))
        first += count
    S = jax.ShapeDtypeStruct
    any_ = pl.BlockSpec(memory_space=pl.ANY)
    vm = pl.BlockSpec(memory_space=pltpu.VMEM)
    made = pl.pallas_call(
        functools.partial(finish_kernel, spans),
        out_shape=[S(a.shape, a.dtype) for a in bulk] + [S((c, w), f32) for _, c, w in spans],
        in_specs=[vm] + [any_] * len(bulk),
        out_specs=[any_] * len(bulk) + [vm] * len(spans),
        scratch_shapes=[pltpu.VMEM(a.shape, a.dtype) for a in bulk] + [pltpu.SemaphoreType.DMA((2, len(bulk)))],
    )(small, *bulk)
    grads = {i: v.reshape(shards[i].shape) for i, v in zip(SMALL, made[len(bulk) :])}
    return made[: len(bulk)], grads


def ring_step(ts, tl, cs, cl, shards):
    f = forward(ts, tl, cs, cl, shards)
    b = backward(ts, tl, cs, cl, shards, f[0:5], f[5:8], f[8:20], f[20:24])
    bulk, grads = finish(b[9], b[:9], shards)
    for i, g in zip(LARGE, bulk[4:9]):
        grads[i] = g
    seqs = (ts, tl, ts, tl)
    return tuple(v.reshape(s.shape) for v, s in zip(bulk, seqs)) + tuple(grads[i] for i in range(16))


def table(length):
    half = length // 2
    t = np.arange(length)
    k = np.arange(half)
    ang = 2.0 * np.pi * (np.outer(k, t) % length) / length
    top = np.cos(ang)
    low = -np.sin(ang)
    low[0] = np.where(t % 2 == 0, 1.0, -1.0)
    return (np.concatenate([top, low]) / math.sqrt(length)).astype(np.float32)

def dft(form, tab, v):
    return jnp.einsum(form, jnp.asarray(tab, bf16), v.astype(bf16), preferred_element_type=f32)

def down(v): return jnp.pad(v[:, :-1], ((0,0),(1,0),(0,0)))
def up(v): return jnp.pad(v[:, 1:], ((0,0),(0,1),(0,0)))
def conv(v, k): return k[0]*down(v)+k[1]*v+k[2]*up(v)
def conv_back(g, k): return k[0]*up(g)+k[1]*g+k[2]*down(g)
def conv_kernel(g, v):
    return jnp.stack([jnp.sum(g*down(v),(0,1)), jnp.sum(g*v,(0,1)), jnp.sum(g*up(v),(0,1))])

def weights(length):
    half = length//2
    w = np.full((half,1),2.0,np.float32); w[0]=1.0
    return np.concatenate([w,w])

def mixer_fwd(proj, sk, ck, fg):
    D = ck.shape[1]; L = proj.shape[1]; H=L//2
    tab = table(L); w = weights(L)
    co = conv(proj, sk)
    gl, gr, va = co[:,:,:D], co[:,:,D:2*D], co[:,:,2*D:]
    cond = conv(va, ck)
    spec = dft("kt,btc->bkc", tab, cond)
    carr = dft("kt,btc->bkc", tab, gr*va)
    th = jnp.tanh(spec*fg[0]); filt = th*fg[1]
    first = (lax.broadcasted_iota(jnp.int32,(H,1),0)==0)
    fa, fb, ca, cb = filt[:,:H], filt[:,H:], carr[:,:H], carr[:,H:]
    pa = fa*ca - jnp.where(first,0.0,fb*cb)
    pb = jnp.where(first, fb*cb, fa*cb+fb*ca)
    prod = jnp.concatenate([pa,pb],1)*w
    longc = dft("kt,bkc->btc", tab, prod)
    return gl*longc, (co, spec, th, carr, longc)

def mixer_bwd(dmix, proj, res, sk, ck, fg):
    co, spec, th, carr, longc = res
    D = ck.shape[1]; L = proj.shape[1]; H=L//2
    tab = table(L); w = weights(L)
    gl, gr, va = co[:,:,:D], co[:,:,D:2*D], co[:,:,2*D:]
    dgl = dmix*longc
    dlong = dmix*gl
    dp = dft("kt,btc->bkc", tab, dlong)*w
    filt = th*fg[1]
    first = (lax.broadcasted_iota(jnp.int32,(H,1),0)==0)
    fa, fb, ca, cb = filt[:,:H], filt[:,H:], carr[:,:H], carr[:,H:]
    da, db = dp[:,:H], dp[:,H:]
    dfa = da*ca + jnp.where(first,0.0,db*cb)
    dfb = jnp.where(first, db*cb, db*ca-da*cb)
    dca = da*fa + jnp.where(first,0.0,db*fb)
    dcb = jnp.where(first, db*fb, db*fa-da*fb)
    df = jnp.concatenate([dfa,dfb],1); dc = jnp.concatenate([dca,dcb],1)
    dth = df*fg[1]*(1-th*th)
    dfg = jnp.stack([jnp.sum(dth*spec,(0,1)), jnp.sum(df*th,(0,1))])
    dcond = dft("kt,bkc->btc", tab, dth*fg[0])
    dgv = dft("kt,bkc->btc", tab, dc)
    dck = conv_kernel(dcond, va)
    dva = conv_back(dcond, ck) + dgv*gr
    dgr = dgv*va
    dco = jnp.concatenate([dgl,dgr,dva],2)
    dsk = conv_kernel(dco, proj)
    return conv_back(dco, sk), dsk, dck, dfg

def mm(a,b): return jnp.dot(a,b,preferred_element_type=f32)
def tn(a,b): return lax.dot_general(a,b,(((0,),(0,)),((),())),preferred_element_type=f32)
def nt(a,b): return lax.dot_general(a,b,(((1,),(1,)),((),())),preferred_element_type=f32)

def norm(v):
    m = jnp.mean(v,-1,keepdims=True); d = v-m
    r = lax.rsqrt(jnp.mean(d*d,-1,keepdims=True)+1e-5)
    return d*r, r

def norm_back(e, h, r):
    return r*(e-jnp.mean(e,-1,keepdims=True)-h*jnp.mean(e*h,-1,keepdims=True))

C0=math.sqrt(2/math.pi); C1=0.044715
def gelu_parts(g):
    t = jnp.tanh(C0*(g+C1*g*g*g))
    return 0.5*g*(1+t), 0.5*(1+t)+0.5*g*(1-t*t)*C0*(1+3*C1*g*g)

def local(ts, tl, P, cs, cl):
    (iw, ib, sk, ck, fg, ow, ob, g1, b1, g2, b2, gw, uw, gb, dw, db) = [p if i in (0,5,11,12,14) else p.astype(f32) for i,p in enumerate(P)]
    D = ow.shape[0]
    ns = ts.shape[0]*ts.shape[1]
    x = jnp.concatenate([ts.reshape(-1,D),tl.reshape(-1,D)]).astype(f32)
    c = jnp.concatenate([cs.reshape(-1,D),cl.reshape(-1,D)])
    h1, r1 = norm(x)
    n1 = (h1*g1+b1).astype(bf16)
    proj = mm(n1, iw)+ib
    ps, pl_ = proj[:ns].reshape(ts.shape[0],ts.shape[1],3*D), proj[ns:].reshape(tl.shape[0],tl.shape[1],3*D)
    ms, rs = mixer_fwd(ps, sk, ck, fg); ml, rl = mixer_fwd(pl_, sk, ck, fg)
    mixed = jnp.concatenate([ms.reshape(-1,D),ml.reshape(-1,D)]).astype(bf16)
    hid = x + mm(mixed, ow)+ob
    h2, r2 = norm(hid)
    n2 = (h2*g2+b2).astype(bf16)
    gp = mm(n2,gw)+gb[0]; up_ = mm(n2,uw)+gb[1]
    ge, gd = gelu_parts(gp)
    ga = (ge*up_).astype(bf16)
    out = (hid+mm(ga,dw)+db).astype(bf16)
    cf = c.astype(f32)
    d_db = jnp.sum(cf,0); d_dw = tn(ga,c)
    dg = nt(c,dw)
    dgate = (dg*up_*gd).astype(bf16); dup=(dg*ge).astype(bf16)
    d_gb = jnp.stack([jnp.sum(dgate.astype(f32),0),jnp.sum(dup.astype(f32),0)])
    d_gw = tn(n2,dgate); d_uw = tn(n2,dup)
    dn2 = nt(dgate,gw)+nt(dup,uw)
    d_g2 = jnp.sum(dn2*h2,0); d_b2=jnp.sum(dn2,0)
    dh = cf + norm_back(dn2*g2,h2,r2)
    gm = dh.astype(bf16)
    d_ob = jnp.sum(gm.astype(f32),0); d_ow = tn(mixed,gm)
    dm = nt(gm,ow)
    dps, a1,a2,a3 = mixer_bwd(dm[:ns].reshape(ts.shape), ps, rs, sk, ck, fg)
    dpl, e1,e2,e3 = mixer_bwd(dm[ns:].reshape(tl.shape), pl_, rl, sk, ck, fg)
    gpj = jnp.concatenate([dps.reshape(-1,3*D),dpl.reshape(-1,3*D)]).astype(bf16)
    d_ib = jnp.sum(gpj.astype(f32),0); d_iw = tn(n1,gpj)
    dn1 = nt(gpj,iw)
    d_g1=jnp.sum(dn1*h1,0); d_b1=jnp.sum(dn1,0)
    dx = dh + norm_back(dn1*g1,h1,r1)
    return (out[:ns].reshape(ts.shape), out[ns:].reshape(tl.shape), dx[:ns].reshape(ts.shape), dx[ns:].reshape(tl.shape),
        d_iw,d_ib,a1+e1,a2+e2,a3+e3,d_ow,d_ob,d_g1,d_b1,d_g2,d_b2,d_gw,d_uw,d_gb,d_dw,d_db)


def fetch_plain(shards):
    params = []
    for i, shard in enumerate(shards):
        if i in LARGE:
            wide = lax.all_gather(shard, "narrow", axis=1, tiled=True)
            params.append(lax.all_gather(wide, "wide", axis=0, tiled=True))
        else:
            params.append(
                lax.all_gather(shard, ("wide", "narrow"), axis=shard.ndim - 1, tiled=True)
            )
    return params


def reduce_plain(grads, shards):
    outs = []
    for i, grad in enumerate(grads):
        if i in LARGE:
            block = lax.psum_scatter(grad.astype(bf16), "wide", scatter_dimension=0, tiled=True)
            block = lax.psum_scatter(block, "narrow", scatter_dimension=1, tiled=True)
            outs.append(block.astype(f32))
        else:
            outs.append(
                lax.psum_scatter(
                    grad, ("wide", "narrow"), scatter_dimension=grad.ndim - 1, tiled=True
                )
            )
    return outs


def plain_step(ts, tl, cs, cl, shards):
    results = local(ts, tl, fetch_plain(shards), cs, cl)
    return tuple(results[:4]) + tuple(reduce_plain(results[4:], shards))


def body(ring, ts, tl, *rest):
    step = ring_step if ring and ts.shape[0] == 1 and tl.shape[0] == 1 else plain_step
    return step(ts, tl, rest[16], rest[17], list(rest[:16]))


def solution(mesh):
    ring = mesh.shape["wide"] == 16 and mesh.shape["narrow"] == 2
    seq = P(("wide", "narrow"), None, None)
    mat = P("wide", "narrow")
    vec = P(("wide", "narrow"))
    pair = P(None, ("wide", "narrow"))
    params = (mat, vec, pair, pair, pair, mat, vec, vec, vec, vec, vec, mat, mat, pair, mat, vec)
    return jax.shard_map(
        functools.partial(body, ring),
        mesh=mesh,
        in_specs=(seq, seq) + params + (seq, seq),
        out_specs=(seq, seq, seq, seq) + params,
        check_vma=False,
    )
```

```python
import functools
import math

import jax
import jax.numpy as jnp
import numpy as np
from jax import lax
from jax.experimental import pallas as pl
from jax.experimental.pallas import tpu as pltpu
from jax.sharding import PartitionSpec as P

bf16 = jnp.bfloat16
f32 = jnp.float32
MESH = pl.DeviceIdType.MESH
Z = 4
D = 768
BLK = 256
PAD = 8


def coords():
    w = lax.axis_index("wide")
    return w // 4, (w // 2) % 2, w % 2, lax.axis_index("narrow")


def flat(z, x, c):
    return (z * 2 + x) * 2 + c


def window(ref, rows, cols, w, y):
    return ref.at[
        pl.ds(pl.multiple_of(w * rows, 16), rows), pl.ds(pl.multiple_of(y * cols, 128), cols)
    ]


def greet(peers):
    barrier = pltpu.get_barrier_semaphore()
    for peer in peers:
        pl.semaphore_signal(barrier, inc=1, device_id=peer, device_id_type=MESH)
    pl.semaphore_wait(barrier, len(peers))


def neighbours():
    z, x, c, y = coords()
    zpeers = [(flat(lax.rem(z + i, Z), x, c), y) for i in (1, 2, 3)]
    return zpeers, (flat(z, 1 - x, c), y), (flat(z, x, c), 1 - y), (flat(z, x, 1 - c), y)


class Gather:
    def __init__(self, items, ici_send, ici_recv, core_send, core_recv, own_sem):
        self.items = items
        self.ici_send, self.ici_recv = ici_send, ici_recv
        self.core_send, self.core_recv, self.own_sem = core_send, core_recv, own_sem
        self.z, self.x, self.c, self.y = coords()
        self.zpeers, self.xpeer, self.ypeer, self.cpeer = neighbours()
        self.count = [0] * len(items)
        self.pending = []

    def shard(self, k):
        ref, _, first, cols = self.items[k]
        return ref if cols == ref.shape[1] else ref.at[:, first : first + cols]

    def view(self, k, i, xf, yf, cf=0):
        ref, full, first, cols = self.items[k]
        zz = lax.rem(self.z + i, Z)
        xx = 1 - self.x if xf else self.x
        yy = 1 - self.y if yf else self.y
        cc = 1 - self.c if cf else self.c
        rows, whole = ref.shape
        row = pl.multiple_of(flat(zz, xx, cc) * rows, 16)
        return full.at[pl.ds(row, rows), pl.ds(pl.multiple_of(yy * whole + first, 128), cols)]

    def copy(self, k, src, dst, peer, send, recv):
        return pltpu.make_async_remote_copy(
            src_ref=src, dst_ref=dst, send_sem=send, recv_sem=recv, device_id=peer, device_id_type=MESH
        )

    def post(self, k, i, xf, yf, peer, send, recv):
        src = self.shard(k) if (i, xf, yf) == (0, 0, 0) else self.view(k, i, xf, yf)
        self.pending.append((k, send))
        self.copy(k, src, self.view(k, i, xf, yf), peer, self.sent(k, send), recv).start()

    def sent(self, k, send):
        return (self.core_send if send[0] else self.ici_send).at[k, send[1]]

    def send(self, k, i, xf, yf, peer, slot):
        self.post(k, i, xf, yf, peer, (0, self.count[k]), self.ici_recv.at[k, slot])
        self.count[k] += 1

    def to_core(self, k, i, xf, yf):
        slot = i * 4 + xf * 2 + yf
        self.post(k, i, xf, yf, self.cpeer, (1, slot), self.core_recv.at[k, slot])

    def arrived(self, k, i, xf, yf, cf=0):
        slot = i * 4 + xf * 2 + yf
        sems = self.core_recv if cf else self.ici_recv
        dst = self.view(k, i, xf, yf, cf)
        self.copy(k, self.shard(k), dst, self.cpeer, self.ici_send.at[k, 0], sems.at[k, slot]).wait_recv()

    def own(self, k):
        return pltpu.make_async_copy(self.shard(k), self.view(k, 0, 0, 0), self.own_sem.at[k])

    def start(self, k):
        self.own(k).start()
        for i in (1, 3, 2):
            self.send(k, 0, 0, 0, self.zpeers[i - 1], ((Z - i) % Z) * 4)
        self.send(k, 0, 0, 0, self.xpeer, 2)
        self.send(k, 0, 0, 0, self.ypeer, 1)
        self.to_core(k, 0, 0, 0)

    def events(self, order):
        out = []
        for kind, k in order:
            if kind == "S":
                out.append(functools.partial(self.start, k))
            elif kind == "z":
                out += [functools.partial(self.zstep, k, i) for i in (1, 3, 2)]
            elif kind == "p":
                out += [functools.partial(self.xystep, k, i, xf) for i in (0, 1, 3, 2) for xf in (1, 0)]
            else:
                out += [functools.partial(self.dstep, k, i) for i in (0, 1, 3, 2)]
        return out

    def zstep(self, k, i):
        self.arrived(k, i, 0, 0)
        self.send(k, i, 0, 0, self.xpeer, i * 4 + 2)
        self.send(k, i, 0, 0, self.ypeer, i * 4 + 1)
        self.to_core(k, i, 0, 0)

    def xystep(self, k, i, xf):
        self.arrived(k, i, xf, 1 - xf)
        if i % 2 == 1 - xf:
            self.send(k, i, xf, 1 - xf, self.ypeer if xf else self.xpeer, i * 4 + 3)
        self.to_core(k, i, xf, 1 - xf)

    def dstep(self, k, i):
        self.arrived(k, i, 1, 1)
        self.to_core(k, i, 1, 1)

    def done(self, k):
        self.own(k).wait()
        for i in range(4):
            for xf in range(2):
                for yf in range(2):
                    self.arrived(k, i, xf, yf, 1)

    def finish(self):
        for k, send in self.pending:
            dst = self.view(k, 0, 0, 0)
            self.copy(k, self.shard(k), dst, self.cpeer, self.sent(k, send), self.ici_recv.at[k, 0]).wait_send()


def normal(v):
    centred = v - jnp.mean(v, axis=-1, keepdims=True)
    scale = lax.rsqrt(jnp.mean(centred * centred, axis=-1, keepdims=True) + 1e-5)
    return centred * scale, scale


def dot(a, b):
    return jnp.dot(a, b, preferred_element_type=f32)


def dot_nt(a, b):
    return lax.dot_general(a, b, (((1,), (1,)), ((), ())), preferred_element_type=f32)


def fold(v):
    return jnp.sum(v.reshape(v.shape[0] // 8, 8, v.shape[1]), axis=0)


def loop(count, fn):
    def go(i, carry):
        fn(i)
        return carry

    lax.fori_loop(0, count, go, 0)


def rows_at(i, size):
    return pl.ds(pl.multiple_of(i * size, size), size)


GELU_A = math.sqrt(2.0 / math.pi)
GELU_B = 0.044715


class Rows:
    def __init__(self, short, long):
        self.short, self.long = short, long
        self.total = short + long
        self.padded = self.total + 3 * PAD
        self.segs = ((0, short, PAD), (short, long, 2 * PAD + short))
        self.chunk = short
        self.count = self.total // short
        self.half = short // 2

    def plain(self, i):
        return rows_at(i, self.chunk)

    def place(self, i):
        return pl.multiple_of(i * self.chunk + PAD + PAD * jnp.minimum(i, 1), PAD)

    def halves(self, i):
        low = jnp.where(i == 0, 0, self.short + (i - 1) * self.half)
        high = low + jnp.where(i == 0, self.half, self.long // 2)
        return tuple(pl.ds(pl.multiple_of(v, self.half), self.half) for v in (low, high))


def window3(ref, p, n):
    span = ref[pl.ds(pl.multiple_of(p - PAD, PAD), n + 2 * PAD), :]
    return span[PAD - 1 : PAD - 1 + n], span[PAD : PAD + n], span[PAD + 1 : PAD + 1 + n]


def taps3(views, taps, flip=False):
    a, b, c = views
    return taps[0] * (c if flip else a) + taps[1] * b + taps[2] * (a if flip else c)


def owners(width, q):
    row = lax.broadcasted_iota(jnp.int32, (32, D), 0)
    owner = 2 * (row % 16) + row // 16
    col = lax.broadcasted_iota(jnp.int32, (32, D), 1) + q * D - owner * width
    return jnp.logical_and(col >= 0, col < width)


def one_hot(width, q):
    col = lax.broadcasted_iota(jnp.int32, (8, D), 1) + q * D
    whole = jnp.floor((col.astype(f32) + 0.5) * (1.0 / width)).astype(jnp.int32)
    place = (col - whole * width)[0:1]
    hit = lax.broadcasted_iota(jnp.int32, (128, D), 0) == place
    return jnp.where(hit, 1.0, 0.0).astype(bf16)


def unpack(wide_ref, first, count, width, out_ref):
    parts = []
    for r in range(first, first + count):
        for y in range(2):
            parts.append(wide_ref.at[y][pl.ds(r, 16, stride=32), :])
    parts = jnp.concatenate(parts, axis=0).astype(bf16)
    for q in range(32 * width // D):
        spread = dot(parts, one_hot(width, q))
        mine = owners(width, q)
        for r in range(count):
            piece = jnp.where(mine, spread[32 * r : 32 * r + 32], 0.0)
            out_ref[r : r + 1, q * D : (q + 1) * D] = jnp.sum(piece, axis=0, keepdims=True)


def repack(vec, count, width, first, out_ref):
    out = None
    for q in range(32 * width // D):
        mine = owners(width, q)
        highs, lows = [], []
        for r in range(count):
            v = jnp.where(mine, vec[r : r + 1, q * D : (q + 1) * D], 0.0)
            high = v.astype(bf16)
            highs.append(high)
            lows.append((v - high.astype(f32)).astype(bf16))
        value = dot_nt(jnp.concatenate(highs + lows, axis=0), one_hot(width, q))
        out = value if out is None else out + value
    n = 32 * count
    for r in range(count):
        v = out[32 * r : 32 * r + 32] + out[n + 32 * r : n + 32 * r + 32]
        for y in range(2):
            out_ref.at[y][pl.ds(first + r, 16, stride=24), :] = v[16 * y : 16 * y + 16]


STEP = 16


def angle_parts(length):
    t = np.arange(length)
    coarse = 2.0 * np.pi * (np.outer(STEP * np.arange(length // 2 // STEP), t) % length) / length
    fine = 2.0 * np.pi * (np.outer(np.arange(STEP), t) % length) / length
    scale = 1.0 / math.sqrt(length)
    parts = [np.cos(coarse) * scale, np.sin(coarse) * scale, np.cos(fine), np.sin(fine)]
    return np.concatenate(parts).astype(np.float32)


def build_table(parts_ref, out_ref):
    length = out_ref.shape[0]
    n = length // 2 // STEP
    fine_cos, fine_sin = parts_ref[2 * n : 2 * n + STEP], parts_ref[2 * n + STEP : 2 * n + 2 * STEP]
    row = lax.broadcasted_iota(jnp.int32, (STEP, length), 0)
    sign = 1.0 - 2.0 * (lax.broadcasted_iota(jnp.int32, (STEP, length), 1) % 2).astype(f32)
    for i in range(n):
        cos, sin = parts_ref[i : i + 1], parts_ref[n + i : n + i + 1]
        low = -(sin * fine_cos + cos * fine_sin)
        if i == 0:
            low = jnp.where(row == 0, sign / math.sqrt(length), low)
        out_ref[i * STEP : (i + 1) * STEP] = (cos * fine_cos - sin * fine_sin).astype(bf16)
        out_ref[length // 2 + i * STEP : length // 2 + (i + 1) * STEP] = low.astype(bf16)


def forward_kernel(shape, widths, *refs):
    (pack, w0, w1, w2, w3, w4, ts, tl, cs, cl, ps, pl_) = refs[:12]
    (g_in, g_out, g_gate, g_up, g_down, v72, v24, v96, o_n1, o_proj, o_spec, o_carr, o_long,
     o_mixed, o_hid, o_n2, o_pd, o_ga, o_ap, o_ge, o_fs, o_fst, o_fl, o_flt) = refs[12:36]
    (f_small, f_in, f_out, f_gate, f_up, smallw, x, cot, n1, n1t, proj, spec, carr, longc,
     mixed, mixedt, hid, n2, n2t, ga, ap, ge, pd, pj, gl, vap, rhs, tr, prod, s_ps, s_pl, s_fs, s_fst,
     s_fl, s_flt, ici_send, ici_recv, core_send, core_recv, own_sem, load_sem, save_sem) = refs[36:]
    rows = shape.total
    short = shape.short
    zp, xp, yp, cp = neighbours()
    greet(zp + [xp, yp, cp])
    items = [(pack, f_small), (w0, f_in), (w1, f_out), (w2, f_gate), (w3, f_up), (w4, g_down)]
    g = Gather([(a, b, 0, a.shape[1]) for a, b in items], ici_send, ici_recv, core_send, core_recv, own_sem)
    steps = g.events(GATHER_ORDER)
    marks = {}
    for token in GATHER_ORDER:
        size = {"S": 1, "z": 3, "p": 8, "d": 4}[token[0]]
        marks[token] = size + (max(marks.values()) if marks else 0)
    position = [0]

    def pump(n):
        for step in steps[position[0] : position[0] + n]:
            step()
        position[0] = min(position[0] + n, len(steps))

    def need(k):
        pump(max(0, marks["d", k] - position[0]))
        g.done(k)

    pump(GATHER_FIRST)
    loads = []
    for a, b in [(ps, s_ps), (pl_, s_pl), (ts, x.at[0:short]), (tl, x.at[short:rows]),
                 (cs, cot.at[0:short]), (cl, cot.at[short:rows])]:
        copy = pltpu.make_async_copy(a, b, load_sem.at[len(loads)])
        copy.start()
        loads.append(copy)
    saves = []

    def save(a, b):
        copy = pltpu.make_async_copy(a, b, save_sem.at[len(saves)])
        copy.start()
        saves.append(copy)

    for start, length, place in shape.segs:
        zero = jnp.zeros((PAD, BLK), f32)
        for ref in (pj.at[0], pj.at[1], pj.at[2], vap):
            ref[place - PAD : place] = zero
            ref[place + length : place + length + PAD] = zero
    for copy in loads:
        copy.wait()
    build_table(s_ps, s_fs)
    build_table(s_pl, s_fl)
    pump(6)
    s_fst[...] = s_fs[...].T
    s_flt[...] = s_fl[...].T
    for a, b in ((s_fs, o_fs), (s_fst, o_fst), (s_fl, o_fl), (s_flt, o_flt)):
        save(a, b)
    need(0)
    for y in range(2):
        smallw[y] = f_small[:, y * 128 : (y + 1) * 128].astype(f32)
    unpack(smallw, 0, 4, widths[0], v72)
    pump(2)
    unpack(smallw, 4, 11, widths[1], v24)
    unpack(smallw, 15, 2, widths[2], v96)
    pump(2)

    def norm_one(i):
        r = rows_at(i, 64)
        h, _ = normal(x[r, :].astype(f32))
        n1[r, :] = (h * v24[6:7, :] + v24[7:8, :]).astype(bf16)

    loop(rows // 64, norm_one)
    pump(2)
    n1t[...] = n1[...].T
    save(n1t, o_n1)
    need(1)
    save(f_in, g_in)

    def mix(j, pumps):
        ch = slice(j * BLK, (j + 1) * BLK)
        los = [b * D + j * BLK for b in range(3)]
        tap = [[v72[1 + k : 2 + k, lo : lo + BLK] for k in range(3)] for lo in los]
        ctap = [v24[k : k + 1, ch] for k in range(3)]
        inner, outer = v24[3:4, ch], v24[4:5, ch]
        for b, lo in enumerate(los):
            value = dot(n1[...], f_in[:, lo : lo + BLK]) + v72[0:1, lo : lo + BLK]
            proj[:, lo : lo + BLK] = value.astype(bf16)
            for start, length, place in shape.segs:
                pj[b, place : place + length] = value[start : start + length]
        pump(pumps[0])
        n = shape.chunk

        def convolve(i):
            r, p = shape.plain(i), shape.place(i)
            here = pl.ds(p, n)
            gl[r, :] = taps3(window3(pj.at[0], p, n), tap[0])
            value = taps3(window3(pj.at[2], p, n), tap[2])
            vap[here, :] = value
            rhs[r, BLK:] = (taps3(window3(pj.at[1], p, n), tap[1]) * value).astype(bf16)

        def condition(i):
            rhs[shape.plain(i), :BLK] = taps3(window3(vap, shape.place(i), n), ctap).astype(bf16)

        loop(shape.count, convolve)
        loop(shape.count, condition)
        pump(pumps[1])
        for (start, length, _), table in zip(shape.segs, (s_fs, s_fl)):
            tr[start : start + length] = dot(table[...], rhs[start : start + length])

        def filt(i):
            a, b = shape.halves(i)
            sa, sb = tr[a, :BLK], tr[b, :BLK]
            ca, cb = tr[a, BLK:], tr[b, BLK:]
            spec[a, ch] = sa.astype(bf16)
            spec[b, ch] = sb.astype(bf16)
            carr[a, ch] = ca.astype(bf16)
            carr[b, ch] = cb.astype(bf16)
            fa = jnp.tanh(sa * inner) * outer
            fb = jnp.tanh(sb * inner) * outer
            real, imag = fa * ca, fb * cb
            row = lax.broadcasted_iota(jnp.int32, real.shape, 0)
            first = jnp.logical_and(row == 0, i <= 1)
            prod[a, :] = jnp.where(first, real, 2.0 * (real - imag)).astype(bf16)
            prod[b, :] = jnp.where(first, imag, 2.0 * (fa * cb + fb * ca)).astype(bf16)

        loop(shape.count, filt)
        pump(pumps[2])
        for (start, length, _), table in zip(shape.segs, (s_fst, s_flt)):
            value = dot(table[...], prod[start : start + length])
            longc[start : start + length, ch] = value.astype(bf16)
            mixed[start : start + length, ch] = (value * gl[start : start + length]).astype(bf16)

    for j in range(3):
        mix(j, MIX_PUMPS[j])
    for a, b in ((proj, o_proj), (spec, o_spec), (carr, o_carr), (longc, o_long)):
        save(a, b)
    pump(3)
    mixedt[...] = mixed[...].T
    save(mixedt, o_mixed)
    need(2)
    save(f_out, g_out)

    def branch_one(i):
        r = rows_at(i, 128)
        value = x[r, :].astype(f32) + dot(mixed[r, :], f_out[...]) + v24[5:6, :]
        hid[r, :] = value
        h, _ = normal(value)
        n2[r, :] = (h * v24[8:9, :] + v24[9:10, :]).astype(bf16)

    loop(rows // 128, branch_one)
    save(hid, o_hid)
    n2t[...] = n2[...].T
    save(n2t, o_n2)

    def glu(i):
        cols = rows_at(i, BLK)
        for m in range(0, rows, 320):
            gate = dot(n2[m : m + 320, :], f_gate[:, cols]) + v96[0:1, cols]
            up = dot(n2[m : m + 320, :], f_up[:, cols]) + v96[1:2, cols]
            square = gate * gate
            t = jnp.tanh(gate * (GELU_A + GELU_A * GELU_B * square))
            half = 0.5 * (1.0 + t)
            act = gate * half
            slope = half + 0.5 * gate * (1.0 - t * t) * (GELU_A + 3.0 * GELU_A * GELU_B * square)
            ga[m : m + 320, cols] = (act * up).astype(bf16)
            ge[m : m + 320, cols] = act.astype(bf16)
            ap[m : m + 320, cols] = (up * slope).astype(bf16)
        pd[cols, :] = dot(ga[:, cols].T, cot[...]).astype(bf16)

    need(3)
    save(f_gate, g_gate)
    need(4)
    save(f_up, g_up)
    tiles = ga.shape[1] // BLK

    def tile(i):
        glu(i)
        for q, n in enumerate(GLU_PUMPS):
            if n:
                pl.when(i == q)(functools.partial(pump, n))
        pl.when(i == tiles // 2 - 1)(save_first)

    def save_first():
        half = pd.shape[0] // 2
        first = slice(0, half)
        pairs = [(a.at[:, first], b.at[:, first]) for a, b in ((ga, o_ga), (ap, o_ap), (ge, o_ge))]
        for k, (a, b) in enumerate(pairs + [(pd.at[first], o_pd.at[first])]):
            pltpu.make_async_copy(a, b, load_sem.at[k]).start()

    loop(tiles, tile)
    half = pd.shape[0] // 2
    rest = slice(half, 2 * half)
    for a, b in ((ga, o_ga), (ap, o_ap), (ge, o_ge)):
        save(a.at[:, rest], b.at[:, rest])
    save(pd.at[rest], o_pd.at[rest])
    first = slice(0, half)
    early = [(a.at[:, first], b.at[:, first]) for a, b in ((ga, o_ga), (ap, o_ap), (ge, o_ge))]
    early.append((pd.at[first], o_pd.at[first]))
    for k, (a, b) in enumerate(early):
        pltpu.make_async_copy(a, b, load_sem.at[k]).wait()
    need(5)
    for copy in saves:
        copy.wait()
    g.finish()


GATHER_ORDER = (
    ("S", 0), ("S", 1), ("S", 2), ("z", 0), ("z", 1), ("p", 0), ("S", 3), ("d", 0), ("z", 2), ("p", 1), ("d", 1),
    ("z", 3), ("p", 2), ("S", 4), ("d", 2), ("p", 3), ("z", 4), ("S", 5), ("d", 3), ("p", 4), ("z", 5), ("d", 4),
    ("p", 5), ("d", 5),
)
GATHER_FIRST = 3
MIX_PUMPS = ((3, 3, 3), (4, 4, 4), (5, 5, 5))
GLU_PUMPS = (0, 2, 0, 2, 0, 2, 0, 2, 0, 2, 0, 2)


def place_rows(piece, first):
    rows, width = piece.shape
    return lax.pad(piece, jnp.zeros((), piece.dtype), ((first, 32 - first - rows, 0), (0, 128 - width, 0)))


LARGE = (0, 5, 11, 12, 14)
SMALL = (1, 2, 3, 4, 6, 7, 8, 9, 10, 15, 13)


def pack_small(shards):
    total = None
    first = 0
    for i in SMALL:
        piece = shards[i].reshape(-1, shards[i].shape[-1])
        placed = place_rows(piece, first)
        first += piece.shape[0]
        total = placed if total is None else total + placed
    return total


def forward(ts, tl, cs, cl, shards):
    shape = Rows(ts.shape[1], tl.shape[1])
    short, long, rows = shape.short, shape.long, shape.total
    widths = (shards[1].shape[0], shards[6].shape[0], shards[13].shape[1])
    large = [shards[i] for i in LARGE]
    ff = shards[11].shape[1] * 2
    full = [(16 * s.shape[0], 2 * s.shape[1]) for s in large]
    S = jax.ShapeDtypeStruct
    V = pltpu.VMEM
    angles = [angle_parts(short), angle_parts(long)]
    ins = [pack_small(shards)] + large + [ts.reshape(short, D), tl.reshape(long, D)]
    ins += [cs.reshape(short, D), cl.reshape(long, D)] + [jnp.asarray(a) for a in angles]
    square = [(n, n) for n in (short, short, long, long)]
    vecs = [(8, 32 * widths[0]), (16, 32 * widths[1]), (8, 32 * widths[2])]
    outs = [S(s, bf16) for s in full] + [S(s, f32) for s in vecs]
    outs += [S((D, rows), bf16), S((rows, 3 * D), bf16)] + [S((rows, D), bf16)] * 3
    outs += [S((D, rows), bf16), S((rows, D), f32), S((D, rows), bf16), S((ff, D), bf16)]
    outs += [S((rows, ff), bf16)] * 3 + [S(s, bf16) for s in square]
    any_ = pl.BlockSpec(memory_space=pl.ANY)
    vm = pl.BlockSpec(memory_space=pltpu.VMEM)
    sem = pltpu.SemaphoreType.DMA
    scratch = [V((512, 256), bf16)] + [V(s, bf16) for s in full[:4]]
    scratch += [V((2, 512, 128), f32), V((rows, D), bf16), V((rows, D), bf16), V((rows, D), bf16), V((D, rows), bf16)]
    scratch += [V((rows, 3 * D), bf16)] + [V((rows, D), bf16)] * 4
    scratch += [V((D, rows), bf16), V((rows, D), f32), V((rows, D), bf16), V((D, rows), bf16)]
    scratch += [V((rows, ff), bf16)] * 3 + [V((ff, D), bf16)]
    scratch += [V((3, shape.padded, BLK), f32), V((rows, BLK), f32), V((shape.padded, BLK), f32)]
    scratch += [V((rows, 2 * BLK), bf16), V((rows, 2 * BLK), f32), V((rows, BLK), bf16)]
    scratch += [V(a.shape, f32) for a in angles] + [V(s, bf16) for s in square]
    scratch += [sem((6, 15)), sem((6, 16)), sem((6, 16)), sem((6, 16)), sem((6,)), sem((6,)), sem((28,))]
    return pl.pallas_call(
        functools.partial(forward_kernel, shape, widths),
        out_shape=outs,
        in_specs=[any_] * len(ins),
        out_specs=[any_] * 5 + [vm] * 3 + [any_] * 16,
        scratch_shapes=scratch,
        compiler_params=pltpu.CompilerParams(collective_id=0, has_side_effects=True, vmem_limit_bytes=67043328),
    )(*ins)


class Reduce:
    def __init__(self, items, send_sem, recv_sem, own_sem):
        self.items = items
        self.send_sem, self.recv_sem, self.own_sem = send_sem, recv_sem, own_sem
        self.z, self.x, self.c, self.y = coords()
        self.zpeers, self.xpeer, self.ypeer, self.cpeer = neighbours()
        self.count = [0] * len(items)
        self.pending = []

    def post(self, k, src, dst, peer, slot):
        copy = pltpu.make_async_remote_copy(
            src_ref=src,
            dst_ref=dst,
            send_sem=self.send_sem.at[k, self.count[k]],
            recv_sem=self.recv_sem.at[k, slot],
            device_id=peer,
            device_id_type=MESH,
        )
        self.pending.append((k, self.count[k]))
        self.count[k] += 1
        copy.start()

    def arrived(self, k, dst, slot):
        pltpu.make_async_remote_copy(
            src_ref=dst,
            dst_ref=dst,
            send_sem=self.send_sem.at[k, 0],
            recv_sem=self.recv_sem.at[k, slot],
            device_id=self.cpeer,
            device_id_type=MESH,
        ).wait_recv()

    def part(self, k, b, core, yy):
        item = self.items[k]
        start = (2 * b + core) * item["rows"] + item["base"]
        rows = pl.ds(pl.multiple_of(start, 8), item["rows"])
        if item["flat"]:
            cols = item["cols"]
            return item["source"].at[rows, pl.ds(pl.multiple_of(yy * cols, 128), cols)]
        return item["source"].at[yy, rows, pl.ds(item["first"], item["cols"])]

    def own(self, k, b, yy):
        held = self.items[k]["held"]
        return held.at[b, yy] if held is not None else self.part(k, b, self.c, yy)

    def block(self, i, xx):
        return lax.rem(self.z + i, Z) * 2 + xx

    def order(self):
        for i in (1, 3, 2, 0):
            yield i, self.block(i, 1 - self.x), self.block(i, self.x)

    def core(self, k):
        item = self.items[k]
        for i, across, along in self.order():
            for b in (across, along):
                for yy in range(2):
                    self.post(k, self.part(k, b, 1 - self.c, yy), item["core"].at[b, yy], self.cpeer, b)
        if item["held"] is not None:
            for i, across, along in self.order():
                for b in (across, along):
                    for yy in range(2):
                        pltpu.make_async_copy(
                            self.part(k, b, self.c, yy), item["held"].at[b, yy], self.own_sem.at[b, yy]
                        ).start()

    def merge(self, k, b):
        item = self.items[k]
        if item["held"] is not None:
            for yy in range(2):
                pltpu.make_async_copy(
                    self.part(k, b, self.c, yy), item["held"].at[b, yy], self.own_sem.at[b, yy]
                ).wait()
        self.arrived(k, item["core"].at[b], b)
        for yy in range(2):
            own = self.own(k, b, yy)
            own[...] = own[...] + item["core"][b, yy]

    def diag(self, k):
        item = self.items[k]
        for i, across, along in self.order():
            self.merge(k, across)
            src = self.own(k, across, 1 - self.y)
            if i % 2 == 0:
                self.post(k, src, item["diag_x"].at[i // 2], self.xpeer, 8 + i // 2)
            else:
                self.post(k, src, item["diag_y"].at[i // 2], self.ypeer, 10 + i // 2)
        for i, across, along in self.order():
            self.merge(k, along)

    def near(self, k):
        item = self.items[k]
        for i, across, along in self.order():
            own = self.own(k, along, 1 - self.y)
            if i % 2 == 0:
                self.arrived(k, item["diag_x"].at[i // 2], 8 + i // 2)
                own[...] = own[...] + item["diag_x"][i // 2]
            self.post(k, own, item["near_y"].at[i], self.ypeer, 12 + i)
            own = self.own(k, across, self.y)
            if i % 2 == 1:
                self.arrived(k, item["diag_y"].at[i // 2], 10 + i // 2)
                own[...] = own[...] + item["diag_y"][i // 2]
            self.post(k, own, item["near_x"].at[i], self.xpeer, 16 + i)

    def far(self, k):
        item = self.items[k]
        for i, across, along in self.order():
            self.arrived(k, item["near_x"].at[i], 16 + i)
            self.arrived(k, item["near_y"].at[i], 12 + i)
            own = self.own(k, along, self.y)
            total = own[...].astype(f32) + item["near_x"][i].astype(f32) + item["near_y"][i].astype(f32)
            own[...] = total.astype(own.dtype)
            if i:
                self.post(k, own, item["far"].at[i - 1], self.zpeers[i - 1], 19 + i)

    def last(self, k):
        item = self.items[k]
        total = self.own(k, self.block(0, self.x), self.y)[...].astype(f32)
        for i in range(3):
            self.arrived(k, item["far"].at[i], 20 + i)
            total = total + item["far"][i].astype(f32)
        item["out"][...] = total

    def finish(self):
        for k, count in self.pending:
            rest = self.items[k]["far"].at[0]
            pltpu.make_async_remote_copy(
                src_ref=rest,
                dst_ref=rest,
                send_sem=self.send_sem.at[k, count],
                recv_sem=self.recv_sem.at[k, 0],
                device_id=self.cpeer,
                device_id_type=MESH,
            ).wait_send()


def backward_kernel(shape, widths, *refs):
    (pd, h_g, h_u, h_d, h_o, h_i, ts, tl, cs, cl, v72, v24, r_n1, r_proj, r_spec, r_carr, r_long,
     r_mixed, r_hid, r_n2, r_ga, r_ap, r_ge, fs, fst, fl, flt) = refs[:27]
    y_s, y_l, o_s, o_l, o_in, o_out, o_gate, o_up, o_down, o_small = refs[27:37]
    nitem = 10
    groups = [refs[37 + q * nitem : 37 + (q + 1) * nitem] for q in range(6)]
    (held, wd, wg, wu, wo, wi, p_small, cot, n2t, apb, geb, acc, big, gm, mixedt, gpj, bspec, bcarr, blong,
     pj, dco, vap, gr, dcp, rhs, tr, s_fs, s_fst, s_fl, s_flt, g72, g24, g96,
     send_sem, recv_sem, own_sem, load_sem, tile_sem, blk_sem, out_sem) = refs[37 + 6 * nitem :]
    rows, short = shape.total, shape.short
    zp, xp, yp, cp = neighbours()
    greet(zp + [xp, yp, cp])

    def item(k, source, out, nrows, cols, first=0, base=0, flat_form=False, held=None):
        names = ("core", "diag_x", "diag_y", "near_x", "near_y", "far")
        made = dict(source=source, out=out, rows=nrows, cols=cols, first=first, base=base, flat=flat_form, held=held)
        made.update({name: group[k] for name, group in zip(names, groups)})
        return made

    half = wg.shape[2] // 2
    span = wi.shape[2] // 3
    n = wi.shape[1]
    r_gate, r_in = o_gate.shape[0], o_in.shape[0]
    items = [
        item(0, pd, o_down, o_down.shape[0], o_down.shape[1], flat_form=True, held=held),
        item(1, wg, o_gate.at[:, 0:half], r_gate, half),
        item(2, wu, o_up.at[:, 0:half], r_gate, half),
        item(3, wg, o_gate.at[:, half : 2 * half], r_gate, half, first=half),
        item(4, wu, o_up.at[:, half : 2 * half], r_gate, half, first=half),
        item(5, wo, o_out, o_out.shape[0], o_out.shape[1]),
    ]
    for t in range(3):
        out = o_in.at[:, t * span : (t + 1) * span]
        items.append(item(6 + t, wd, out, r_in, span, base=t * n, flat_form=True))
    items.append(item(9, p_small, o_small, o_small.shape[0], o_small.shape[1]))
    red = Reduce(items, send_sem, recv_sem, own_sem)
    red.core(0)
    loads = {}

    def load(name, a, b):
        copy = pltpu.make_async_copy(a, b, load_sem.at[len(loads)])
        copy.start()
        loads[name] = copy

    def wait(*names):
        for name in names:
            loads[name].wait()

    def halves(name, a, b, first, size):
        cols = b.shape[2]
        for y in range(2):
            lo = y * cols + first
            load(name + str(y), a.at[:, lo : lo + size], b.at[y, :, first : first + size])

    load("cs", cs, cot.at[0:short])
    load("cl", cl, cot.at[short:rows])
    load("n2t", r_n2, n2t)
    quarter = wd.shape[0] // 4
    for q in (0, 2):
        load("wd%d" % q, h_d.at[q * quarter : (q + 1) * quarter], wd.at[q * quarter : (q + 1) * quarter])
    halves("ga", h_g, wg, 0, half)
    halves("ua", h_u, wu, 0, half)
    per = 2 * (half // BLK)
    total_tiles = 2 * per

    def tile_start(i):
        h, t, y = i // per, lax.rem(i, per) // 2, lax.rem(i, 2)
        return h * half + t * BLK, y

    def tile_copy(i, which):
        first, y = tile_start(i)
        cols = pl.ds(pl.multiple_of(y * 2 * half + first, BLK), BLK)
        slot = lax.rem(i, 2)
        src, dst = ((r_ap, apb), (r_ge, geb))[which]
        return pltpu.make_async_copy(src.at[:, cols], dst.at[slot], tile_sem.at[which, slot])

    for which in range(2):
        tile_copy(0, which).start()
    for q in (1, 3):
        load("wd%d" % q, h_d.at[q * quarter : (q + 1) * quarter], wd.at[q * quarter : (q + 1) * quarter])
    halves("gb", h_g, wg, half, half)
    halves("ub", h_u, wu, half, half)
    load("hid", r_hid, big)
    wide3 = gpj.shape[1]
    load("ga_a", r_ga.at[:, 0:wide3], gpj)
    load("ga_b", r_ga.at[:, wide3:], gm)
    load("mixedt", r_mixed, mixedt)
    halves("wo", h_o, wo, 0, wo.shape[2])
    halves("wi", h_i, wi, 0, wi.shape[2])
    for name, a, b in (("fs", fs, s_fs), ("fst", fst, s_fst), ("fl", fl, s_fl), ("flt", flt, s_flt)):
        load(name, a, b)

    def block_copies(j):
        ch = slice(j * BLK, (j + 1) * BLK)
        return [
            pltpu.make_async_copy(src.at[:, ch], dst, blk_sem.at[k])
            for k, (src, dst) in enumerate(((r_spec, bspec), (r_carr, bcarr), (r_long, blong)))
        ]

    for copy in block_copies(0):
        copy.start()
    acc[...] = jnp.zeros_like(acc)
    zero = jnp.zeros((PAD, BLK), f32)
    for start, length, place in shape.segs:
        for ref in (pj.at[0], pj.at[1], pj.at[2], dco, vap, dcp):
            ref[place - PAD : place] = zero
            ref[place + length : place + length + PAD] = zero
    g24[...] = jnp.zeros_like(g24)
    p_small[...] = jnp.zeros_like(p_small)
    red.diag(0)
    wait("cs", "cl", "n2t", "wd0", "wd2", "ga0", "ga1", "ua0", "ua1")

    def glu_back(i):
        first, y = tile_start(i)
        slot = lax.rem(i, 2)

        @pl.when(i + 1 < total_tiles)
        def _():
            for which in range(2):
                tile_copy(i + 1, which).start()

        for which in range(2):
            tile_copy(i, which).wait()
        cols = pl.ds(pl.multiple_of(first, BLK), BLK)
        every = pl.ds(pl.multiple_of(y * 2 * half + first, BLK), BLK)
        d_act = dot_nt(cot[...], wd[every, :])
        d_gate = (d_act * apb[slot].astype(f32)).astype(bf16)
        d_up = (d_act * geb[slot].astype(f32)).astype(bf16)
        g96[0:1, every] = jnp.sum(fold(d_gate.astype(f32)), axis=0, keepdims=True)
        g96[1:2, every] = jnp.sum(fold(d_up.astype(f32)), axis=0, keepdims=True)
        for m in range(0, rows, 320):
            acc[m : m + 320] += dot_nt(d_gate[m : m + 320], wg[y, :, cols]) + dot_nt(d_up[m : m + 320], wu[y, :, cols])
        wg[y, :, cols] = dot(n2t[...], d_gate).astype(bf16)
        wu[y, :, cols] = dot(n2t[...], d_up).astype(bf16)

    def tile_range(first, steps):
        def tile(i):
            glu_back(i + first)
            for q, step in steps.items():
                pl.when(i == q)(step)

        loop(per, tile)

    def both(*steps):
        def run():
            for name, k in steps:
                getattr(red, name)(k)

        return run

    tile_range(0, {2: both(("near", 0))})
    red.core(1)
    red.core(2)
    wait("wd1", "wd3", "gb0", "gb1", "ub0", "ub1")
    tile_range(per, {2: both(("diag", 1), ("diag", 2))})
    red.core(3)
    red.core(4)
    red.far(0)
    red.near(1)
    wait("hid", "ga_a", "ga_b")

    def branch_two(i):
        r = rows_at(i, 128)
        value = dot(gpj[r, :], wd[0:wide3, :]) + dot(gm[r, :], wd[wide3:, :])
        gm[r, :] = (big[r, :] + value + v24[10:11, :]).astype(bf16)

    loop(rows // 128, branch_two)
    outs = [
        pltpu.make_async_copy(gm.at[0:short], y_s, out_sem.at[0]),
        pltpu.make_async_copy(gm.at[short:rows], y_l, out_sem.at[1]),
    ]
    for copy in outs:
        copy.start()
    load("proj", r_proj, gpj)
    red.near(2)
    red.diag(3)
    red.diag(4)
    red.last(0)
    for copy in outs:
        copy.wait()

    def norm_two(i):
        r = rows_at(i, 64)
        h, scale = normal(big[r, :])
        d_norm = acc[r, :]
        c = cot[r, :].astype(f32)
        e = d_norm * v24[8:9, :]
        d_hid = c + scale * (e - jnp.mean(e, -1, keepdims=True) - h * jnp.mean(e * h, -1, keepdims=True))
        low = d_hid.astype(bf16)
        acc[r, :] = d_hid
        gm[r, :] = low
        for row, v in ((8, d_norm * h), (9, d_norm), (10, c), (5, low.astype(f32))):
            g24[row : row + 1, :] += jnp.sum(fold(v), axis=0, keepdims=True)

    loop(rows // 64, norm_two)
    red.far(1)
    wait("mixedt", "wo0", "wo1")
    wide = wo.shape[2]

    def out_back(i):
        r = rows_at(i, 128)
        big[r, :] = dot_nt(gm[r, 0:wide], wo[0]) + dot_nt(gm[r, wide : 2 * wide], wo[1])

    loop(rows // 128, out_back)
    for y in range(2):
        wo[y] = dot(mixedt[...], gm[:, y * wide : (y + 1) * wide]).astype(bf16)
    red.core(5)
    load("n1t", r_n1, n2t)
    load("ts", ts, gm.at[0:short])
    load("tl", tl, gm.at[short:rows])
    red.far(2)
    wait("proj", "fs", "fst", "fl", "flt")
    size = shape.chunk

    def mix_back(j, pumps):
        ch = slice(j * BLK, (j + 1) * BLK)
        los = [b * D + j * BLK for b in range(3)]
        tap = [[v72[1 + k : 2 + k, lo : lo + BLK] for k in range(3)] for lo in los]
        ctap = [v24[k : k + 1, ch] for k in range(3)]
        inner, outer = v24[3:4, ch], v24[4:5, ch]
        for copy in block_copies(j):
            copy.wait()

        def spread_out(i):
            here = pl.ds(shape.place(i), size)
            for b in range(3):
                pj[b, here, :] = gpj[shape.plain(i), los[b] : los[b] + BLK].astype(f32)

        def gates(i):
            r, p = shape.plain(i), shape.place(i)
            here = pl.ds(p, size)
            d_mix = big[r, ch]
            rhs[r, :BLK] = (d_mix * taps3(window3(pj.at[0], p, size), tap[0])).astype(bf16)
            dco[here, :] = d_mix * blong[r, :].astype(f32)
            gr[r, :] = taps3(window3(pj.at[1], p, size), tap[1])
            vap[here, :] = taps3(window3(pj.at[2], p, size), tap[2])

        loop(shape.count, spread_out)
        loop(shape.count, gates)

        def conv_down(b):
            def go(i, sums):
                r, p = shape.plain(i), shape.place(i)
                views = window3(dco, p, size)
                low = taps3(views, tap[b], True).astype(bf16)
                gpj[r, los[b] : los[b] + BLK] = low
                parts = [low.astype(f32)] + [views[1] * v for v in window3(pj.at[b], p, size)]
                return tuple(s + fold(v) for s, v in zip(sums, parts))

            sums = lax.fori_loop(0, shape.count, go, (jnp.zeros((8, BLK), f32),) * 4)
            for k in range(4):
                g72[k : k + 1, los[b] : los[b] + BLK] = jnp.sum(sums[k], axis=0, keepdims=True)

        for (start, length, _), table in zip(shape.segs, (s_fs, s_fl)):
            tr[start : start + length] = dot(table[...], rhs[start : start + length, :BLK])
        conv_down(0)
        pumps[0]()

        def filt_back(i, sums):
            a, b = shape.halves(i)
            pa, pb = tr[a, :], tr[b, :]
            sa, sb = bspec[a, :].astype(f32), bspec[b, :].astype(f32)
            ca, cb = bcarr[a, :].astype(f32), bcarr[b, :].astype(f32)
            ta, tb = jnp.tanh(sa * inner), jnp.tanh(sb * inner)
            fa, fb = ta * outer, tb * outer
            first = jnp.logical_and(lax.broadcasted_iota(jnp.int32, pa.shape, 0) == 0, i <= 1)
            pa = jnp.where(first, pa, 2.0 * pa)
            pb = jnp.where(first, pb, 2.0 * pb)
            ra, rb = pa * ca, pb * cb
            ua, ub = pa * fa, pb * fb
            dfa = jnp.where(first, ra, ra + rb)
            dfb = jnp.where(first, rb, pb * ca - pa * cb)
            rhs[a, BLK:] = jnp.where(first, ua, ua + ub).astype(bf16)
            rhs[b, BLK:] = jnp.where(first, ub, pb * fa - pa * fb).astype(bf16)
            dta, dtb = dfa * outer * (1.0 - ta * ta), dfb * outer * (1.0 - tb * tb)
            rhs[a, :BLK] = (dta * inner).astype(bf16)
            rhs[b, :BLK] = (dtb * inner).astype(bf16)
            return sums[0] + fold(dta * sa + dtb * sb), sums[1] + fold(dfa * ta + dfb * tb)

        sums = lax.fori_loop(0, shape.count, filt_back, (jnp.zeros((8, BLK), f32),) * 2)
        for k in range(2):
            g24[3 + k : 4 + k, ch] = jnp.sum(sums[k], axis=0, keepdims=True)
        if j < 2:
            for copy in block_copies(j + 1):
                copy.start()
        for (start, length, place), table in zip(shape.segs, (s_fst, s_flt)):
            dcp[place : place + length] = dot(table[...], rhs[start : start + length, :BLK])
            tr[start : start + length] = dot(table[...], rhs[start : start + length, BLK:])
        pumps[1]()

        def right(i):
            here = pl.ds(shape.place(i), size)
            dco[here, :] = tr[shape.plain(i), :] * vap[here, :]

        loop(shape.count, right)
        conv_down(1)

        def value(i, sums):
            r, p = shape.plain(i), shape.place(i)
            views = window3(dcp, p, size)
            dco[pl.ds(p, size), :] = taps3(views, ctap, True) + tr[r, :] * gr[r, :]
            return tuple(s + fold(views[1] * v) for s, v in zip(sums, window3(vap, p, size)))

        sums = lax.fori_loop(0, shape.count, value, (jnp.zeros((8, BLK), f32),) * 3)
        for k in range(3):
            g24[k : k + 1, ch] = jnp.sum(sums[k], axis=0, keepdims=True)
        conv_down(2)
        pumps[2]()

    none = lambda: None
    mix_back(0, [none, both(("diag", 5)), none])
    mix_back(1, [both(("near", 3)), both(("near", 4)), both(("last", 1))])
    mix_back(2, [both(("last", 2)), none, none])
    wait("n1t", "wi0", "wi1")

    def in_weight(i):
        t, y = i // 2, lax.rem(i, 2)
        cols = pl.ds(pl.multiple_of((3 * y + t) * span, 128), span)
        there = pl.ds(pl.multiple_of(y * span, 128), span)
        wd[rows_at(t, n), there] = dot(n2t[...], gpj[:, cols]).astype(bf16)
        for q, step in IN_STEPS.items():
            pl.when(i == q)(both(*step))

    loop(6, in_weight)
    deep = wi.shape[2]

    def in_back(i):
        r = rows_at(i, 128)
        big[r, :] = dot_nt(gpj[r, 0:deep], wi[0]) + dot_nt(gpj[r, deep : 2 * deep], wi[1])
        for q, step in BACK_STEPS.items():
            pl.when(i == q)(both(*step))

    loop(rows // 128, in_back)
    wait("ts", "tl")

    def norm_one(i):
        r = rows_at(i, 64)
        h, scale = normal(gm[r, :].astype(f32))
        d_norm = big[r, :]
        e = d_norm * v24[6:7, :]
        acc[r, :] += scale * (e - jnp.mean(e, -1, keepdims=True) - h * jnp.mean(e * h, -1, keepdims=True))
        for row, v in ((6, d_norm * h), (7, d_norm)):
            g24[row : row + 1, :] += jnp.sum(fold(v), axis=0, keepdims=True)

    loop(rows // 64, norm_one)
    outs = [
        pltpu.make_async_copy(acc.at[0:short], o_s, out_sem.at[0]),
        pltpu.make_async_copy(acc.at[short:rows], o_l, out_sem.at[1]),
    ]
    for copy in outs:
        copy.start()
    red.far(5)
    red.near(6)
    red.last(3)
    repack(g72, 4, widths[0], 0, p_small)
    red.near(7)
    repack(g24, 11, widths[1], 4, p_small)
    repack(g96, 2, widths[2], 15, p_small)
    red.core(9)
    both(*TAIL_STEPS)()
    for copy in outs:
        copy.wait()
    red.finish()


IN_STEPS = {
    1: (("core", 6), ("near", 5)),
    3: (("core", 7), ("far", 3)),
    5: (("core", 8), ("diag", 6)),
}
BACK_STEPS = {1: (("diag", 7),), 4: (("diag", 8), ("far", 4))}
TAIL_STEPS = (
    ("near", 8), ("last", 4), ("diag", 9), ("far", 6), ("near", 9), ("far", 7), ("far", 8), ("far", 9),
    ("last", 5), ("last", 6), ("last", 7), ("last", 8), ("last", 9),
)


def backward(ts, tl, cs, cl, shards, weights, vecs, res, tables):
    shape = Rows(ts.shape[1], tl.shape[1])
    short, long, rows = shape.short, shape.long, shape.total
    widths = (shards[1].shape[0], shards[6].shape[0], shards[13].shape[1])
    S = jax.ShapeDtypeStruct
    V = pltpu.VMEM
    w_in, w_out, w_gate, w_up, w_down = weights
    n1t, proj, spec, carr, longc, mixedt, hid, n2t, pd, ga, ap, ge = res
    ins = [pd, w_gate, w_up, w_down, w_out, w_in, ts.reshape(short, D), tl.reshape(long, D), cs.reshape(short, D),
           cl.reshape(long, D), vecs[0], vecs[1], n1t, proj, spec, carr, longc, mixedt, hid, n2t, ga, ap, ge]
    ins += list(tables)
    any_ = pl.BlockSpec(memory_space=pl.ANY)
    vm = pl.BlockSpec(memory_space=pltpu.VMEM)
    in_specs = [any_] * 10 + [vm] * 2 + [any_] * 15
    shard = [shards[i].shape for i in LARGE]
    outs = [S((short, D), bf16), S((long, D), bf16), S((short, D), f32), S((long, D), f32)]
    outs += [S(s, f32) for s in shard] + [S((24, 128), f32)]
    half, span = shard[2][1] // 2, shard[0][1] // 3
    dims = [shard[4]] + [(shard[2][0], half)] * 4 + [shard[1]] + [(shard[0][0], span)] * 3 + [(24, 128)]
    kinds = [bf16] * 9 + [f32]
    scratch = []
    for lead in ((8, 2), (2,), (2,), (4,), (4,), (3,)):
        scratch += [V(lead + d, t) for d, t in zip(dims, kinds)]
    wide = lambda s: (2, 16 * s[0], s[1])
    scratch += [
        V((8, 2) + shard[4], bf16), V((16 * shard[4][0], 2 * shard[4][1]), bf16), V(wide(shard[2]), bf16),
        V(wide(shard[3]), bf16), V(wide(shard[1]), bf16), V(wide(shard[0]), bf16), V((2, 384, 128), f32),
        V((rows, D), bf16), V((D, rows), bf16), V((2, rows, BLK), bf16), V((2, rows, BLK), bf16),
        V((rows, D), f32), V((rows, D), f32), V((rows, D), bf16), V((D, rows), bf16), V((rows, 3 * D), bf16),
        V((rows, BLK), bf16), V((rows, BLK), bf16), V((rows, BLK), bf16),
        V((3, shape.padded, BLK), f32), V((shape.padded, BLK), f32), V((shape.padded, BLK), f32),
        V((rows, BLK), f32), V((shape.padded, BLK), f32), V((rows, 2 * BLK), bf16), V((rows, BLK), f32),
    ]
    scratch += [V((m, m), bf16) for m in (short, short, long, long)]
    scratch += [V((8, 32 * widths[0]), f32), V((16, 32 * widths[1]), f32), V((8, 32 * widths[2]), f32)]
    sem = pltpu.SemaphoreType.DMA
    scratch += [sem((10, 31)), sem((10, 23)), sem((8, 2)), sem((36,)), sem((2, 2)), sem((3,)), sem((2,))]
    return pl.pallas_call(
        functools.partial(backward_kernel, shape, widths),
        out_shape=outs,
        in_specs=in_specs,
        out_specs=[any_] * 4 + [vm] * 6,
        scratch_shapes=scratch,
        compiler_params=pltpu.CompilerParams(collective_id=1, has_side_effects=True, vmem_limit_bytes=67043328),
    )(*ins)


def finish_kernel(spans, *refs):
    n = 9
    small, bulk = refs[0], refs[1 : 1 + n]
    outs = refs[1 + n : 1 + 2 * n]
    smalls = refs[1 + 2 * n : 1 + 2 * n + len(spans)]
    bufs = refs[1 + 2 * n + len(spans) : 1 + 3 * n + len(spans)]
    sem = refs[-1]
    ins = [pltpu.make_async_copy(a, b, sem.at[0, k]) for k, (a, b) in enumerate(zip(bulk, bufs))]
    for copy in ins:
        copy.start()
    for (first, count, width), ref in zip(spans, smalls):
        ref[...] = small[first : first + count, 0:width]
    back = [pltpu.make_async_copy(a, b, sem.at[1, k]) for k, (a, b) in enumerate(zip(bufs, outs))]
    for one, two in zip(ins, back):
        one.wait()
        two.start()
    for copy in back:
        copy.wait()


def finish(small, bulk, shards):
    spans = []
    first = 0
    for i in SMALL:
        s = shards[i].shape
        count = s[0] if len(s) == 2 else 1
        spans.append((first, count, s[-1]))
        first += count
    S = jax.ShapeDtypeStruct
    any_ = pl.BlockSpec(memory_space=pl.ANY)
    vm = pl.BlockSpec(memory_space=pltpu.VMEM)
    made = pl.pallas_call(
        functools.partial(finish_kernel, spans),
        out_shape=[S(a.shape, a.dtype) for a in bulk] + [S((c, w), f32) for _, c, w in spans],
        in_specs=[vm] + [any_] * len(bulk),
        out_specs=[any_] * len(bulk) + [vm] * len(spans),
        scratch_shapes=[pltpu.VMEM(a.shape, a.dtype) for a in bulk] + [pltpu.SemaphoreType.DMA((2, len(bulk)))],
    )(small, *bulk)
    grads = {i: v.reshape(shards[i].shape) for i, v in zip(SMALL, made[len(bulk) :])}
    return made[: len(bulk)], grads


def ring_step(ts, tl, cs, cl, shards):
    f = forward(ts, tl, cs, cl, shards)
    b = backward(ts, tl, cs, cl, shards, f[0:5], f[5:8], f[8:20], f[20:24])
    bulk, grads = finish(b[9], b[:9], shards)
    for i, g in zip(LARGE, bulk[4:9]):
        grads[i] = g
    seqs = (ts, tl, ts, tl)
    return tuple(v.reshape(s.shape) for v, s in zip(bulk, seqs)) + tuple(grads[i] for i in range(16))


def table(length):
    half = length // 2
    t = np.arange(length)
    k = np.arange(half)
    ang = 2.0 * np.pi * (np.outer(k, t) % length) / length
    top = np.cos(ang)
    low = -np.sin(ang)
    low[0] = np.where(t % 2 == 0, 1.0, -1.0)
    return (np.concatenate([top, low]) / math.sqrt(length)).astype(np.float32)

def dft(form, tab, v):
    return jnp.einsum(form, jnp.asarray(tab, bf16), v.astype(bf16), preferred_element_type=f32)

def down(v): return jnp.pad(v[:, :-1], ((0,0),(1,0),(0,0)))
def up(v): return jnp.pad(v[:, 1:], ((0,0),(0,1),(0,0)))
def conv(v, k): return k[0]*down(v)+k[1]*v+k[2]*up(v)
def conv_back(g, k): return k[0]*up(g)+k[1]*g+k[2]*down(g)
def conv_kernel(g, v):
    return jnp.stack([jnp.sum(g*down(v),(0,1)), jnp.sum(g*v,(0,1)), jnp.sum(g*up(v),(0,1))])

def weights(length):
    half = length//2
    w = np.full((half,1),2.0,np.float32); w[0]=1.0
    return np.concatenate([w,w])

def mixer_fwd(proj, sk, ck, fg):
    D = ck.shape[1]; L = proj.shape[1]; H=L//2
    tab = table(L); w = weights(L)
    co = conv(proj, sk)
    gl, gr, va = co[:,:,:D], co[:,:,D:2*D], co[:,:,2*D:]
    cond = conv(va, ck)
    spec = dft("kt,btc->bkc", tab, cond)
    carr = dft("kt,btc->bkc", tab, gr*va)
    th = jnp.tanh(spec*fg[0]); filt = th*fg[1]
    first = (lax.broadcasted_iota(jnp.int32,(H,1),0)==0)
    fa, fb, ca, cb = filt[:,:H], filt[:,H:], carr[:,:H], carr[:,H:]
    pa = fa*ca - jnp.where(first,0.0,fb*cb)
    pb = jnp.where(first, fb*cb, fa*cb+fb*ca)
    prod = jnp.concatenate([pa,pb],1)*w
    longc = dft("kt,bkc->btc", tab, prod)
    return gl*longc, (co, spec, th, carr, longc)

def mixer_bwd(dmix, proj, res, sk, ck, fg):
    co, spec, th, carr, longc = res
    D = ck.shape[1]; L = proj.shape[1]; H=L//2
    tab = table(L); w = weights(L)
    gl, gr, va = co[:,:,:D], co[:,:,D:2*D], co[:,:,2*D:]
    dgl = dmix*longc
    dlong = dmix*gl
    dp = dft("kt,btc->bkc", tab, dlong)*w
    filt = th*fg[1]
    first = (lax.broadcasted_iota(jnp.int32,(H,1),0)==0)
    fa, fb, ca, cb = filt[:,:H], filt[:,H:], carr[:,:H], carr[:,H:]
    da, db = dp[:,:H], dp[:,H:]
    dfa = da*ca + jnp.where(first,0.0,db*cb)
    dfb = jnp.where(first, db*cb, db*ca-da*cb)
    dca = da*fa + jnp.where(first,0.0,db*fb)
    dcb = jnp.where(first, db*fb, db*fa-da*fb)
    df = jnp.concatenate([dfa,dfb],1); dc = jnp.concatenate([dca,dcb],1)
    dth = df*fg[1]*(1-th*th)
    dfg = jnp.stack([jnp.sum(dth*spec,(0,1)), jnp.sum(df*th,(0,1))])
    dcond = dft("kt,bkc->btc", tab, dth*fg[0])
    dgv = dft("kt,bkc->btc", tab, dc)
    dck = conv_kernel(dcond, va)
    dva = conv_back(dcond, ck) + dgv*gr
    dgr = dgv*va
    dco = jnp.concatenate([dgl,dgr,dva],2)
    dsk = conv_kernel(dco, proj)
    return conv_back(dco, sk), dsk, dck, dfg

def mm(a,b): return jnp.dot(a,b,preferred_element_type=f32)
def tn(a,b): return lax.dot_general(a,b,(((0,),(0,)),((),())),preferred_element_type=f32)
def nt(a,b): return lax.dot_general(a,b,(((1,),(1,)),((),())),preferred_element_type=f32)

def norm(v):
    m = jnp.mean(v,-1,keepdims=True); d = v-m
    r = lax.rsqrt(jnp.mean(d*d,-1,keepdims=True)+1e-5)
    return d*r, r

def norm_back(e, h, r):
    return r*(e-jnp.mean(e,-1,keepdims=True)-h*jnp.mean(e*h,-1,keepdims=True))

C0=math.sqrt(2/math.pi); C1=0.044715
def gelu_parts(g):
    t = jnp.tanh(C0*(g+C1*g*g*g))
    return 0.5*g*(1+t), 0.5*(1+t)+0.5*g*(1-t*t)*C0*(1+3*C1*g*g)

def local(ts, tl, P, cs, cl):
    (iw, ib, sk, ck, fg, ow, ob, g1, b1, g2, b2, gw, uw, gb, dw, db) = [p if i in (0,5,11,12,14) else p.astype(f32) for i,p in enumerate(P)]
    D = ow.shape[0]
    ns = ts.shape[0]*ts.shape[1]
    x = jnp.concatenate([ts.reshape(-1,D),tl.reshape(-1,D)]).astype(f32)
    c = jnp.concatenate([cs.reshape(-1,D),cl.reshape(-1,D)])
    h1, r1 = norm(x)
    n1 = (h1*g1+b1).astype(bf16)
    proj = mm(n1, iw)+ib
    ps, pl_ = proj[:ns].reshape(ts.shape[0],ts.shape[1],3*D), proj[ns:].reshape(tl.shape[0],tl.shape[1],3*D)
    ms, rs = mixer_fwd(ps, sk, ck, fg); ml, rl = mixer_fwd(pl_, sk, ck, fg)
    mixed = jnp.concatenate([ms.reshape(-1,D),ml.reshape(-1,D)]).astype(bf16)
    hid = x + mm(mixed, ow)+ob
    h2, r2 = norm(hid)
    n2 = (h2*g2+b2).astype(bf16)
    gp = mm(n2,gw)+gb[0]; up_ = mm(n2,uw)+gb[1]
    ge, gd = gelu_parts(gp)
    ga = (ge*up_).astype(bf16)
    out = (hid+mm(ga,dw)+db).astype(bf16)
    cf = c.astype(f32)
    d_db = jnp.sum(cf,0); d_dw = tn(ga,c)
    dg = nt(c,dw)
    dgate = (dg*up_*gd).astype(bf16); dup=(dg*ge).astype(bf16)
    d_gb = jnp.stack([jnp.sum(dgate.astype(f32),0),jnp.sum(dup.astype(f32),0)])
    d_gw = tn(n2,dgate); d_uw = tn(n2,dup)
    dn2 = nt(dgate,gw)+nt(dup,uw)
    d_g2 = jnp.sum(dn2*h2,0); d_b2=jnp.sum(dn2,0)
    dh = cf + norm_back(dn2*g2,h2,r2)
    gm = dh.astype(bf16)
    d_ob = jnp.sum(gm.astype(f32),0); d_ow = tn(mixed,gm)
    dm = nt(gm,ow)
    dps, a1,a2,a3 = mixer_bwd(dm[:ns].reshape(ts.shape), ps, rs, sk, ck, fg)
    dpl, e1,e2,e3 = mixer_bwd(dm[ns:].reshape(tl.shape), pl_, rl, sk, ck, fg)
    gpj = jnp.concatenate([dps.reshape(-1,3*D),dpl.reshape(-1,3*D)]).astype(bf16)
    d_ib = jnp.sum(gpj.astype(f32),0); d_iw = tn(n1,gpj)
    dn1 = nt(gpj,iw)
    d_g1=jnp.sum(dn1*h1,0); d_b1=jnp.sum(dn1,0)
    dx = dh + norm_back(dn1*g1,h1,r1)
    return (out[:ns].reshape(ts.shape), out[ns:].reshape(tl.shape), dx[:ns].reshape(ts.shape), dx[ns:].reshape(tl.shape),
        d_iw,d_ib,a1+e1,a2+e2,a3+e3,d_ow,d_ob,d_g1,d_b1,d_g2,d_b2,d_gw,d_uw,d_gb,d_dw,d_db)


def fetch_plain(shards):
    params = []
    for i, shard in enumerate(shards):
        if i in LARGE:
            wide = lax.all_gather(shard, "narrow", axis=1, tiled=True)
            params.append(lax.all_gather(wide, "wide", axis=0, tiled=True))
        else:
            params.append(
                lax.all_gather(shard, ("wide", "narrow"), axis=shard.ndim - 1, tiled=True)
            )
    return params


def reduce_plain(grads, shards):
    outs = []
    for i, grad in enumerate(grads):
        if i in LARGE:
            block = lax.psum_scatter(grad.astype(bf16), "wide", scatter_dimension=0, tiled=True)
            block = lax.psum_scatter(block, "narrow", scatter_dimension=1, tiled=True)
            outs.append(block.astype(f32))
        else:
            outs.append(
                lax.psum_scatter(
                    grad, ("wide", "narrow"), scatter_dimension=grad.ndim - 1, tiled=True
                )
            )
    return outs


def plain_step(ts, tl, cs, cl, shards):
    results = local(ts, tl, fetch_plain(shards), cs, cl)
    return tuple(results[:4]) + tuple(reduce_plain(results[4:], shards))


def body(ring, ts, tl, *rest):
    step = ring_step if ring and ts.shape[0] == 1 and tl.shape[0] == 1 else plain_step
    return step(ts, tl, rest[16], rest[17], list(rest[:16]))


def solution(mesh):
    ring = mesh.shape["wide"] == 16 and mesh.shape["narrow"] == 2
    seq = P(("wide", "narrow"), None, None)
    mat = P("wide", "narrow")
    vec = P(("wide", "narrow"))
    pair = P(None, ("wide", "narrow"))
    params = (mat, vec, pair, pair, pair, mat, vec, vec, vec, vec, vec, mat, mat, pair, mat, vec)
    return jax.shard_map(
        functools.partial(body, ring),
        mesh=mesh,
        in_specs=(seq, seq) + params + (seq, seq),
        out_specs=(seq, seq, seq, seq) + params,
        check_vma=False,
    )
```

```python
import functools
import math

import jax
import jax.numpy as jnp
import numpy as np
from jax import lax
from jax.experimental import pallas as pl
from jax.experimental.pallas import tpu as pltpu
from jax.sharding import PartitionSpec as P

bf16 = jnp.bfloat16
f32 = jnp.float32
MESH = pl.DeviceIdType.MESH
Z = 4
D = 768
BLK = 256
PAD = 8


def coords():
    w = lax.axis_index("wide")
    return w // 4, (w // 2) % 2, w % 2, lax.axis_index("narrow")


def flat(z, x, c):
    return (z * 2 + x) * 2 + c


def greet(peers):
    barrier = pltpu.get_barrier_semaphore()
    for peer in peers:
        pl.semaphore_signal(barrier, inc=1, device_id=peer, device_id_type=MESH)
    pl.semaphore_wait(barrier, len(peers))


def neighbours():
    z, x, c, y = coords()
    zpeers = [(flat(lax.rem(z + i, Z), x, c), y) for i in (1, 2, 3)]
    return zpeers, (flat(z, 1 - x, c), y), (flat(z, x, c), 1 - y), (flat(z, x, 1 - c), y)


class Gather:
    def __init__(self, items, ici_send, ici_recv, core_send, core_recv, own_sem):
        self.items = items
        self.ici_send, self.ici_recv = ici_send, ici_recv
        self.core_send, self.core_recv, self.own_sem = core_send, core_recv, own_sem
        self.z, self.x, self.c, self.y = coords()
        self.zpeers, self.xpeer, self.ypeer, self.cpeer = neighbours()
        self.count = [0] * len(items)
        self.pending = []

    def shard(self, k):
        ref, _, first, cols = self.items[k]
        return ref if cols == ref.shape[1] else ref.at[:, first : first + cols]

    def view(self, k, i, xf, yf, cf=0):
        ref, full, first, cols = self.items[k]
        zz = lax.rem(self.z + i, Z)
        xx = 1 - self.x if xf else self.x
        yy = 1 - self.y if yf else self.y
        cc = 1 - self.c if cf else self.c
        rows, whole = ref.shape
        row = pl.multiple_of(flat(zz, xx, cc) * rows, 16)
        return full.at[pl.ds(row, rows), pl.ds(pl.multiple_of(yy * whole + first, 128), cols)]

    def copy(self, k, src, dst, peer, send, recv):
        return pltpu.make_async_remote_copy(
            src_ref=src, dst_ref=dst, send_sem=send, recv_sem=recv, device_id=peer, device_id_type=MESH
        )

    def post(self, k, i, xf, yf, peer, send, recv):
        src = self.shard(k) if (i, xf, yf) == (0, 0, 0) else self.view(k, i, xf, yf)
        self.pending.append((k, send))
        self.copy(k, src, self.view(k, i, xf, yf), peer, self.sent(k, send), recv).start()

    def sent(self, k, send):
        return (self.core_send if send[0] else self.ici_send).at[k, send[1]]

    def send(self, k, i, xf, yf, peer, slot):
        self.post(k, i, xf, yf, peer, (0, self.count[k]), self.ici_recv.at[k, slot])
        self.count[k] += 1

    def to_core(self, k, i, xf, yf):
        slot = i * 4 + xf * 2 + yf
        self.post(k, i, xf, yf, self.cpeer, (1, slot), self.core_recv.at[k, slot])

    def arrived(self, k, i, xf, yf, cf=0):
        slot = i * 4 + xf * 2 + yf
        sems = self.core_recv if cf else self.ici_recv
        dst = self.view(k, i, xf, yf, cf)
        self.copy(k, self.shard(k), dst, self.cpeer, self.ici_send.at[k, 0], sems.at[k, slot]).wait_recv()

    def own(self, k):
        return pltpu.make_async_copy(self.shard(k), self.view(k, 0, 0, 0), self.own_sem.at[k])

    def start(self, k):
        self.own(k).start()
        for i in (1, 3, 2):
            self.send(k, 0, 0, 0, self.zpeers[i - 1], ((Z - i) % Z) * 4)
        self.send(k, 0, 0, 0, self.xpeer, 2)
        self.send(k, 0, 0, 0, self.ypeer, 1)
        self.to_core(k, 0, 0, 0)

    def events(self, order):
        out = []
        for kind, k in order:
            if kind == "S":
                out.append(functools.partial(self.start, k))
            elif kind == "z":
                out += [functools.partial(self.zstep, k, i) for i in (1, 3, 2)]
            elif kind == "p":
                out += [functools.partial(self.xystep, k, i, xf) for i in (0, 1, 3, 2) for xf in (1, 0)]
            else:
                out += [functools.partial(self.dstep, k, i) for i in (0, 1, 3, 2)]
        return out

    def zstep(self, k, i):
        self.arrived(k, i, 0, 0)
        self.send(k, i, 0, 0, self.xpeer, i * 4 + 2)
        self.send(k, i, 0, 0, self.ypeer, i * 4 + 1)
        self.to_core(k, i, 0, 0)

    def xystep(self, k, i, xf):
        self.arrived(k, i, xf, 1 - xf)
        if i % 2 == 1 - xf:
            self.send(k, i, xf, 1 - xf, self.ypeer if xf else self.xpeer, i * 4 + 3)
        self.to_core(k, i, xf, 1 - xf)

    def dstep(self, k, i):
        self.arrived(k, i, 1, 1)
        self.to_core(k, i, 1, 1)

    def done(self, k):
        self.own(k).wait()
        for i in range(4):
            for xf in range(2):
                for yf in range(2):
                    self.arrived(k, i, xf, yf, 1)

    def finish(self):
        for k, send in self.pending:
            dst = self.view(k, 0, 0, 0)
            self.copy(k, self.shard(k), dst, self.cpeer, self.sent(k, send), self.ici_recv.at[k, 0]).wait_send()


def normal(v):
    centred = v - jnp.mean(v, axis=-1, keepdims=True)
    scale = lax.rsqrt(jnp.mean(centred * centred, axis=-1, keepdims=True) + 1e-5)
    return centred * scale, scale


def dot(a, b):
    return jnp.dot(a, b, preferred_element_type=f32)


def dot_nt(a, b):
    return lax.dot_general(a, b, (((1,), (1,)), ((), ())), preferred_element_type=f32)


def fold(v):
    return jnp.sum(v.reshape(v.shape[0] // 8, 8, v.shape[1]), axis=0)


def loop(count, fn):
    def go(i, carry):
        fn(i)
        return carry

    lax.fori_loop(0, count, go, 0)


def rows_at(i, size):
    return pl.ds(pl.multiple_of(i * size, size), size)


GELU_A = math.sqrt(2.0 / math.pi)
GELU_B = 0.044715


class Rows:
    def __init__(self, short, long):
        self.short, self.long = short, long
        self.total = short + long
        self.padded = self.total + 3 * PAD
        self.segs = ((0, short, PAD), (short, long, 2 * PAD + short))
        self.chunk = short
        self.count = self.total // short
        self.half = short // 2

    def plain(self, i):
        return rows_at(i, self.chunk)

    def place(self, i):
        return pl.multiple_of(i * self.chunk + PAD + PAD * jnp.minimum(i, 1), PAD)

    def halves(self, i):
        low = jnp.where(i == 0, 0, self.short + (i - 1) * self.half)
        high = low + jnp.where(i == 0, self.half, self.long // 2)
        return tuple(pl.ds(pl.multiple_of(v, self.half), self.half) for v in (low, high))


def window3(ref, p, n):
    span = ref[pl.ds(pl.multiple_of(p - PAD, PAD), n + 2 * PAD), :]
    return span[PAD - 1 : PAD - 1 + n], span[PAD : PAD + n], span[PAD + 1 : PAD + 1 + n]


def taps3(views, taps, flip=False):
    a, b, c = views
    return taps[0] * (c if flip else a) + taps[1] * b + taps[2] * (a if flip else c)


def owners(width, q):
    row = lax.broadcasted_iota(jnp.int32, (32, D), 0)
    owner = 2 * (row % 16) + row // 16
    col = lax.broadcasted_iota(jnp.int32, (32, D), 1) + q * D - owner * width
    return jnp.logical_and(col >= 0, col < width)


def one_hot(width, q):
    col = lax.broadcasted_iota(jnp.int32, (8, D), 1) + q * D
    whole = jnp.floor((col.astype(f32) + 0.5) * (1.0 / width)).astype(jnp.int32)
    place = (col - whole * width)[0:1]
    hit = lax.broadcasted_iota(jnp.int32, (128, D), 0) == place
    return jnp.where(hit, 1.0, 0.0).astype(bf16)


def unpack(wide_ref, first, count, width, out_ref):
    parts = []
    for r in range(first, first + count):
        for y in range(2):
            parts.append(wide_ref.at[y][pl.ds(r, 16, stride=32), :])
    parts = jnp.concatenate(parts, axis=0).astype(bf16)
    for q in range(32 * width // D):
        spread = dot(parts, one_hot(width, q))
        mine = owners(width, q)
        for r in range(count):
            piece = jnp.where(mine, spread[32 * r : 32 * r + 32], 0.0)
            out_ref[r : r + 1, q * D : (q + 1) * D] = jnp.sum(piece, axis=0, keepdims=True)


def repack(vec, count, width, first, out_ref):
    out = None
    for q in range(32 * width // D):
        mine = owners(width, q)
        highs, lows = [], []
        for r in range(count):
            v = jnp.where(mine, vec[r : r + 1, q * D : (q + 1) * D], 0.0)
            high = v.astype(bf16)
            highs.append(high)
            lows.append((v - high.astype(f32)).astype(bf16))
        value = dot_nt(jnp.concatenate(highs + lows, axis=0), one_hot(width, q))
        out = value if out is None else out + value
    n = 32 * count
    for r in range(count):
        v = out[32 * r : 32 * r + 32] + out[n + 32 * r : n + 32 * r + 32]
        for y in range(2):
            out_ref.at[y][pl.ds(first + r, 16, stride=24), :] = v[16 * y : 16 * y + 16]


STEP = 16


def angle_parts(length):
    t = np.arange(length)
    coarse = 2.0 * np.pi * (np.outer(STEP * np.arange(length // 2 // STEP), t) % length) / length
    fine = 2.0 * np.pi * (np.outer(np.arange(STEP), t) % length) / length
    scale = 1.0 / math.sqrt(length)
    parts = [np.cos(coarse) * scale, np.sin(coarse) * scale, np.cos(fine), np.sin(fine)]
    return np.concatenate(parts).astype(np.float32)


def build_table(parts_ref, out_ref):
    length = out_ref.shape[0]
    n = length // 2 // STEP
    fine_cos, fine_sin = parts_ref[2 * n : 2 * n + STEP], parts_ref[2 * n + STEP : 2 * n + 2 * STEP]
    row = lax.broadcasted_iota(jnp.int32, (STEP, length), 0)
    sign = 1.0 - 2.0 * (lax.broadcasted_iota(jnp.int32, (STEP, length), 1) % 2).astype(f32)
    for i in range(n):
        cos, sin = parts_ref[i : i + 1], parts_ref[n + i : n + i + 1]
        low = -(sin * fine_cos + cos * fine_sin)
        if i == 0:
            low = jnp.where(row == 0, sign / math.sqrt(length), low)
        out_ref[i * STEP : (i + 1) * STEP] = (cos * fine_cos - sin * fine_sin).astype(bf16)
        out_ref[length // 2 + i * STEP : length // 2 + (i + 1) * STEP] = low.astype(bf16)


def forward_kernel(shape, widths, *refs):
    (pack, w0, w1, w2, w3, w4, ts, tl, cs, cl, ps, pl_) = refs[:12]
    (g_in, g_out, g_gate, g_up, g_down, v72, v24, v96, o_n1, o_proj, o_spec, o_carr, o_long,
     o_mixed, o_hid, o_n2, o_pd, o_ga, o_ap, o_ge, o_fs, o_fst, o_fl, o_flt, o_gl, o_gr, o_va) = refs[12:39]
    (f_small, f_in, f_out, f_gate, f_up, smallw, x, cot, n1, n1t, proj, spec, carr, longc,
     mixed, mixedt, hid, n2, n2t, ga, ap, ge, pd, pj, gl, vap, rhs, tr, prod, lows, s_ps, s_pl, s_fs, s_fst,
     s_fl, s_flt, ici_send, ici_recv, core_send, core_recv, own_sem, load_sem, save_sem) = refs[39:]
    rows = shape.total
    short = shape.short
    zp, xp, yp, cp = neighbours()
    greet(zp + [xp, yp, cp])
    items = [(pack, f_small), (w0, f_in), (w1, f_out), (w2, f_gate), (w3, f_up), (w4, g_down)]
    g = Gather([(a, b, 0, a.shape[1]) for a, b in items], ici_send, ici_recv, core_send, core_recv, own_sem)
    steps = g.events(GATHER_ORDER)
    marks = {}
    for token in GATHER_ORDER:
        size = {"S": 1, "z": 3, "p": 8, "d": 4}[token[0]]
        marks[token] = size + (max(marks.values()) if marks else 0)
    position = [0]

    def pump(n):
        for step in steps[position[0] : position[0] + n]:
            step()
        position[0] = min(position[0] + n, len(steps))

    def need(k):
        pump(max(0, marks["d", k] - position[0]))
        g.done(k)

    pump(GATHER_FIRST)
    loads = []
    for a, b in [(ps, s_ps), (pl_, s_pl), (ts, x.at[0:short]), (tl, x.at[short:rows]),
                 (cs, cot.at[0:short]), (cl, cot.at[short:rows])]:
        copy = pltpu.make_async_copy(a, b, load_sem.at[len(loads)])
        copy.start()
        loads.append(copy)
    saves = []

    def save(a, b):
        copy = pltpu.make_async_copy(a, b, save_sem.at[len(saves)])
        copy.start()
        saves.append(copy)

    for start, length, place in shape.segs:
        zero = jnp.zeros((PAD, BLK), f32)
        for ref in (pj.at[0], pj.at[1], pj.at[2], vap):
            ref[place - PAD : place] = zero
            ref[place + length : place + length + PAD] = zero
    for copy in loads:
        copy.wait()
    build_table(s_ps, s_fs)
    build_table(s_pl, s_fl)
    pump(6)
    s_fst[...] = s_fs[...].T
    s_flt[...] = s_fl[...].T
    for a, b in ((s_fs, o_fs), (s_fst, o_fst), (s_fl, o_fl), (s_flt, o_flt)):
        save(a, b)
    need(0)
    for y in range(2):
        smallw[y] = f_small[:, y * 128 : (y + 1) * 128].astype(f32)
    unpack(smallw, 0, 4, widths[0], v72)
    pump(2)
    unpack(smallw, 4, 11, widths[1], v24)
    unpack(smallw, 15, 2, widths[2], v96)
    pump(2)

    def norm_one(i):
        r = rows_at(i, 64)
        h, _ = normal(x[r, :].astype(f32))
        n1[r, :] = (h * v24[6:7, :] + v24[7:8, :]).astype(bf16)

    loop(rows // 64, norm_one)
    pump(2)
    n1t[...] = n1[...].T
    save(n1t, o_n1)
    need(1)
    save(f_in, g_in)

    def mix(j, pumps):
        ch = slice(j * BLK, (j + 1) * BLK)
        los = [b * D + j * BLK for b in range(3)]
        tap = [[v72[1 + k : 2 + k, lo : lo + BLK] for k in range(3)] for lo in los]
        ctap = [v24[k : k + 1, ch] for k in range(3)]
        inner, outer = v24[3:4, ch], v24[4:5, ch]
        for b, lo in enumerate(los):
            value = dot(n1[...], f_in[:, lo : lo + BLK]) + v72[0:1, lo : lo + BLK]
            proj[:, lo : lo + BLK] = value.astype(bf16)
            for start, length, place in shape.segs:
                pj[b, place : place + length] = value[start : start + length]
        pump(pumps[0])
        n = shape.chunk

        def convolve(i):
            r, p = shape.plain(i), shape.place(i)
            here = pl.ds(p, n)
            left = taps3(window3(pj.at[0], p, n), tap[0])
            right = taps3(window3(pj.at[1], p, n), tap[1])
            value = taps3(window3(pj.at[2], p, n), tap[2])
            gl[r, :] = left
            vap[here, :] = value
            rhs[r, BLK:] = (right * value).astype(bf16)
            for q, v in enumerate((left, right, value)):
                lows[q, r, ch] = v.astype(bf16)

        def condition(i):
            rhs[shape.plain(i), :BLK] = taps3(window3(vap, shape.place(i), n), ctap).astype(bf16)

        loop(shape.count, convolve)
        loop(shape.count, condition)
        pump(pumps[1])
        for (start, length, _), table in zip(shape.segs, (s_fs, s_fl)):
            tr[start : start + length] = dot(table[...], rhs[start : start + length])

        def filt(i):
            a, b = shape.halves(i)
            sa, sb = tr[a, :BLK], tr[b, :BLK]
            ca, cb = tr[a, BLK:], tr[b, BLK:]
            spec[a, ch] = sa.astype(bf16)
            spec[b, ch] = sb.astype(bf16)
            carr[a, ch] = ca.astype(bf16)
            carr[b, ch] = cb.astype(bf16)
            fa = jnp.tanh(sa * inner) * outer
            fb = jnp.tanh(sb * inner) * outer
            real, imag = fa * ca, fb * cb
            row = lax.broadcasted_iota(jnp.int32, real.shape, 0)
            first = jnp.logical_and(row == 0, i <= 1)
            prod[a, :] = jnp.where(first, real, 2.0 * (real - imag)).astype(bf16)
            prod[b, :] = jnp.where(first, imag, 2.0 * (fa * cb + fb * ca)).astype(bf16)

        loop(shape.count, filt)
        pump(pumps[2])
        for (start, length, _), table in zip(shape.segs, (s_fst, s_flt)):
            value = dot(table[...], prod[start : start + length])
            longc[start : start + length, ch] = value.astype(bf16)
            mixed[start : start + length, ch] = (value * gl[start : start + length]).astype(bf16)

    for j in range(3):
        mix(j, MIX_PUMPS[j])
    for a, b in ((proj, o_proj), (spec, o_spec), (carr, o_carr), (longc, o_long)):
        save(a, b)
    for q, b in enumerate((o_gl, o_gr, o_va)):
        save(lows.at[q], b)
    pump(3)
    mixedt[...] = mixed[...].T
    save(mixedt, o_mixed)
    need(2)
    save(f_out, g_out)

    def branch_one(i):
        r = rows_at(i, 128)
        value = x[r, :].astype(f32) + dot(mixed[r, :], f_out[...]) + v24[5:6, :]
        hid[r, :] = value
        h, _ = normal(value)
        n2[r, :] = (h * v24[8:9, :] + v24[9:10, :]).astype(bf16)

    loop(rows // 128, branch_one)
    save(hid, o_hid)
    n2t[...] = n2[...].T
    save(n2t, o_n2)

    def gate_half(i):
        cols = rows_at(i, BLK)
        for m in range(0, rows, 320):
            gate = dot(n2[m : m + 320, :], f_gate[:, cols]) + v96[0:1, cols]
            square = gate * gate
            t = jnp.tanh(gate * (GELU_A + GELU_A * GELU_B * square))
            half = 0.5 * (1.0 + t)
            slope = half + 0.5 * gate * (1.0 - t * t) * (GELU_A + 3.0 * GELU_A * GELU_B * square)
            ge[m : m + 320, cols] = (gate * half).astype(bf16)
            ap[m : m + 320, cols] = slope.astype(bf16)

    def up_half(i):
        cols = rows_at(i, BLK)
        for m in range(0, rows, 320):
            up = dot(n2[m : m + 320, :], f_up[:, cols]) + v96[1:2, cols]
            ga[m : m + 320, cols] = (ge[m : m + 320, cols].astype(f32) * up).astype(bf16)
            ap[m : m + 320, cols] = (ap[m : m + 320, cols].astype(f32) * up).astype(bf16)
        pd[cols, :] = dot(ga[:, cols].T, cot[...]).astype(bf16)

    def pairs(part):
        return [(ga.at[:, part], o_ga.at[:, part]), (ap.at[:, part], o_ap.at[:, part]), (pd.at[part], o_pd.at[part])]

    def save_first():
        for k, (a, b) in enumerate(pairs(slice(0, pd.shape[0] // 2))):
            pltpu.make_async_copy(a, b, load_sem.at[k]).start()

    tiles = ga.shape[1] // BLK

    def staged(fn, counts, more):
        def tile(i):
            fn(i)
            for q, n in enumerate(counts):
                if n:
                    pl.when(i == q)(functools.partial(pump, n))
            if more:
                pl.when(i == tiles // 2 - 1)(save_first)

        loop(tiles, tile)

    need(3)
    save(f_gate, g_gate)
    staged(gate_half, GATE_PUMPS, False)
    save(ge, o_ge)
    need(4)
    save(f_up, g_up)
    staged(up_half, UP_PUMPS, True)
    half = pd.shape[0] // 2
    for a, b in pairs(slice(half, 2 * half)):
        save(a, b)
    for k, (a, b) in enumerate(pairs(slice(0, half))):
        pltpu.make_async_copy(a, b, load_sem.at[k]).wait()
    need(5)
    for copy in saves:
        copy.wait()
    g.finish()


GATHER_ORDER = (
    ("S", 0), ("S", 1), ("S", 2), ("S", 3), ("z", 0), ("z", 1), ("p", 0), ("d", 0), ("z", 2), ("p", 1), ("d", 1),
    ("z", 3), ("p", 2), ("S", 4), ("d", 2), ("p", 3), ("z", 4), ("S", 5), ("d", 3), ("p", 4), ("z", 5), ("d", 4),
    ("p", 5), ("d", 5),
)
GATHER_FIRST = 4
MIX_PUMPS = ((3, 3, 3), (4, 4, 4), (5, 5, 5))
GATE_PUMPS = (0, 2, 0, 2, 0, 2, 0, 2, 0, 2, 0, 2)
UP_PUMPS = (0, 2, 0, 2, 0, 2, 0, 2, 0, 2, 0, 2)


def place_rows(piece, first):
    rows, width = piece.shape
    return lax.pad(piece, jnp.zeros((), piece.dtype), ((first, 32 - first - rows, 0), (0, 128 - width, 0)))


LARGE = (0, 5, 11, 12, 14)
SMALL = (1, 2, 3, 4, 6, 7, 8, 9, 10, 15, 13)


def pack_small(shards):
    total = None
    first = 0
    for i in SMALL:
        piece = shards[i].reshape(-1, shards[i].shape[-1])
        placed = place_rows(piece, first)
        first += piece.shape[0]
        total = placed if total is None else total + placed
    return total


def forward(ts, tl, cs, cl, shards):
    shape = Rows(ts.shape[1], tl.shape[1])
    short, long, rows = shape.short, shape.long, shape.total
    widths = (shards[1].shape[0], shards[6].shape[0], shards[13].shape[1])
    large = [shards[i] for i in LARGE]
    ff = shards[11].shape[1] * 2
    full = [(16 * s.shape[0], 2 * s.shape[1]) for s in large]
    S = jax.ShapeDtypeStruct
    V = pltpu.VMEM
    angles = [angle_parts(short), angle_parts(long)]
    ins = [pack_small(shards)] + large + [ts.reshape(short, D), tl.reshape(long, D)]
    ins += [cs.reshape(short, D), cl.reshape(long, D)] + [jnp.asarray(a) for a in angles]
    square = [(n, n) for n in (short, short, long, long)]
    vecs = [(8, 32 * widths[0]), (16, 32 * widths[1]), (8, 32 * widths[2])]
    outs = [S(s, bf16) for s in full] + [S(s, f32) for s in vecs]
    outs += [S((D, rows), bf16), S((rows, 3 * D), bf16)] + [S((rows, D), bf16)] * 3
    outs += [S((D, rows), bf16), S((rows, D), f32), S((D, rows), bf16), S((ff, D), bf16)]
    outs += [S((rows, ff), bf16)] * 3 + [S(s, bf16) for s in square] + [S((rows, D), bf16)] * 3
    any_ = pl.BlockSpec(memory_space=pl.ANY)
    vm = pl.BlockSpec(memory_space=pltpu.VMEM)
    sem = pltpu.SemaphoreType.DMA
    scratch = [V((512, 256), bf16)] + [V(s, bf16) for s in full[:4]]
    scratch += [V((2, 512, 128), f32), V((rows, D), bf16), V((rows, D), bf16), V((rows, D), bf16), V((D, rows), bf16)]
    scratch += [V((rows, 3 * D), bf16)] + [V((rows, D), bf16)] * 4
    scratch += [V((D, rows), bf16), V((rows, D), f32), V((rows, D), bf16), V((D, rows), bf16)]
    scratch += [V((rows, ff), bf16)] * 3 + [V((ff, D), bf16)]
    scratch += [V((3, shape.padded, BLK), f32), V((rows, BLK), f32), V((shape.padded, BLK), f32)]
    scratch += [V((rows, 2 * BLK), bf16), V((rows, 2 * BLK), f32), V((rows, BLK), bf16), V((3, rows, D), bf16)]
    scratch += [V(a.shape, f32) for a in angles] + [V(s, bf16) for s in square]
    scratch += [sem((6, 15)), sem((6, 16)), sem((6, 16)), sem((6, 16)), sem((6,)), sem((6,)), sem((28,))]
    return pl.pallas_call(
        functools.partial(forward_kernel, shape, widths),
        out_shape=outs,
        in_specs=[any_] * len(ins),
        out_specs=[any_] * 5 + [vm] * 3 + [any_] * 19,
        scratch_shapes=scratch,
        compiler_params=pltpu.CompilerParams(collective_id=0, has_side_effects=True, vmem_limit_bytes=67043328),
    )(*ins)


class Reduce:
    def __init__(self, items, send_sem, recv_sem, own_sem):
        self.items = items
        self.send_sem, self.recv_sem, self.own_sem = send_sem, recv_sem, own_sem
        self.z, self.x, self.c, self.y = coords()
        self.zpeers, self.xpeer, self.ypeer, self.cpeer = neighbours()
        self.count = [0] * len(items)
        self.pending = []

    def post(self, k, src, dst, peer, slot):
        copy = pltpu.make_async_remote_copy(
            src_ref=src,
            dst_ref=dst,
            send_sem=self.send_sem.at[k, self.count[k]],
            recv_sem=self.recv_sem.at[k, slot],
            device_id=peer,
            device_id_type=MESH,
        )
        self.pending.append((k, self.count[k]))
        self.count[k] += 1
        copy.start()

    def arrived(self, k, dst, slot):
        pltpu.make_async_remote_copy(
            src_ref=dst,
            dst_ref=dst,
            send_sem=self.send_sem.at[k, 0],
            recv_sem=self.recv_sem.at[k, slot],
            device_id=self.cpeer,
            device_id_type=MESH,
        ).wait_recv()

    def part(self, k, b, core, yy):
        item = self.items[k]
        start = (2 * b + core) * item["rows"] + item["base"]
        rows = pl.ds(pl.multiple_of(start, 8), item["rows"])
        if item["flat"]:
            cols = item["cols"]
            return item["source"].at[rows, pl.ds(pl.multiple_of(yy * cols, 128), cols)]
        return item["source"].at[yy, rows, pl.ds(item["first"], item["cols"])]

    def own(self, k, b, yy):
        held = self.items[k]["held"]
        return held.at[b, yy] if held is not None else self.part(k, b, self.c, yy)

    def block(self, i, xx):
        return lax.rem(self.z + i, Z) * 2 + xx

    def order(self):
        for i in (1, 3, 2, 0):
            yield i, self.block(i, 1 - self.x), self.block(i, self.x)

    def core(self, k):
        item = self.items[k]
        for i, across, along in self.order():
            for b in (across, along):
                for yy in range(2):
                    self.post(k, self.part(k, b, 1 - self.c, yy), item["core"].at[b, yy], self.cpeer, b)
        if item["held"] is not None:
            for i, across, along in self.order():
                for b in (across, along):
                    for yy in range(2):
                        pltpu.make_async_copy(
                            self.part(k, b, self.c, yy), item["held"].at[b, yy], self.own_sem.at[b, yy]
                        ).start()

    def merge(self, k, b):
        item = self.items[k]
        if item["held"] is not None:
            for yy in range(2):
                pltpu.make_async_copy(
                    self.part(k, b, self.c, yy), item["held"].at[b, yy], self.own_sem.at[b, yy]
                ).wait()
        self.arrived(k, item["core"].at[b], b)
        for yy in range(2):
            own = self.own(k, b, yy)
            own[...] = own[...] + item["core"][b, yy]

    def diag(self, k):
        item = self.items[k]
        for i, across, along in self.order():
            self.merge(k, across)
            src = self.own(k, across, 1 - self.y)
            if i % 2 == 0:
                self.post(k, src, item["diag_x"].at[i // 2], self.xpeer, 8 + i // 2)
            else:
                self.post(k, src, item["diag_y"].at[i // 2], self.ypeer, 10 + i // 2)
        for i, across, along in self.order():
            self.merge(k, along)

    def near(self, k):
        item = self.items[k]
        for i, across, along in self.order():
            own = self.own(k, along, 1 - self.y)
            if i % 2 == 0:
                self.arrived(k, item["diag_x"].at[i // 2], 8 + i // 2)
                own[...] = own[...] + item["diag_x"][i // 2]
            self.post(k, own, item["near_y"].at[i], self.ypeer, 12 + i)
            own = self.own(k, across, self.y)
            if i % 2 == 1:
                self.arrived(k, item["diag_y"].at[i // 2], 10 + i // 2)
                own[...] = own[...] + item["diag_y"][i // 2]
            self.post(k, own, item["near_x"].at[i], self.xpeer, 16 + i)

    def far(self, k):
        item = self.items[k]
        for i, across, along in self.order():
            self.arrived(k, item["near_x"].at[i], 16 + i)
            self.arrived(k, item["near_y"].at[i], 12 + i)
            own = self.own(k, along, self.y)
            total = own[...].astype(f32) + item["near_x"][i].astype(f32) + item["near_y"][i].astype(f32)
            own[...] = total.astype(own.dtype)
            if i:
                self.post(k, own, item["far"].at[i - 1], self.zpeers[i - 1], 19 + i)

    def last(self, k):
        item = self.items[k]
        total = self.own(k, self.block(0, self.x), self.y)[...].astype(f32)
        for i in range(3):
            self.arrived(k, item["far"].at[i], 20 + i)
            total = total + item["far"][i].astype(f32)
        item["out"][...] = total

    def finish(self):
        for k, count in self.pending:
            rest = self.items[k]["far"].at[0]
            pltpu.make_async_remote_copy(
                src_ref=rest,
                dst_ref=rest,
                send_sem=self.send_sem.at[k, count],
                recv_sem=self.recv_sem.at[k, 0],
                device_id=self.cpeer,
                device_id_type=MESH,
            ).wait_send()


def backward_kernel(shape, widths, *refs):
    (pd, h_g, h_u, h_d, h_o, h_i, ts, tl, cs, cl, v72, v24, r_n1, r_proj, r_spec, r_carr, r_long,
     r_mixed, r_hid, r_n2, r_ga, r_ap, r_ge, fs, fst, fl, flt, r_gl, r_gr, r_va) = refs[:30]
    y_s, y_l, o_s, o_l, o_in, o_out, o_gate, o_up, o_down, o_small = refs[30:40]
    nitem = 10
    groups = [refs[40 + q * nitem : 40 + (q + 1) * nitem] for q in range(6)]
    (held, wd, wg, wu, wo, wi, p_small, cot, n2t, apb, geb, acc, big, gm, mixedt, gpj, bspec, bcarr, blong, bgl, bgr, bva,
     dco, dcp, rhs, tr, s_fs, s_fst, s_fl, s_flt, g72, g24, g96,
     send_sem, recv_sem, own_sem, load_sem, tile_sem, blk_sem, out_sem) = refs[40 + 6 * nitem :]
    rows, short = shape.total, shape.short
    zp, xp, yp, cp = neighbours()
    greet(zp + [xp, yp, cp])

    def item(k, source, out, nrows, cols, first=0, base=0, flat_form=False, held=None):
        names = ("core", "diag_x", "diag_y", "near_x", "near_y", "far")
        made = dict(source=source, out=out, rows=nrows, cols=cols, first=first, base=base, flat=flat_form, held=held)
        made.update({name: group[k] for name, group in zip(names, groups)})
        return made

    half = wg.shape[2] // 2
    span = wi.shape[2] // 3
    n = wi.shape[1]
    r_gate, r_in = o_gate.shape[0], o_in.shape[0]
    items = [
        item(0, pd, o_down, o_down.shape[0], o_down.shape[1], flat_form=True, held=held),
        item(1, wg, o_gate.at[:, 0:half], r_gate, half),
        item(2, wu, o_up.at[:, 0:half], r_gate, half),
        item(3, wg, o_gate.at[:, half : 2 * half], r_gate, half, first=half),
        item(4, wu, o_up.at[:, half : 2 * half], r_gate, half, first=half),
        item(5, wo, o_out, o_out.shape[0], o_out.shape[1]),
    ]
    for t in range(3):
        out = o_in.at[:, t * span : (t + 1) * span]
        items.append(item(6 + t, wd, out, r_in, span, base=t * n, flat_form=True))
    items.append(item(9, p_small, o_small, o_small.shape[0], o_small.shape[1]))
    red = Reduce(items, send_sem, recv_sem, own_sem)
    red.core(0)
    loads = {}

    def load(name, a, b):
        copy = pltpu.make_async_copy(a, b, load_sem.at[len(loads)])
        copy.start()
        loads[name] = copy

    def wait(*names):
        for name in names:
            loads[name].wait()

    def halves(name, a, b, first, size):
        cols = b.shape[2]
        for y in range(2):
            lo = y * cols + first
            load(name + str(y), a.at[:, lo : lo + size], b.at[y, :, first : first + size])

    load("cs", cs, cot.at[0:short])
    load("cl", cl, cot.at[short:rows])
    load("n2t", r_n2, n2t)
    quarter = wd.shape[0] // 4
    for q in (0, 2):
        load("wd%d" % q, h_d.at[q * quarter : (q + 1) * quarter], wd.at[q * quarter : (q + 1) * quarter])
    halves("ga", h_g, wg, 0, half)
    halves("ua", h_u, wu, 0, half)
    per = 2 * (half // BLK)
    total_tiles = 2 * per

    def tile_start(i):
        h, t, y = i // per, lax.rem(i, per) // 2, lax.rem(i, 2)
        return h * half + t * BLK, y

    def tile_copy(i, which):
        first, y = tile_start(i)
        cols = pl.ds(pl.multiple_of(y * 2 * half + first, BLK), BLK)
        slot = lax.rem(i, 2)
        src, dst = ((r_ap, apb), (r_ge, geb))[which]
        return pltpu.make_async_copy(src.at[:, cols], dst.at[slot], tile_sem.at[which, slot])

    for which in range(2):
        tile_copy(0, which).start()
    for q in (1, 3):
        load("wd%d" % q, h_d.at[q * quarter : (q + 1) * quarter], wd.at[q * quarter : (q + 1) * quarter])
    halves("gb", h_g, wg, half, half)
    halves("ub", h_u, wu, half, half)
    load("hid", r_hid, big)
    wide3 = gpj.shape[1]
    load("ga_a", r_ga.at[:, 0:wide3], gpj)
    load("ga_b", r_ga.at[:, wide3:], gm)
    load("mixedt", r_mixed, mixedt)
    halves("wo", h_o, wo, 0, wo.shape[2])
    halves("wi", h_i, wi, 0, wi.shape[2])
    for name, a, b in (("fs", fs, s_fs), ("fst", fst, s_fst), ("fl", fl, s_fl), ("flt", flt, s_flt)):
        load(name, a, b)

    blocks = ((r_spec, bspec), (r_carr, bcarr), (r_long, blong), (r_gl, bgl), (r_gr, bgr), (r_va, bva))

    def block_copies(j, first, last):
        ch = slice(j * BLK, (j + 1) * BLK)
        return [
            pltpu.make_async_copy(blocks[k][0].at[:, ch], blocks[k][1], blk_sem.at[k]) for k in range(first, last)
        ]

    for copy in block_copies(0, 0, 6):
        copy.start()
    acc[...] = jnp.zeros_like(acc)
    zero = jnp.zeros((PAD, BLK), f32)
    for start, length, place in shape.segs:
        for ref in (dco, dcp):
            ref[place - PAD : place] = zero
            ref[place + length : place + length + PAD] = zero
    g24[...] = jnp.zeros_like(g24)
    p_small[...] = jnp.zeros_like(p_small)
    red.diag(0)
    wait("cs", "cl", "n2t", "wd0", "wd2", "ga0", "ga1", "ua0", "ua1")

    def glu_back(i):
        first, y = tile_start(i)
        slot = lax.rem(i, 2)

        @pl.when(i + 1 < total_tiles)
        def _():
            for which in range(2):
                tile_copy(i + 1, which).start()

        for which in range(2):
            tile_copy(i, which).wait()
        cols = pl.ds(pl.multiple_of(first, BLK), BLK)
        every = pl.ds(pl.multiple_of(y * 2 * half + first, BLK), BLK)
        d_act = dot_nt(cot[...], wd[every, :])
        d_gate = (d_act * apb[slot].astype(f32)).astype(bf16)
        d_up = (d_act * geb[slot].astype(f32)).astype(bf16)
        g96[0:1, every] = jnp.sum(fold(d_gate.astype(f32)), axis=0, keepdims=True)
        g96[1:2, every] = jnp.sum(fold(d_up.astype(f32)), axis=0, keepdims=True)
        for m in range(0, rows, 320):
            acc[m : m + 320] += dot_nt(d_gate[m : m + 320], wg[y, :, cols]) + dot_nt(d_up[m : m + 320], wu[y, :, cols])
        wg[y, :, cols] = dot(n2t[...], d_gate).astype(bf16)
        wu[y, :, cols] = dot(n2t[...], d_up).astype(bf16)

    def tile_range(first, steps):
        def tile(i):
            glu_back(i + first)
            for q, step in steps.items():
                pl.when(i == q)(step)

        loop(per, tile)

    def both(*steps):
        def run():
            for name, k in steps:
                getattr(red, name)(k)

        return run

    tile_range(0, {2: both(("near", 0))})
    red.core(1)
    red.core(2)
    wait("wd1", "wd3", "gb0", "gb1", "ub0", "ub1")
    tile_range(per, {2: both(("diag", 1), ("diag", 2))})
    red.core(3)
    red.core(4)
    red.far(0)
    red.near(1)
    wait("hid", "ga_a", "ga_b")

    def branch_two(i):
        r = rows_at(i, 128)
        value = dot(gpj[r, :], wd[0:wide3, :]) + dot(gm[r, :], wd[wide3:, :])
        gm[r, :] = (big[r, :] + value + v24[10:11, :]).astype(bf16)

    loop(rows // 128, branch_two)
    outs = [
        pltpu.make_async_copy(gm.at[0:short], y_s, out_sem.at[0]),
        pltpu.make_async_copy(gm.at[short:rows], y_l, out_sem.at[1]),
    ]
    for copy in outs:
        copy.start()
    load("proj", r_proj, gpj)
    red.near(2)
    red.diag(3)
    red.diag(4)
    for copy in outs:
        copy.wait()

    def norm_two(i):
        r = rows_at(i, 64)
        h, scale = normal(big[r, :])
        d_norm = acc[r, :]
        c = cot[r, :].astype(f32)
        e = d_norm * v24[8:9, :]
        d_hid = c + scale * (e - jnp.mean(e, -1, keepdims=True) - h * jnp.mean(e * h, -1, keepdims=True))
        low = d_hid.astype(bf16)
        acc[r, :] = d_hid
        gm[r, :] = low
        for row, v in ((8, d_norm * h), (9, d_norm), (10, c), (5, low.astype(f32))):
            g24[row : row + 1, :] += jnp.sum(fold(v), axis=0, keepdims=True)

    loop(rows // 64, norm_two)
    wait("mixedt", "wo0", "wo1")
    wide = wo.shape[2]

    def out_back(i):
        r = rows_at(i, 128)
        big[r, :] = dot_nt(gm[r, 0:wide], wo[0]) + dot_nt(gm[r, wide : 2 * wide], wo[1])

    loop(rows // 128, out_back)
    for y in range(2):
        wo[y] = dot(mixedt[...], gm[:, y * wide : (y + 1) * wide]).astype(bf16)
    red.core(5)
    load("n1t", r_n1, n2t)
    load("ts", ts, gm.at[0:short])
    load("tl", tl, gm.at[short:rows])
    red.far(1)
    wait("proj", "fs", "fst", "fl", "flt")
    size = shape.chunk

    def mix_back(j, pumps):
        ch = slice(j * BLK, (j + 1) * BLK)
        los = [b * D + j * BLK for b in range(3)]
        tap = [[v72[1 + k : 2 + k, lo : lo + BLK] for k in range(3)] for lo in los]
        ctap = [v24[k : k + 1, ch] for k in range(3)]
        inner, outer = v24[3:4, ch], v24[4:5, ch]
        for copy in block_copies(j, 0, 4):
            copy.wait()

        def gates(i):
            r = shape.plain(i)
            d_mix = big[r, ch]
            rhs[r, :BLK] = (d_mix * bgl[r, :].astype(f32)).astype(bf16)
            dco[pl.ds(shape.place(i), size), :] = d_mix * blong[r, :].astype(f32)

        loop(shape.count, gates)

        def conv_down(b):
            def go(i, sums):
                r, p = shape.plain(i), shape.place(i)
                views = window3(dco, p, size)
                low = taps3(views, tap[b], True).astype(bf16)
                given = gpj[r, los[b] : los[b] + BLK].astype(f32)
                gpj[r, los[b] : los[b] + BLK] = low
                parts = [low.astype(f32)] + [views[2 - k] * given for k in range(3)]
                return tuple(s + fold(v) for s, v in zip(sums, parts))

            sums = lax.fori_loop(0, shape.count, go, (jnp.zeros((8, BLK), f32),) * 4)
            for k in range(4):
                g72[k : k + 1, los[b] : los[b] + BLK] = jnp.sum(sums[k], axis=0, keepdims=True)

        for (start, length, _), table in zip(shape.segs, (s_fs, s_fl)):
            tr[start : start + length] = dot(table[...], rhs[start : start + length, :BLK])
        conv_down(0)
        pumps[0]()

        def filt_back(i, sums):
            a, b = shape.halves(i)
            pa, pb = tr[a, :], tr[b, :]
            sa, sb = bspec[a, :].astype(f32), bspec[b, :].astype(f32)
            ca, cb = bcarr[a, :].astype(f32), bcarr[b, :].astype(f32)
            ta, tb = jnp.tanh(sa * inner), jnp.tanh(sb * inner)
            fa, fb = ta * outer, tb * outer
            first = jnp.logical_and(lax.broadcasted_iota(jnp.int32, pa.shape, 0) == 0, i <= 1)
            pa = jnp.where(first, pa, 2.0 * pa)
            pb = jnp.where(first, pb, 2.0 * pb)
            ra, rb = pa * ca, pb * cb
            ua, ub = pa * fa, pb * fb
            dfa = jnp.where(first, ra, ra + rb)
            dfb = jnp.where(first, rb, pb * ca - pa * cb)
            rhs[a, BLK:] = jnp.where(first, ua, ua + ub).astype(bf16)
            rhs[b, BLK:] = jnp.where(first, ub, pb * fa - pa * fb).astype(bf16)
            dta, dtb = dfa * outer * (1.0 - ta * ta), dfb * outer * (1.0 - tb * tb)
            rhs[a, :BLK] = (dta * inner).astype(bf16)
            rhs[b, :BLK] = (dtb * inner).astype(bf16)
            return sums[0] + fold(dta * sa + dtb * sb), sums[1] + fold(dfa * ta + dfb * tb)

        sums = lax.fori_loop(0, shape.count, filt_back, (jnp.zeros((8, BLK), f32),) * 2)
        for k in range(2):
            g24[3 + k : 4 + k, ch] = jnp.sum(sums[k], axis=0, keepdims=True)
        if j < 2:
            for copy in block_copies(j + 1, 0, 4):
                copy.start()
        for copy in block_copies(j, 4, 6):
            copy.wait()
        for (start, length, place), table in zip(shape.segs, (s_fst, s_flt)):
            dcp[place : place + length] = dot(table[...], rhs[start : start + length, :BLK])
            tr[start : start + length] = dot(table[...], rhs[start : start + length, BLK:])
        pumps[1]()

        def right(i):
            here = pl.ds(shape.place(i), size)
            r = shape.plain(i)
            dco[here, :] = tr[r, :] * bva[r, :].astype(f32)

        loop(shape.count, right)
        conv_down(1)

        def value(i, sums):
            r, p = shape.plain(i), shape.place(i)
            views = window3(dcp, p, size)
            dco[pl.ds(p, size), :] = taps3(views, ctap, True) + tr[r, :] * bgr[r, :].astype(f32)
            given = bva[r, :].astype(f32)
            return tuple(s + fold(views[2 - k] * given) for k, s in enumerate(sums))

        sums = lax.fori_loop(0, shape.count, value, (jnp.zeros((8, BLK), f32),) * 3)
        for k in range(3):
            g24[k : k + 1, ch] = jnp.sum(sums[k], axis=0, keepdims=True)
        if j < 2:
            for copy in block_copies(j + 1, 4, 6):
                copy.start()
        conv_down(2)
        pumps[2]()

    none = lambda: None
    mix_back(0, [none, both(("diag", 5)), both(("far", 2))])
    mix_back(1, [both(("near", 3)), both(("near", 4)), none])
    mix_back(2, [none, none, none])
    wait("n1t", "wi0", "wi1")

    def in_weight(i):
        t, y = i // 2, lax.rem(i, 2)
        cols = pl.ds(pl.multiple_of((3 * y + t) * span, 128), span)
        there = pl.ds(pl.multiple_of(y * span, 128), span)
        wd[rows_at(t, n), there] = dot(n2t[...], gpj[:, cols]).astype(bf16)
        for q, step in IN_STEPS.items():
            pl.when(i == q)(both(*step))

    loop(6, in_weight)
    deep = wi.shape[2]

    def in_back(i):
        r = rows_at(i, 128)
        big[r, :] = dot_nt(gpj[r, 0:deep], wi[0]) + dot_nt(gpj[r, deep : 2 * deep], wi[1])
        for q, step in BACK_STEPS.items():
            pl.when(i == q)(both(*step))

    loop(rows // 128, in_back)
    wait("ts", "tl")

    def norm_one(i):
        r = rows_at(i, 64)
        h, scale = normal(gm[r, :].astype(f32))
        d_norm = big[r, :]
        e = d_norm * v24[6:7, :]
        acc[r, :] += scale * (e - jnp.mean(e, -1, keepdims=True) - h * jnp.mean(e * h, -1, keepdims=True))
        for row, v in ((6, d_norm * h), (7, d_norm)):
            g24[row : row + 1, :] += jnp.sum(fold(v), axis=0, keepdims=True)

    loop(rows // 64, norm_one)
    outs = [
        pltpu.make_async_copy(acc.at[0:short], o_s, out_sem.at[0]),
        pltpu.make_async_copy(acc.at[short:rows], o_l, out_sem.at[1]),
    ]
    for copy in outs:
        copy.start()
    red.far(5)
    red.near(6)
    repack(g72, 4, widths[0], 0, p_small)
    red.near(7)
    repack(g24, 11, widths[1], 4, p_small)
    repack(g96, 2, widths[2], 15, p_small)
    red.core(9)
    both(*TAIL_STEPS)()
    for copy in outs:
        copy.wait()
    red.finish()


IN_STEPS = {
    1: (("core", 6), ("near", 5)),
    3: (("core", 7), ("far", 3)),
    5: (("core", 8), ("diag", 6)),
}
BACK_STEPS = {1: (("diag", 7),), 4: (("diag", 8), ("far", 4))}
TAIL_STEPS = (
    ("near", 8), ("diag", 9), ("far", 6), ("near", 9), ("far", 7), ("far", 8), ("far", 9),
    ("last", 0), ("last", 1), ("last", 2), ("last", 3), ("last", 4), ("last", 5), ("last", 6), ("last", 7), ("last", 8), ("last", 9),
)


def backward(ts, tl, cs, cl, shards, weights, vecs, res, tables):
    shape = Rows(ts.shape[1], tl.shape[1])
    short, long, rows = shape.short, shape.long, shape.total
    widths = (shards[1].shape[0], shards[6].shape[0], shards[13].shape[1])
    S = jax.ShapeDtypeStruct
    V = pltpu.VMEM
    w_in, w_out, w_gate, w_up, w_down = weights
    n1t, proj, spec, carr, longc, mixedt, hid, n2t, pd, ga, ap, ge = res[:12]
    ins = [pd, w_gate, w_up, w_down, w_out, w_in, ts.reshape(short, D), tl.reshape(long, D), cs.reshape(short, D),
           cl.reshape(long, D), vecs[0], vecs[1], n1t, proj, spec, carr, longc, mixedt, hid, n2t, ga, ap, ge]
    ins += list(tables) + list(res[12:])
    any_ = pl.BlockSpec(memory_space=pl.ANY)
    vm = pl.BlockSpec(memory_space=pltpu.VMEM)
    in_specs = [any_] * 10 + [vm] * 2 + [any_] * 18
    shard = [shards[i].shape for i in LARGE]
    outs = [S((short, D), bf16), S((long, D), bf16), S((short, D), f32), S((long, D), f32)]
    outs += [S(s, f32) for s in shard] + [S((24, 128), f32)]
    half, span = shard[2][1] // 2, shard[0][1] // 3
    dims = [shard[4]] + [(shard[2][0], half)] * 4 + [shard[1]] + [(shard[0][0], span)] * 3 + [(24, 128)]
    kinds = [bf16] * 9 + [f32]
    scratch = []
    for lead in ((8, 2), (2,), (2,), (4,), (4,), (3,)):
        scratch += [V(lead + d, t) for d, t in zip(dims, kinds)]
    wide = lambda s: (2, 16 * s[0], s[1])
    scratch += [
        V((8, 2) + shard[4], bf16), V((16 * shard[4][0], 2 * shard[4][1]), bf16), V(wide(shard[2]), bf16),
        V(wide(shard[3]), bf16), V(wide(shard[1]), bf16), V(wide(shard[0]), bf16), V((2, 384, 128), f32),
        V((rows, D), bf16), V((D, rows), bf16), V((2, rows, BLK), bf16), V((2, rows, BLK), bf16),
        V((rows, D), f32), V((rows, D), f32), V((rows, D), bf16), V((D, rows), bf16), V((rows, 3 * D), bf16),
        *[V((rows, BLK), bf16)] * 6, V((shape.padded, BLK), f32), V((shape.padded, BLK), f32),
        V((rows, 2 * BLK), bf16), V((rows, BLK), f32),
    ]
    scratch += [V((m, m), bf16) for m in (short, short, long, long)]
    scratch += [V((8, 32 * widths[0]), f32), V((16, 32 * widths[1]), f32), V((8, 32 * widths[2]), f32)]
    sem = pltpu.SemaphoreType.DMA
    scratch += [sem((10, 31)), sem((10, 23)), sem((8, 2)), sem((36,)), sem((2, 2)), sem((6,)), sem((2,))]
    return pl.pallas_call(
        functools.partial(backward_kernel, shape, widths),
        out_shape=outs,
        in_specs=in_specs,
        out_specs=[any_] * 4 + [vm] * 6,
        scratch_shapes=scratch,
        compiler_params=pltpu.CompilerParams(collective_id=1, has_side_effects=True, vmem_limit_bytes=67043328),
    )(*ins)


def finish_kernel(spans, *refs):
    n = 9
    small, bulk = refs[0], refs[1 : 1 + n]
    outs = refs[1 + n : 1 + 2 * n]
    smalls = refs[1 + 2 * n : 1 + 2 * n + len(spans)]
    bufs = refs[1 + 2 * n + len(spans) : 1 + 3 * n + len(spans)]
    sem = refs[-1]
    ins = [pltpu.make_async_copy(a, b, sem.at[0, k]) for k, (a, b) in enumerate(zip(bulk, bufs))]
    for copy in ins:
        copy.start()
    for (first, count, width), ref in zip(spans, smalls):
        ref[...] = small[first : first + count, 0:width]
    back = [pltpu.make_async_copy(a, b, sem.at[1, k]) for k, (a, b) in enumerate(zip(bufs, outs))]
    for one, two in zip(ins, back):
        one.wait()
        two.start()
    for copy in back:
        copy.wait()


def finish(small, bulk, shards):
    spans = []
    first = 0
    for i in SMALL:
        s = shards[i].shape
        count = s[0] if len(s) == 2 else 1
        spans.append((first, count, s[-1]))
        first += count
    S = jax.ShapeDtypeStruct
    any_ = pl.BlockSpec(memory_space=pl.ANY)
    vm = pl.BlockSpec(memory_space=pltpu.VMEM)
    made = pl.pallas_call(
        functools.partial(finish_kernel, spans),
        out_shape=[S(a.shape, a.dtype) for a in bulk] + [S((c, w), f32) for _, c, w in spans],
        in_specs=[vm] + [any_] * len(bulk),
        out_specs=[any_] * len(bulk) + [vm] * len(spans),
        scratch_shapes=[pltpu.VMEM(a.shape, a.dtype) for a in bulk] + [pltpu.SemaphoreType.DMA((2, len(bulk)))],
    )(small, *bulk)
    grads = {i: v.reshape(shards[i].shape) for i, v in zip(SMALL, made[len(bulk) :])}
    return made[: len(bulk)], grads


def ring_step(ts, tl, cs, cl, shards):
    f = forward(ts, tl, cs, cl, shards)
    b = backward(ts, tl, cs, cl, shards, f[0:5], f[5:8], f[8:20] + f[24:27], f[20:24])
    bulk, grads = finish(b[9], b[:9], shards)
    for i, g in zip(LARGE, bulk[4:9]):
        grads[i] = g
    seqs = (ts, tl, ts, tl)
    return tuple(v.reshape(s.shape) for v, s in zip(bulk, seqs)) + tuple(grads[i] for i in range(16))


def table(length):
    half = length // 2
    t = np.arange(length)
    k = np.arange(half)
    ang = 2.0 * np.pi * (np.outer(k, t) % length) / length
    top = np.cos(ang)
    low = -np.sin(ang)
    low[0] = np.where(t % 2 == 0, 1.0, -1.0)
    return (np.concatenate([top, low]) / math.sqrt(length)).astype(np.float32)

def dft(form, tab, v):
    return jnp.einsum(form, jnp.asarray(tab, bf16), v.astype(bf16), preferred_element_type=f32)

def down(v): return jnp.pad(v[:, :-1], ((0,0),(1,0),(0,0)))
def up(v): return jnp.pad(v[:, 1:], ((0,0),(0,1),(0,0)))
def conv(v, k): return k[0]*down(v)+k[1]*v+k[2]*up(v)
def conv_back(g, k): return k[0]*up(g)+k[1]*g+k[2]*down(g)
def conv_kernel(g, v):
    return jnp.stack([jnp.sum(g*down(v),(0,1)), jnp.sum(g*v,(0,1)), jnp.sum(g*up(v),(0,1))])

def weights(length):
    half = length//2
    w = np.full((half,1),2.0,np.float32); w[0]=1.0
    return np.concatenate([w,w])

def mixer_fwd(proj, sk, ck, fg):
    D = ck.shape[1]; L = proj.shape[1]; H=L//2
    tab = table(L); w = weights(L)
    co = conv(proj, sk)
    gl, gr, va = co[:,:,:D], co[:,:,D:2*D], co[:,:,2*D:]
    cond = conv(va, ck)
    spec = dft("kt,btc->bkc", tab, cond)
    carr = dft("kt,btc->bkc", tab, gr*va)
    th = jnp.tanh(spec*fg[0]); filt = th*fg[1]
    first = (lax.broadcasted_iota(jnp.int32,(H,1),0)==0)
    fa, fb, ca, cb = filt[:,:H], filt[:,H:], carr[:,:H], carr[:,H:]
    pa = fa*ca - jnp.where(first,0.0,fb*cb)
    pb = jnp.where(first, fb*cb, fa*cb+fb*ca)
    prod = jnp.concatenate([pa,pb],1)*w
    longc = dft("kt,bkc->btc", tab, prod)
    return gl*longc, (co, spec, th, carr, longc)

def mixer_bwd(dmix, proj, res, sk, ck, fg):
    co, spec, th, carr, longc = res
    D = ck.shape[1]; L = proj.shape[1]; H=L//2
    tab = table(L); w = weights(L)
    gl, gr, va = co[:,:,:D], co[:,:,D:2*D], co[:,:,2*D:]
    dgl = dmix*longc
    dlong = dmix*gl
    dp = dft("kt,btc->bkc", tab, dlong)*w
    filt = th*fg[1]
    first = (lax.broadcasted_iota(jnp.int32,(H,1),0)==0)
    fa, fb, ca, cb = filt[:,:H], filt[:,H:], carr[:,:H], carr[:,H:]
    da, db = dp[:,:H], dp[:,H:]
    dfa = da*ca + jnp.where(first,0.0,db*cb)
    dfb = jnp.where(first, db*cb, db*ca-da*cb)
    dca = da*fa + jnp.where(first,0.0,db*fb)
    dcb = jnp.where(first, db*fb, db*fa-da*fb)
    df = jnp.concatenate([dfa,dfb],1); dc = jnp.concatenate([dca,dcb],1)
    dth = df*fg[1]*(1-th*th)
    dfg = jnp.stack([jnp.sum(dth*spec,(0,1)), jnp.sum(df*th,(0,1))])
    dcond = dft("kt,bkc->btc", tab, dth*fg[0])
    dgv = dft("kt,bkc->btc", tab, dc)
    dck = conv_kernel(dcond, va)
    dva = conv_back(dcond, ck) + dgv*gr
    dgr = dgv*va
    dco = jnp.concatenate([dgl,dgr,dva],2)
    dsk = conv_kernel(dco, proj)
    return conv_back(dco, sk), dsk, dck, dfg

def mm(a,b): return jnp.dot(a,b,preferred_element_type=f32)
def tn(a,b): return lax.dot_general(a,b,(((0,),(0,)),((),())),preferred_element_type=f32)
def nt(a,b): return lax.dot_general(a,b,(((1,),(1,)),((),())),preferred_element_type=f32)

def norm(v):
    m = jnp.mean(v,-1,keepdims=True); d = v-m
    r = lax.rsqrt(jnp.mean(d*d,-1,keepdims=True)+1e-5)
    return d*r, r

def norm_back(e, h, r):
    return r*(e-jnp.mean(e,-1,keepdims=True)-h*jnp.mean(e*h,-1,keepdims=True))

C0=math.sqrt(2/math.pi); C1=0.044715
def gelu_parts(g):
    t = jnp.tanh(C0*(g+C1*g*g*g))
    return 0.5*g*(1+t), 0.5*(1+t)+0.5*g*(1-t*t)*C0*(1+3*C1*g*g)

def local(ts, tl, P, cs, cl):
    (iw, ib, sk, ck, fg, ow, ob, g1, b1, g2, b2, gw, uw, gb, dw, db) = [p if i in (0,5,11,12,14) else p.astype(f32) for i,p in enumerate(P)]
    D = ow.shape[0]
    ns = ts.shape[0]*ts.shape[1]
    x = jnp.concatenate([ts.reshape(-1,D),tl.reshape(-1,D)]).astype(f32)
    c = jnp.concatenate([cs.reshape(-1,D),cl.reshape(-1,D)])
    h1, r1 = norm(x)
    n1 = (h1*g1+b1).astype(bf16)
    proj = mm(n1, iw)+ib
    ps, pl_ = proj[:ns].reshape(ts.shape[0],ts.shape[1],3*D), proj[ns:].reshape(tl.shape[0],tl.shape[1],3*D)
    ms, rs = mixer_fwd(ps, sk, ck, fg); ml, rl = mixer_fwd(pl_, sk, ck, fg)
    mixed = jnp.concatenate([ms.reshape(-1,D),ml.reshape(-1,D)]).astype(bf16)
    hid = x + mm(mixed, ow)+ob
    h2, r2 = norm(hid)
    n2 = (h2*g2+b2).astype(bf16)
    gp = mm(n2,gw)+gb[0]; up_ = mm(n2,uw)+gb[1]
    ge, gd = gelu_parts(gp)
    ga = (ge*up_).astype(bf16)
    out = (hid+mm(ga,dw)+db).astype(bf16)
    cf = c.astype(f32)
    d_db = jnp.sum(cf,0); d_dw = tn(ga,c)
    dg = nt(c,dw)
    dgate = (dg*up_*gd).astype(bf16); dup=(dg*ge).astype(bf16)
    d_gb = jnp.stack([jnp.sum(dgate.astype(f32),0),jnp.sum(dup.astype(f32),0)])
    d_gw = tn(n2,dgate); d_uw = tn(n2,dup)
    dn2 = nt(dgate,gw)+nt(dup,uw)
    d_g2 = jnp.sum(dn2*h2,0); d_b2=jnp.sum(dn2,0)
    dh = cf + norm_back(dn2*g2,h2,r2)
    gm = dh.astype(bf16)
    d_ob = jnp.sum(gm.astype(f32),0); d_ow = tn(mixed,gm)
    dm = nt(gm,ow)
    dps, a1,a2,a3 = mixer_bwd(dm[:ns].reshape(ts.shape), ps, rs, sk, ck, fg)
    dpl, e1,e2,e3 = mixer_bwd(dm[ns:].reshape(tl.shape), pl_, rl, sk, ck, fg)
    gpj = jnp.concatenate([dps.reshape(-1,3*D),dpl.reshape(-1,3*D)]).astype(bf16)
    d_ib = jnp.sum(gpj.astype(f32),0); d_iw = tn(n1,gpj)
    dn1 = nt(gpj,iw)
    d_g1=jnp.sum(dn1*h1,0); d_b1=jnp.sum(dn1,0)
    dx = dh + norm_back(dn1*g1,h1,r1)
    return (out[:ns].reshape(ts.shape), out[ns:].reshape(tl.shape), dx[:ns].reshape(ts.shape), dx[ns:].reshape(tl.shape),
        d_iw,d_ib,a1+e1,a2+e2,a3+e3,d_ow,d_ob,d_g1,d_b1,d_g2,d_b2,d_gw,d_uw,d_gb,d_dw,d_db)


def fetch_plain(shards):
    params = []
    for i, shard in enumerate(shards):
        if i in LARGE:
            wide = lax.all_gather(shard, "narrow", axis=1, tiled=True)
            params.append(lax.all_gather(wide, "wide", axis=0, tiled=True))
        else:
            params.append(
                lax.all_gather(shard, ("wide", "narrow"), axis=shard.ndim - 1, tiled=True)
            )
    return params


def reduce_plain(grads, shards):
    outs = []
    for i, grad in enumerate(grads):
        if i in LARGE:
            block = lax.psum_scatter(grad.astype(bf16), "wide", scatter_dimension=0, tiled=True)
            block = lax.psum_scatter(block, "narrow", scatter_dimension=1, tiled=True)
            outs.append(block.astype(f32))
        else:
            outs.append(
                lax.psum_scatter(
                    grad, ("wide", "narrow"), scatter_dimension=grad.ndim - 1, tiled=True
                )
            )
    return outs


def plain_step(ts, tl, cs, cl, shards):
    results = local(ts, tl, fetch_plain(shards), cs, cl)
    return tuple(results[:4]) + tuple(reduce_plain(results[4:], shards))


def body(ring, ts, tl, *rest):
    step = ring_step if ring and ts.shape[0] == 1 and tl.shape[0] == 1 else plain_step
    return step(ts, tl, rest[16], rest[17], list(rest[:16]))


def solution(mesh):
    ring = mesh.shape["wide"] == 16 and mesh.shape["narrow"] == 2
    seq = P(("wide", "narrow"), None, None)
    mat = P("wide", "narrow")
    vec = P(("wide", "narrow"))
    pair = P(None, ("wide", "narrow"))
    params = (mat, vec, pair, pair, pair, mat, vec, vec, vec, vec, vec, mat, mat, pair, mat, vec)
    return jax.shard_map(
        functools.partial(body, ring),
        mesh=mesh,
        in_specs=(seq, seq) + params + (seq, seq),
        out_specs=(seq, seq, seq, seq) + params,
        check_vma=False,
    )
```

```python
import functools
import math

import jax
import jax.numpy as jnp
import numpy as np
from jax import lax
from jax.experimental import pallas as pl
from jax.experimental.pallas import tpu as pltpu
from jax.sharding import PartitionSpec as P

bf16 = jnp.bfloat16
f32 = jnp.float32
MESH = pl.DeviceIdType.MESH
Z = 4
D = 768
BLK = 256
PAD = 8


def coords():
    w = lax.axis_index("wide")
    return w // 4, (w // 2) % 2, w % 2, lax.axis_index("narrow")


def flat(z, x, c):
    return (z * 2 + x) * 2 + c


def greet(peers):
    barrier = pltpu.get_barrier_semaphore()
    for peer in peers:
        pl.semaphore_signal(barrier, inc=1, device_id=peer, device_id_type=MESH)
    pl.semaphore_wait(barrier, len(peers))


def neighbours():
    z, x, c, y = coords()
    zpeers = [(flat(lax.rem(z + i, Z), x, c), y) for i in (1, 2, 3)]
    return zpeers, (flat(z, 1 - x, c), y), (flat(z, x, c), 1 - y), (flat(z, x, 1 - c), y)


class Gather:
    def __init__(self, items, ici_send, ici_recv, core_send, core_recv, own_sem):
        self.items = items
        self.ici_send, self.ici_recv = ici_send, ici_recv
        self.core_send, self.core_recv, self.own_sem = core_send, core_recv, own_sem
        self.z, self.x, self.c, self.y = coords()
        self.zpeers, self.xpeer, self.ypeer, self.cpeer = neighbours()
        self.count = [0] * len(items)
        self.pending = []

    def shard(self, k):
        ref, _, first, cols = self.items[k]
        return ref if cols == ref.shape[1] else ref.at[:, first : first + cols]

    def view(self, k, i, xf, yf, cf=0):
        ref, full, first, cols = self.items[k]
        zz = lax.rem(self.z + i, Z)
        xx = 1 - self.x if xf else self.x
        yy = 1 - self.y if yf else self.y
        cc = 1 - self.c if cf else self.c
        rows, whole = ref.shape
        row = pl.multiple_of(flat(zz, xx, cc) * rows, 16)
        return full.at[pl.ds(row, rows), pl.ds(pl.multiple_of(yy * whole + first, 128), cols)]

    def copy(self, k, src, dst, peer, send, recv):
        return pltpu.make_async_remote_copy(
            src_ref=src, dst_ref=dst, send_sem=send, recv_sem=recv, device_id=peer, device_id_type=MESH
        )

    def post(self, k, i, xf, yf, peer, send, recv):
        src = self.shard(k) if (i, xf, yf) == (0, 0, 0) else self.view(k, i, xf, yf)
        self.pending.append((k, send))
        self.copy(k, src, self.view(k, i, xf, yf), peer, self.sent(k, send), recv).start()

    def sent(self, k, send):
        return (self.core_send if send[0] else self.ici_send).at[k, send[1]]

    def send(self, k, i, xf, yf, peer, slot):
        self.post(k, i, xf, yf, peer, (0, self.count[k]), self.ici_recv.at[k, slot])
        self.count[k] += 1

    def to_core(self, k, i, xf, yf):
        slot = i * 4 + xf * 2 + yf
        self.post(k, i, xf, yf, self.cpeer, (1, slot), self.core_recv.at[k, slot])

    def arrived(self, k, i, xf, yf, cf=0):
        slot = i * 4 + xf * 2 + yf
        sems = self.core_recv if cf else self.ici_recv
        dst = self.view(k, i, xf, yf, cf)
        self.copy(k, self.shard(k), dst, self.cpeer, self.ici_send.at[k, 0], sems.at[k, slot]).wait_recv()

    def own(self, k):
        return pltpu.make_async_copy(self.shard(k), self.view(k, 0, 0, 0), self.own_sem.at[k])

    def start(self, k):
        self.own(k).start()
        for i in (1, 3, 2):
            self.send(k, 0, 0, 0, self.zpeers[i - 1], ((Z - i) % Z) * 4)
        self.send(k, 0, 0, 0, self.xpeer, 2)
        self.send(k, 0, 0, 0, self.ypeer, 1)
        self.to_core(k, 0, 0, 0)

    def events(self, order):
        out = []
        for kind, k in order:
            if kind == "S":
                out.append(functools.partial(self.start, k))
            elif kind == "z":
                out += [functools.partial(self.zstep, k, i) for i in (1, 3, 2)]
            elif kind == "p":
                out += [functools.partial(self.xystep, k, i, xf) for i in (0, 1, 3, 2) for xf in (1, 0)]
            else:
                out += [functools.partial(self.dstep, k, i) for i in (0, 1, 3, 2)]
        return out

    def zstep(self, k, i):
        self.arrived(k, i, 0, 0)
        self.send(k, i, 0, 0, self.xpeer, i * 4 + 2)
        self.send(k, i, 0, 0, self.ypeer, i * 4 + 1)
        self.to_core(k, i, 0, 0)

    def xystep(self, k, i, xf):
        self.arrived(k, i, xf, 1 - xf)
        if i % 2 == 1 - xf:
            self.send(k, i, xf, 1 - xf, self.ypeer if xf else self.xpeer, i * 4 + 3)
        self.to_core(k, i, xf, 1 - xf)

    def dstep(self, k, i):
        self.arrived(k, i, 1, 1)
        self.to_core(k, i, 1, 1)

    def done(self, k):
        self.own(k).wait()
        for i in range(4):
            for xf in range(2):
                for yf in range(2):
                    self.arrived(k, i, xf, yf, 1)

    def finish(self):
        for k, send in self.pending:
            dst = self.view(k, 0, 0, 0)
            self.copy(k, self.shard(k), dst, self.cpeer, self.sent(k, send), self.ici_recv.at[k, 0]).wait_send()


def normal(v):
    centred = v - jnp.mean(v, axis=-1, keepdims=True)
    scale = lax.rsqrt(jnp.mean(centred * centred, axis=-1, keepdims=True) + 1e-5)
    return centred * scale, scale


def dot(a, b):
    return jnp.dot(a, b, preferred_element_type=f32)


def dot_nt(a, b):
    return lax.dot_general(a, b, (((1,), (1,)), ((), ())), preferred_element_type=f32)


def fold(v):
    return jnp.sum(v.reshape(v.shape[0] // 8, 8, v.shape[1]), axis=0)


def loop(count, fn):
    def go(i, carry):
        fn(i)
        return carry

    lax.fori_loop(0, count, go, 0)


def rows_at(i, size):
    return pl.ds(pl.multiple_of(i * size, size), size)


GELU_A = math.sqrt(2.0 / math.pi)
GELU_B = 0.044715


class Rows:
    def __init__(self, short, long):
        self.short, self.long = short, long
        self.total = short + long
        self.padded = self.total + 3 * PAD
        self.segs = ((0, short, PAD), (short, long, 2 * PAD + short))
        self.chunk = short
        self.count = self.total // short
        self.half = short // 2

    def plain(self, i):
        return rows_at(i, self.chunk)

    def place(self, i):
        return pl.multiple_of(i * self.chunk + PAD + PAD * jnp.minimum(i, 1), PAD)

    def halves(self, i):
        low = jnp.where(i == 0, 0, self.short + (i - 1) * self.half)
        high = low + jnp.where(i == 0, self.half, self.long // 2)
        return tuple(pl.ds(pl.multiple_of(v, self.half), self.half) for v in (low, high))


def window3(ref, p, n):
    span = ref[pl.ds(pl.multiple_of(p - PAD, PAD), n + 2 * PAD), :]
    return span[PAD - 1 : PAD - 1 + n], span[PAD : PAD + n], span[PAD + 1 : PAD + 1 + n]


def taps3(views, taps, flip=False):
    a, b, c = views
    return taps[0] * (c if flip else a) + taps[1] * b + taps[2] * (a if flip else c)


def owners(width, q):
    row = lax.broadcasted_iota(jnp.int32, (32, D), 0)
    owner = 2 * (row % 16) + row // 16
    col = lax.broadcasted_iota(jnp.int32, (32, D), 1) + q * D - owner * width
    return jnp.logical_and(col >= 0, col < width)


def one_hot(width, q):
    col = lax.broadcasted_iota(jnp.int32, (8, D), 1) + q * D
    whole = jnp.floor((col.astype(f32) + 0.5) * (1.0 / width)).astype(jnp.int32)
    place = (col - whole * width)[0:1]
    hit = lax.broadcasted_iota(jnp.int32, (128, D), 0) == place
    return jnp.where(hit, 1.0, 0.0).astype(bf16)


def unpack(wide_ref, first, count, width, out_ref):
    parts = []
    for r in range(first, first + count):
        for y in range(2):
            parts.append(wide_ref.at[y][pl.ds(r, 16, stride=32), :])
    parts = jnp.concatenate(parts, axis=0).astype(bf16)
    for q in range(32 * width // D):
        spread = dot(parts, one_hot(width, q))
        mine = owners(width, q)
        for r in range(count):
            piece = jnp.where(mine, spread[32 * r : 32 * r + 32], 0.0)
            out_ref[r : r + 1, q * D : (q + 1) * D] = jnp.sum(piece, axis=0, keepdims=True)


def repack(vec, count, width, first, out_ref):
    out = None
    for q in range(32 * width // D):
        mine = owners(width, q)
        highs, lows = [], []
        for r in range(count):
            v = jnp.where(mine, vec[r : r + 1, q * D : (q + 1) * D], 0.0)
            high = v.astype(bf16)
            highs.append(high)
            lows.append((v - high.astype(f32)).astype(bf16))
        value = dot_nt(jnp.concatenate(highs + lows, axis=0), one_hot(width, q))
        out = value if out is None else out + value
    n = 32 * count
    for r in range(count):
        v = out[32 * r : 32 * r + 32] + out[n + 32 * r : n + 32 * r + 32]
        for y in range(2):
            out_ref.at[y][pl.ds(first + r, 16, stride=24), :] = v[16 * y : 16 * y + 16]


STEP = 16


def angle_parts(length):
    t = np.arange(length)
    coarse = 2.0 * np.pi * (np.outer(STEP * np.arange(length // 2 // STEP), t) % length) / length
    fine = 2.0 * np.pi * (np.outer(np.arange(STEP), t) % length) / length
    scale = 1.0 / math.sqrt(length)
    parts = [np.cos(coarse) * scale, np.sin(coarse) * scale, np.cos(fine), np.sin(fine)]
    return np.concatenate(parts).astype(np.float32)


def build_table(parts_ref, out_ref):
    length = out_ref.shape[0]
    n = length // 2 // STEP
    fine_cos, fine_sin = parts_ref[2 * n : 2 * n + STEP], parts_ref[2 * n + STEP : 2 * n + 2 * STEP]
    row = lax.broadcasted_iota(jnp.int32, (STEP, length), 0)
    sign = 1.0 - 2.0 * (lax.broadcasted_iota(jnp.int32, (STEP, length), 1) % 2).astype(f32)
    for i in range(n):
        cos, sin = parts_ref[i : i + 1], parts_ref[n + i : n + i + 1]
        low = -(sin * fine_cos + cos * fine_sin)
        if i == 0:
            low = jnp.where(row == 0, sign / math.sqrt(length), low)
        out_ref[i * STEP : (i + 1) * STEP] = (cos * fine_cos - sin * fine_sin).astype(bf16)
        out_ref[length // 2 + i * STEP : length // 2 + (i + 1) * STEP] = low.astype(bf16)


def forward_kernel(shape, widths, *refs):
    (pack, w0, w1, w2, w3, w4, ts, tl, cs, cl, ps, pl_) = refs[:12]
    (g_in, g_out, g_gate, g_up, g_down, v72, v24, v96, o_n1, o_proj, o_spec, o_carr, o_long,
     o_mixed, o_hid, o_n2, o_pd, o_ga, o_ap, o_ge, o_fs, o_fst, o_fl, o_flt, o_gl, o_gr, o_va) = refs[12:39]
    (f_small, f_in, f_out, f_gate, f_up, smallw, x, cot, n1, n1t, proj, spec, carr, longc,
     mixed, mixedt, hid, n2, n2t, ga, ap, ge, pd, pj, gl, vap, rhs, tr, prod, lows, s_ps, s_pl, s_fs, s_fst,
     s_fl, s_flt, ici_send, ici_recv, core_send, core_recv, own_sem, load_sem, save_sem) = refs[39:]
    rows = shape.total
    short = shape.short
    zp, xp, yp, cp = neighbours()
    greet(zp + [xp, yp, cp])
    items = [(pack, f_small), (w0, f_in), (w1, f_out), (w2, f_gate), (w3, f_up), (w4, g_down)]
    g = Gather([(a, b, 0, a.shape[1]) for a, b in items], ici_send, ici_recv, core_send, core_recv, own_sem)
    steps = g.events(GATHER_ORDER)
    marks = {}
    for token in GATHER_ORDER:
        size = {"S": 1, "z": 3, "p": 8, "d": 4}[token[0]]
        marks[token] = size + (max(marks.values()) if marks else 0)
    position = [0]

    def pump(n):
        for step in steps[position[0] : position[0] + n]:
            step()
        position[0] = min(position[0] + n, len(steps))

    def need(k):
        pump(max(0, marks["d", k] - position[0]))
        g.done(k)

    pump(GATHER_FIRST)
    loads = []
    for a, b in [(ps, s_ps), (pl_, s_pl), (ts, x.at[0:short]), (tl, x.at[short:rows]),
                 (cs, cot.at[0:short]), (cl, cot.at[short:rows])]:
        copy = pltpu.make_async_copy(a, b, load_sem.at[len(loads)])
        copy.start()
        loads.append(copy)
    saves = []

    def save(a, b):
        copy = pltpu.make_async_copy(a, b, save_sem.at[len(saves)])
        copy.start()
        saves.append(copy)

    for start, length, place in shape.segs:
        zero = jnp.zeros((PAD, BLK), f32)
        for ref in (pj.at[0], pj.at[1], pj.at[2], vap):
            ref[place - PAD : place] = zero
            ref[place + length : place + length + PAD] = zero
    for copy in loads:
        copy.wait()
    build_table(s_ps, s_fs)
    build_table(s_pl, s_fl)
    pump(6)
    s_fst[...] = s_fs[...].T
    s_flt[...] = s_fl[...].T
    for a, b in ((s_fs, o_fs), (s_fst, o_fst), (s_fl, o_fl), (s_flt, o_flt)):
        save(a, b)
    need(0)
    for y in range(2):
        smallw[y] = f_small[:, y * 128 : (y + 1) * 128].astype(f32)
    unpack(smallw, 0, 4, widths[0], v72)
    pump(2)
    unpack(smallw, 4, 11, widths[1], v24)
    unpack(smallw, 15, 2, widths[2], v96)
    pump(2)

    def norm_one(i):
        r = rows_at(i, 64)
        h, _ = normal(x[r, :].astype(f32))
        n1[r, :] = (h * v24[6:7, :] + v24[7:8, :]).astype(bf16)

    loop(rows // 64, norm_one)
    pump(2)
    n1t[...] = n1[...].T
    save(n1t, o_n1)
    need(1)
    save(f_in, g_in)

    def mix(j, pumps):
        ch = slice(j * BLK, (j + 1) * BLK)
        los = [b * D + j * BLK for b in range(3)]
        tap = [[v72[1 + k : 2 + k, lo : lo + BLK] for k in range(3)] for lo in los]
        ctap = [v24[k : k + 1, ch] for k in range(3)]
        inner, outer = v24[3:4, ch], v24[4:5, ch]
        for b, lo in enumerate(los):
            value = dot(n1[...], f_in[:, lo : lo + BLK]) + v72[0:1, lo : lo + BLK]
            proj[:, lo : lo + BLK] = value.astype(bf16)
            for start, length, place in shape.segs:
                pj[b, place : place + length] = value[start : start + length]
        pump(pumps[0])
        n = shape.chunk

        def convolve(i):
            r, p = shape.plain(i), shape.place(i)
            here = pl.ds(p, n)
            left = taps3(window3(pj.at[0], p, n), tap[0])
            right = taps3(window3(pj.at[1], p, n), tap[1])
            value = taps3(window3(pj.at[2], p, n), tap[2])
            gl[r, :] = left
            vap[here, :] = value
            rhs[r, BLK:] = (right * value).astype(bf16)
            for q, v in enumerate((left, right, value)):
                lows[q, r, ch] = v.astype(bf16)

        def condition(i):
            rhs[shape.plain(i), :BLK] = taps3(window3(vap, shape.place(i), n), ctap).astype(bf16)

        loop(shape.count, convolve)
        loop(shape.count, condition)
        pump(pumps[1])
        for (start, length, _), table in zip(shape.segs, (s_fs, s_fl)):
            tr[start : start + length] = dot(table[...], rhs[start : start + length])

        def filt(i):
            a, b = shape.halves(i)
            sa, sb = tr[a, :BLK], tr[b, :BLK]
            ca, cb = tr[a, BLK:], tr[b, BLK:]
            spec[a, ch] = sa.astype(bf16)
            spec[b, ch] = sb.astype(bf16)
            carr[a, ch] = ca.astype(bf16)
            carr[b, ch] = cb.astype(bf16)
            fa = jnp.tanh(sa * inner) * outer
            fb = jnp.tanh(sb * inner) * outer
            real, imag = fa * ca, fb * cb
            row = lax.broadcasted_iota(jnp.int32, real.shape, 0)
            first = jnp.logical_and(row == 0, i <= 1)
            prod[a, :] = jnp.where(first, real, 2.0 * (real - imag)).astype(bf16)
            prod[b, :] = jnp.where(first, imag, 2.0 * (fa * cb + fb * ca)).astype(bf16)

        loop(shape.count, filt)
        pump(pumps[2])
        for (start, length, _), table in zip(shape.segs, (s_fst, s_flt)):
            value = dot(table[...], prod[start : start + length])
            longc[start : start + length, ch] = value.astype(bf16)
            mixed[start : start + length, ch] = (value * gl[start : start + length]).astype(bf16)

    for j in range(3):
        mix(j, MIX_PUMPS[j])
    for a, b in ((proj, o_proj), (spec, o_spec), (carr, o_carr), (longc, o_long)):
        save(a, b)
    for q, b in enumerate((o_gl, o_gr, o_va)):
        save(lows.at[q], b)
    pump(3)
    mixedt[...] = mixed[...].T
    save(mixedt, o_mixed)
    need(2)
    save(f_out, g_out)

    def branch_one(i):
        r = rows_at(i, 128)
        value = x[r, :].astype(f32) + dot(mixed[r, :], f_out[...]) + v24[5:6, :]
        hid[r, :] = value
        h, _ = normal(value)
        n2[r, :] = (h * v24[8:9, :] + v24[9:10, :]).astype(bf16)

    loop(rows // 128, branch_one)
    save(hid, o_hid)
    n2t[...] = n2[...].T
    save(n2t, o_n2)

    def gate_half(i):
        cols = rows_at(i, BLK)
        for m in range(0, rows, 320):
            gate = dot(n2[m : m + 320, :], f_gate[:, cols]) + v96[0:1, cols]
            square = gate * gate
            t = jnp.tanh(gate * (GELU_A + GELU_A * GELU_B * square))
            half = 0.5 * (1.0 + t)
            slope = half + 0.5 * gate * (1.0 - t * t) * (GELU_A + 3.0 * GELU_A * GELU_B * square)
            ge[m : m + 320, cols] = (gate * half).astype(bf16)
            ap[m : m + 320, cols] = slope.astype(bf16)

    def up_half(i):
        cols = rows_at(i, BLK)
        for m in range(0, rows, 320):
            up = dot(n2[m : m + 320, :], f_up[:, cols]) + v96[1:2, cols]
            ga[m : m + 320, cols] = (ge[m : m + 320, cols].astype(f32) * up).astype(bf16)
            ap[m : m + 320, cols] = (ap[m : m + 320, cols].astype(f32) * up).astype(bf16)
        pd[cols, :] = dot(ga[:, cols].T, cot[...]).astype(bf16)

    def pairs(part):
        return [(ga.at[:, part], o_ga.at[:, part]), (ap.at[:, part], o_ap.at[:, part]), (pd.at[part], o_pd.at[part])]

    def save_first():
        for k, (a, b) in enumerate(pairs(slice(0, pd.shape[0] // 2))):
            pltpu.make_async_copy(a, b, load_sem.at[k]).start()

    tiles = ga.shape[1] // BLK

    def staged(fn, counts, more):
        def tile(i):
            fn(i)
            for q, n in enumerate(counts):
                if n:
                    pl.when(i == q)(functools.partial(pump, n))
            if more:
                pl.when(i == tiles // 2 - 1)(save_first)

        loop(tiles, tile)

    need(3)
    save(f_gate, g_gate)
    staged(gate_half, GATE_PUMPS, False)
    save(ge, o_ge)
    need(4)
    save(f_up, g_up)
    staged(up_half, UP_PUMPS, True)
    half = pd.shape[0] // 2
    for a, b in pairs(slice(half, 2 * half)):
        save(a, b)
    for k, (a, b) in enumerate(pairs(slice(0, half))):
        pltpu.make_async_copy(a, b, load_sem.at[k]).wait()
    need(5)
    for copy in saves:
        copy.wait()
    g.finish()


GATHER_ORDER = (
    ("S", 0), ("S", 1), ("S", 2), ("S", 3), ("z", 0), ("z", 1), ("p", 0), ("d", 0), ("z", 2), ("p", 1), ("d", 1),
    ("z", 3), ("p", 2), ("S", 4), ("d", 2), ("p", 3), ("z", 4), ("S", 5), ("d", 3), ("p", 4), ("z", 5), ("d", 4),
    ("p", 5), ("d", 5),
)
GATHER_FIRST = 4
MIX_PUMPS = ((3, 3, 3), (4, 4, 4), (5, 5, 5))
GATE_PUMPS = (0, 2, 0, 2, 0, 2, 0, 2, 0, 2, 0, 2)
UP_PUMPS = (0, 2, 0, 2, 0, 2, 0, 2, 0, 2, 0, 2)


def place_rows(piece, first):
    rows, width = piece.shape
    return lax.pad(piece, jnp.zeros((), piece.dtype), ((first, 32 - first - rows, 0), (0, 128 - width, 0)))


LARGE = (0, 5, 11, 12, 14)
SMALL = (1, 2, 3, 4, 6, 7, 8, 9, 10, 15, 13)


def pack_small(shards):
    total = None
    first = 0
    for i in SMALL:
        piece = shards[i].reshape(-1, shards[i].shape[-1])
        placed = place_rows(piece, first)
        first += piece.shape[0]
        total = placed if total is None else total + placed
    return total


def forward(ts, tl, cs, cl, shards):
    shape = Rows(ts.shape[1], tl.shape[1])
    short, long, rows = shape.short, shape.long, shape.total
    widths = (shards[1].shape[0], shards[6].shape[0], shards[13].shape[1])
    large = [shards[i] for i in LARGE]
    ff = shards[11].shape[1] * 2
    full = [(16 * s.shape[0], 2 * s.shape[1]) for s in large]
    S = jax.ShapeDtypeStruct
    V = pltpu.VMEM
    angles = [angle_parts(short), angle_parts(long)]
    ins = [pack_small(shards)] + large + [ts.reshape(short, D), tl.reshape(long, D)]
    ins += [cs.reshape(short, D), cl.reshape(long, D)] + [jnp.asarray(a) for a in angles]
    square = [(n, n) for n in (short, short, long, long)]
    vecs = [(8, 32 * widths[0]), (16, 32 * widths[1]), (8, 32 * widths[2])]
    outs = [S(s, bf16) for s in full] + [S(s, f32) for s in vecs]
    outs += [S((D, rows), bf16), S((rows, 3 * D), bf16)] + [S((rows, D), bf16)] * 3
    outs += [S((D, rows), bf16), S((rows, D), f32), S((D, rows), bf16), S((ff, D), bf16)]
    outs += [S((rows, ff), bf16)] * 3 + [S(s, bf16) for s in square] + [S((rows, D), bf16)] * 3
    any_ = pl.BlockSpec(memory_space=pl.ANY)
    vm = pl.BlockSpec(memory_space=pltpu.VMEM)
    sem = pltpu.SemaphoreType.DMA
    scratch = [V((512, 256), bf16)] + [V(s, bf16) for s in full[:4]]
    scratch += [V((2, 512, 128), f32), V((rows, D), bf16), V((rows, D), bf16), V((rows, D), bf16), V((D, rows), bf16)]
    scratch += [V((rows, 3 * D), bf16)] + [V((rows, D), bf16)] * 4
    scratch += [V((D, rows), bf16), V((rows, D), f32), V((rows, D), bf16), V((D, rows), bf16)]
    scratch += [V((rows, ff), bf16)] * 3 + [V((ff, D), bf16)]
    scratch += [V((3, shape.padded, BLK), f32), V((rows, BLK), f32), V((shape.padded, BLK), f32)]
    scratch += [V((rows, 2 * BLK), bf16), V((rows, 2 * BLK), f32), V((rows, BLK), bf16), V((3, rows, D), bf16)]
    scratch += [V(a.shape, f32) for a in angles] + [V(s, bf16) for s in square]
    scratch += [sem((6, 15)), sem((6, 16)), sem((6, 16)), sem((6, 16)), sem((6,)), sem((6,)), sem((28,))]
    return pl.pallas_call(
        functools.partial(forward_kernel, shape, widths),
        out_shape=outs,
        in_specs=[any_] * len(ins),
        out_specs=[any_] * 5 + [vm] * 3 + [any_] * 19,
        scratch_shapes=scratch,
        compiler_params=pltpu.CompilerParams(collective_id=0, has_side_effects=True, vmem_limit_bytes=67043328),
    )(*ins)


class Reduce:
    def __init__(self, items, send_sem, recv_sem, own_sem):
        self.items = items
        self.send_sem, self.recv_sem, self.own_sem = send_sem, recv_sem, own_sem
        self.z, self.x, self.c, self.y = coords()
        self.zpeers, self.xpeer, self.ypeer, self.cpeer = neighbours()
        self.count = [0] * len(items)
        self.pending = []

    def post(self, k, src, dst, peer, slot):
        copy = pltpu.make_async_remote_copy(
            src_ref=src,
            dst_ref=dst,
            send_sem=self.send_sem.at[k, self.count[k]],
            recv_sem=self.recv_sem.at[k, slot],
            device_id=peer,
            device_id_type=MESH,
        )
        self.pending.append((k, self.count[k]))
        self.count[k] += 1
        copy.start()

    def arrived(self, k, dst, slot):
        pltpu.make_async_remote_copy(
            src_ref=dst,
            dst_ref=dst,
            send_sem=self.send_sem.at[k, 0],
            recv_sem=self.recv_sem.at[k, slot],
            device_id=self.cpeer,
            device_id_type=MESH,
        ).wait_recv()

    def part(self, k, b, core, yy):
        item = self.items[k]
        start = (2 * b + core) * item["rows"] + item["base"]
        rows = pl.ds(pl.multiple_of(start, 8), item["rows"])
        if item["flat"]:
            cols = item["cols"]
            return item["source"].at[rows, pl.ds(pl.multiple_of(yy * cols, 128), cols)]
        return item["source"].at[yy, rows, pl.ds(item["first"], item["cols"])]

    def own(self, k, b, yy):
        held = self.items[k]["held"]
        return held.at[b, yy] if held is not None else self.part(k, b, self.c, yy)

    def block(self, i, xx):
        return lax.rem(self.z + i, Z) * 2 + xx

    def order(self):
        for i in (1, 3, 2, 0):
            yield i, self.block(i, 1 - self.x), self.block(i, self.x)

    def core(self, k):
        item = self.items[k]
        for i, across, along in self.order():
            for b in (across, along):
                for yy in range(2):
                    self.post(k, self.part(k, b, 1 - self.c, yy), item["core"].at[b, yy], self.cpeer, b)
        if item["held"] is not None:
            for i, across, along in self.order():
                for b in (across, along):
                    for yy in range(2):
                        pltpu.make_async_copy(
                            self.part(k, b, self.c, yy), item["held"].at[b, yy], self.own_sem.at[b, yy]
                        ).start()

    def merge(self, k, b):
        item = self.items[k]
        if item["held"] is not None:
            for yy in range(2):
                pltpu.make_async_copy(
                    self.part(k, b, self.c, yy), item["held"].at[b, yy], self.own_sem.at[b, yy]
                ).wait()
        self.arrived(k, item["core"].at[b], b)
        for yy in range(2):
            own = self.own(k, b, yy)
            own[...] = own[...] + item["core"][b, yy]

    def diag(self, k):
        item = self.items[k]
        for i, across, along in self.order():
            self.merge(k, across)
            src = self.own(k, across, 1 - self.y)
            if i % 2 == 0:
                self.post(k, src, item["diag_x"].at[i // 2], self.xpeer, 8 + i // 2)
            else:
                self.post(k, src, item["diag_y"].at[i // 2], self.ypeer, 10 + i // 2)
        for i, across, along in self.order():
            self.merge(k, along)

    def near(self, k):
        item = self.items[k]
        for i, across, along in self.order():
            own = self.own(k, along, 1 - self.y)
            if i % 2 == 0:
                self.arrived(k, item["diag_x"].at[i // 2], 8 + i // 2)
                own[...] = own[...] + item["diag_x"][i // 2]
            self.post(k, own, item["near_y"].at[i], self.ypeer, 12 + i)
            own = self.own(k, across, self.y)
            if i % 2 == 1:
                self.arrived(k, item["diag_y"].at[i // 2], 10 + i // 2)
                own[...] = own[...] + item["diag_y"][i // 2]
            self.post(k, own, item["near_x"].at[i], self.xpeer, 16 + i)

    def far(self, k):
        item = self.items[k]
        for i, across, along in self.order():
            self.arrived(k, item["near_x"].at[i], 16 + i)
            self.arrived(k, item["near_y"].at[i], 12 + i)
            own = self.own(k, along, self.y)
            total = own[...].astype(f32) + item["near_x"][i].astype(f32) + item["near_y"][i].astype(f32)
            own[...] = total.astype(own.dtype)
            if i:
                self.post(k, own, item["far"].at[i - 1], self.zpeers[i - 1], 19 + i)

    def last(self, k):
        item = self.items[k]
        total = self.own(k, self.block(0, self.x), self.y)[...].astype(f32)
        for i in range(3):
            self.arrived(k, item["far"].at[i], 20 + i)
            total = total + item["far"][i].astype(f32)
        item["out"][...] = total

    def finish(self):
        for k, count in self.pending:
            rest = self.items[k]["far"].at[0]
            pltpu.make_async_remote_copy(
                src_ref=rest,
                dst_ref=rest,
                send_sem=self.send_sem.at[k, count],
                recv_sem=self.recv_sem.at[k, 0],
                device_id=self.cpeer,
                device_id_type=MESH,
            ).wait_send()


def backward_kernel(shape, widths, *refs):
    (pd, h_g, h_u, h_d, h_o, h_i, ts, tl, cs, cl, v72, v24, r_n1, r_proj, r_spec, r_carr, r_long,
     r_mixed, r_hid, r_n2, r_ga, r_ap, r_ge, fs, fst, fl, flt, r_gl, r_gr, r_va) = refs[:30]
    y_s, y_l, o_s, o_l, o_in, o_out, o_gate, o_up, o_down, o_small = refs[30:40]
    nitem = 10
    groups = [refs[40 + q * nitem : 40 + (q + 1) * nitem] for q in range(6)]
    (held, wd, wg, wu, wo, wi, p_small, cot, n2t, apb, geb, acc, big, gm, mixedt, gpj, bspec, bcarr, blong, bgl, bgr, bva,
     dco, dcp, rhs, tr, s_fs, s_fst, s_fl, s_flt, g72, g24, g96,
     send_sem, recv_sem, own_sem, load_sem, tile_sem, blk_sem, out_sem) = refs[40 + 6 * nitem :]
    rows, short = shape.total, shape.short
    zp, xp, yp, cp = neighbours()
    greet(zp + [xp, yp, cp])

    def item(k, source, out, nrows, cols, first=0, base=0, flat_form=False, held=None):
        names = ("core", "diag_x", "diag_y", "near_x", "near_y", "far")
        made = dict(source=source, out=out, rows=nrows, cols=cols, first=first, base=base, flat=flat_form, held=held)
        made.update({name: group[k] for name, group in zip(names, groups)})
        return made

    half = wg.shape[2] // 2
    span = wi.shape[2] // 3
    n = wi.shape[1]
    r_gate, r_in = o_gate.shape[0], o_in.shape[0]
    items = [
        item(0, pd, o_down, o_down.shape[0], o_down.shape[1], flat_form=True, held=held),
        item(1, wg, o_gate.at[:, 0:half], r_gate, half),
        item(2, wu, o_up.at[:, 0:half], r_gate, half),
        item(3, wg, o_gate.at[:, half : 2 * half], r_gate, half, first=half),
        item(4, wu, o_up.at[:, half : 2 * half], r_gate, half, first=half),
        item(5, wo, o_out, o_out.shape[0], o_out.shape[1]),
    ]
    for t in range(3):
        out = o_in.at[:, t * span : (t + 1) * span]
        items.append(item(6 + t, wd, out, r_in, span, base=t * n, flat_form=True))
    items.append(item(9, p_small, o_small, o_small.shape[0], o_small.shape[1]))
    red = Reduce(items, send_sem, recv_sem, own_sem)
    red.core(0)
    loads = {}

    def load(name, a, b):
        copy = pltpu.make_async_copy(a, b, load_sem.at[len(loads)])
        copy.start()
        loads[name] = copy

    def wait(*names):
        for name in names:
            loads[name].wait()

    def halves(name, a, b, first, size):
        cols = b.shape[2]
        for y in range(2):
            lo = y * cols + first
            load(name + str(y), a.at[:, lo : lo + size], b.at[y, :, first : first + size])

    load("cs", cs, cot.at[0:short])
    load("cl", cl, cot.at[short:rows])
    load("n2t", r_n2, n2t)
    quarter = wd.shape[0] // 4
    for q in (0, 2):
        load("wd%d" % q, h_d.at[q * quarter : (q + 1) * quarter], wd.at[q * quarter : (q + 1) * quarter])
    halves("ga", h_g, wg, 0, half)
    halves("ua", h_u, wu, 0, half)
    per = 2 * (half // BLK)
    total_tiles = 2 * per

    def tile_start(i):
        h, t, y = i // per, lax.rem(i, per) // 2, lax.rem(i, 2)
        return h * half + t * BLK, y

    def tile_copy(i, which):
        first, y = tile_start(i)
        cols = pl.ds(pl.multiple_of(y * 2 * half + first, BLK), BLK)
        slot = lax.rem(i, 2)
        src, dst = ((r_ap, apb), (r_ge, geb))[which]
        return pltpu.make_async_copy(src.at[:, cols], dst.at[slot], tile_sem.at[which, slot])

    for which in range(2):
        tile_copy(0, which).start()
    for q in (1, 3):
        load("wd%d" % q, h_d.at[q * quarter : (q + 1) * quarter], wd.at[q * quarter : (q + 1) * quarter])
    halves("gb", h_g, wg, half, half)
    halves("ub", h_u, wu, half, half)
    load("hid", r_hid, big)
    wide3 = gpj.shape[1]
    load("ga_a", r_ga.at[:, 0:wide3], gpj)
    load("ga_b", r_ga.at[:, wide3:], gm)
    load("mixedt", r_mixed, mixedt)
    halves("wo", h_o, wo, 0, wo.shape[2])
    halves("wi", h_i, wi, 0, wi.shape[2])
    for name, a, b in (("fs", fs, s_fs), ("fst", fst, s_fst), ("fl", fl, s_fl), ("flt", flt, s_flt)):
        load(name, a, b)

    blocks = ((r_spec, bspec), (r_carr, bcarr), (r_long, blong), (r_gl, bgl), (r_gr, bgr), (r_va, bva))

    def block_copies(j, first, last):
        ch = slice(j * BLK, (j + 1) * BLK)
        return [
            pltpu.make_async_copy(blocks[k][0].at[:, ch], blocks[k][1], blk_sem.at[k]) for k in range(first, last)
        ]

    for copy in block_copies(0, 0, 6):
        copy.start()
    acc[...] = jnp.zeros_like(acc)
    zero = jnp.zeros((PAD, BLK), f32)
    for start, length, place in shape.segs:
        for ref in (dco, dcp):
            ref[place - PAD : place] = zero
            ref[place + length : place + length + PAD] = zero
    g24[...] = jnp.zeros_like(g24)
    p_small[...] = jnp.zeros_like(p_small)
    red.diag(0)
    wait("cs", "cl", "n2t", "wd0", "wd2", "ga0", "ga1", "ua0", "ua1")

    def glu_back(i):
        first, y = tile_start(i)
        slot = lax.rem(i, 2)

        @pl.when(i + 1 < total_tiles)
        def _():
            for which in range(2):
                tile_copy(i + 1, which).start()

        for which in range(2):
            tile_copy(i, which).wait()
        cols = pl.ds(pl.multiple_of(first, BLK), BLK)
        every = pl.ds(pl.multiple_of(y * 2 * half + first, BLK), BLK)
        d_act = dot_nt(cot[...], wd[every, :])
        d_gate = (d_act * apb[slot].astype(f32)).astype(bf16)
        d_up = (d_act * geb[slot].astype(f32)).astype(bf16)
        g96[0:1, every] = jnp.sum(fold(d_gate.astype(f32)), axis=0, keepdims=True)
        g96[1:2, every] = jnp.sum(fold(d_up.astype(f32)), axis=0, keepdims=True)
        for m in range(0, rows, 320):
            acc[m : m + 320] += dot_nt(d_gate[m : m + 320], wg[y, :, cols]) + dot_nt(d_up[m : m + 320], wu[y, :, cols])
        wg[y, :, cols] = dot(n2t[...], d_gate).astype(bf16)
        wu[y, :, cols] = dot(n2t[...], d_up).astype(bf16)

    def tile_range(first, steps):
        def tile(i):
            glu_back(i + first)
            for q, step in steps.items():
                pl.when(i == q)(step)

        loop(per, tile)

    def both(*steps):
        def run():
            for name, k in steps:
                getattr(red, name)(k)

        return run

    tile_range(0, {2: both(("near", 0))})
    red.core(1)
    red.core(2)
    wait("wd1", "wd3", "gb0", "gb1", "ub0", "ub1")
    tile_range(per, {2: both(("diag", 1), ("diag", 2))})
    red.core(3)
    red.core(4)
    red.near(1)
    wait("hid", "ga_a", "ga_b")

    def branch_two(i):
        r = rows_at(i, 128)
        value = dot(gpj[r, :], wd[0:wide3, :]) + dot(gm[r, :], wd[wide3:, :])
        gm[r, :] = (big[r, :] + value + v24[10:11, :]).astype(bf16)

    loop(rows // 128, branch_two)
    outs = [
        pltpu.make_async_copy(gm.at[0:short], y_s, out_sem.at[0]),
        pltpu.make_async_copy(gm.at[short:rows], y_l, out_sem.at[1]),
    ]
    for copy in outs:
        copy.start()
    load("proj", r_proj, gpj)
    red.near(2)
    red.far(0)
    red.diag(3)
    red.diag(4)
    for copy in outs:
        copy.wait()

    def norm_two(i):
        r = rows_at(i, 64)
        h, scale = normal(big[r, :])
        d_norm = acc[r, :]
        c = cot[r, :].astype(f32)
        e = d_norm * v24[8:9, :]
        d_hid = c + scale * (e - jnp.mean(e, -1, keepdims=True) - h * jnp.mean(e * h, -1, keepdims=True))
        low = d_hid.astype(bf16)
        acc[r, :] = d_hid
        gm[r, :] = low
        for row, v in ((8, d_norm * h), (9, d_norm), (10, c), (5, low.astype(f32))):
            g24[row : row + 1, :] += jnp.sum(fold(v), axis=0, keepdims=True)

    loop(rows // 64, norm_two)
    wait("mixedt", "wo0", "wo1")
    wide = wo.shape[2]

    def out_back(i):
        r = rows_at(i, 128)
        big[r, :] = dot_nt(gm[r, 0:wide], wo[0]) + dot_nt(gm[r, wide : 2 * wide], wo[1])

    loop(rows // 128, out_back)
    for y in range(2):
        wo[y] = dot(mixedt[...], gm[:, y * wide : (y + 1) * wide]).astype(bf16)
    red.core(5)
    load("n1t", r_n1, n2t)
    load("ts", ts, gm.at[0:short])
    load("tl", tl, gm.at[short:rows])
    red.far(1)
    wait("proj", "fs", "fst", "fl", "flt")
    size = shape.chunk

    def mix_back(j, pumps):
        ch = slice(j * BLK, (j + 1) * BLK)
        los = [b * D + j * BLK for b in range(3)]
        tap = [[v72[1 + k : 2 + k, lo : lo + BLK] for k in range(3)] for lo in los]
        ctap = [v24[k : k + 1, ch] for k in range(3)]
        inner, outer = v24[3:4, ch], v24[4:5, ch]
        for copy in block_copies(j, 0, 4):
            copy.wait()

        def gates(i):
            r = shape.plain(i)
            d_mix = big[r, ch]
            rhs[r, :BLK] = (d_mix * bgl[r, :].astype(f32)).astype(bf16)
            dco[pl.ds(shape.place(i), size), :] = d_mix * blong[r, :].astype(f32)

        loop(shape.count, gates)

        def conv_down(b):
            def go(i, sums):
                r, p = shape.plain(i), shape.place(i)
                views = window3(dco, p, size)
                low = taps3(views, tap[b], True).astype(bf16)
                given = gpj[r, los[b] : los[b] + BLK].astype(f32)
                gpj[r, los[b] : los[b] + BLK] = low
                parts = [low.astype(f32)] + [views[2 - k] * given for k in range(3)]
                return tuple(s + fold(v) for s, v in zip(sums, parts))

            sums = lax.fori_loop(0, shape.count, go, (jnp.zeros((8, BLK), f32),) * 4)
            for k in range(4):
                g72[k : k + 1, los[b] : los[b] + BLK] = jnp.sum(sums[k], axis=0, keepdims=True)

        for (start, length, _), table in zip(shape.segs, (s_fs, s_fl)):
            tr[start : start + length] = dot(table[...], rhs[start : start + length, :BLK])
        conv_down(0)
        pumps[0]()

        def filt_back(i, sums):
            a, b = shape.halves(i)
            pa, pb = tr[a, :], tr[b, :]
            sa, sb = bspec[a, :].astype(f32), bspec[b, :].astype(f32)
            ca, cb = bcarr[a, :].astype(f32), bcarr[b, :].astype(f32)
            ta, tb = jnp.tanh(sa * inner), jnp.tanh(sb * inner)
            fa, fb = ta * outer, tb * outer
            first = jnp.logical_and(lax.broadcasted_iota(jnp.int32, pa.shape, 0) == 0, i <= 1)
            pa = jnp.where(first, pa, 2.0 * pa)
            pb = jnp.where(first, pb, 2.0 * pb)
            ra, rb = pa * ca, pb * cb
            ua, ub = pa * fa, pb * fb
            dfa = jnp.where(first, ra, ra + rb)
            dfb = jnp.where(first, rb, pb * ca - pa * cb)
            rhs[a, BLK:] = jnp.where(first, ua, ua + ub).astype(bf16)
            rhs[b, BLK:] = jnp.where(first, ub, pb * fa - pa * fb).astype(bf16)
            dta, dtb = dfa * outer * (1.0 - ta * ta), dfb * outer * (1.0 - tb * tb)
            rhs[a, :BLK] = (dta * inner).astype(bf16)
            rhs[b, :BLK] = (dtb * inner).astype(bf16)
            return sums[0] + fold(dta * sa + dtb * sb), sums[1] + fold(dfa * ta + dfb * tb)

        sums = lax.fori_loop(0, shape.count, filt_back, (jnp.zeros((8, BLK), f32),) * 2)
        for k in range(2):
            g24[3 + k : 4 + k, ch] = jnp.sum(sums[k], axis=0, keepdims=True)
        if j < 2:
            for copy in block_copies(j + 1, 0, 4):
                copy.start()
        for copy in block_copies(j, 4, 6):
            copy.wait()
        for (start, length, place), table in zip(shape.segs, (s_fst, s_flt)):
            dcp[place : place + length] = dot(table[...], rhs[start : start + length, :BLK])
            tr[start : start + length] = dot(table[...], rhs[start : start + length, BLK:])
        pumps[1]()

        def right(i):
            here = pl.ds(shape.place(i), size)
            r = shape.plain(i)
            dco[here, :] = tr[r, :] * bva[r, :].astype(f32)

        loop(shape.count, right)
        conv_down(1)

        def value(i, sums):
            r, p = shape.plain(i), shape.place(i)
            views = window3(dcp, p, size)
            dco[pl.ds(p, size), :] = taps3(views, ctap, True) + tr[r, :] * bgr[r, :].astype(f32)
            given = bva[r, :].astype(f32)
            return tuple(s + fold(views[2 - k] * given) for k, s in enumerate(sums))

        sums = lax.fori_loop(0, shape.count, value, (jnp.zeros((8, BLK), f32),) * 3)
        for k in range(3):
            g24[k : k + 1, ch] = jnp.sum(sums[k], axis=0, keepdims=True)
        if j < 2:
            for copy in block_copies(j + 1, 4, 6):
                copy.start()
        conv_down(2)
        pumps[2]()

    none = lambda: None
    mix_back(0, [none, both(("diag", 5)), both(("far", 2))])
    mix_back(1, [both(("near", 3)), both(("near", 4)), none])
    mix_back(2, [none, none, none])
    wait("n1t", "wi0", "wi1")

    def in_weight(i):
        t, y = i // 2, lax.rem(i, 2)
        cols = pl.ds(pl.multiple_of((3 * y + t) * span, 128), span)
        there = pl.ds(pl.multiple_of(y * span, 128), span)
        wd[rows_at(t, n), there] = dot(n2t[...], gpj[:, cols]).astype(bf16)
        for q, step in IN_STEPS.items():
            pl.when(i == q)(both(*step))

    loop(6, in_weight)
    deep = wi.shape[2]

    def in_back(i):
        r = rows_at(i, 128)
        big[r, :] = dot_nt(gpj[r, 0:deep], wi[0]) + dot_nt(gpj[r, deep : 2 * deep], wi[1])
        for q, step in BACK_STEPS.items():
            pl.when(i == q)(both(*step))

    loop(rows // 128, in_back)
    wait("ts", "tl")

    def norm_one(i):
        r = rows_at(i, 64)
        h, scale = normal(gm[r, :].astype(f32))
        d_norm = big[r, :]
        e = d_norm * v24[6:7, :]
        acc[r, :] += scale * (e - jnp.mean(e, -1, keepdims=True) - h * jnp.mean(e * h, -1, keepdims=True))
        for row, v in ((6, d_norm * h), (7, d_norm)):
            g24[row : row + 1, :] += jnp.sum(fold(v), axis=0, keepdims=True)

    loop(rows // 64, norm_one)
    outs = [
        pltpu.make_async_copy(acc.at[0:short], o_s, out_sem.at[0]),
        pltpu.make_async_copy(acc.at[short:rows], o_l, out_sem.at[1]),
    ]
    for copy in outs:
        copy.start()
    red.far(5)
    red.near(6)
    repack(g72, 4, widths[0], 0, p_small)
    red.near(7)
    repack(g24, 11, widths[1], 4, p_small)
    repack(g96, 2, widths[2], 15, p_small)
    red.core(9)
    both(*TAIL_STEPS)()
    for copy in outs:
        copy.wait()
    red.finish()


IN_STEPS = {
    1: (("core", 6), ("near", 5)),
    3: (("core", 7), ("far", 3)),
    5: (("core", 8), ("diag", 6)),
}
BACK_STEPS = {1: (("diag", 7),), 4: (("diag", 8), ("far", 4))}
TAIL_STEPS = (
    ("near", 8), ("diag", 9), ("far", 6), ("near", 9), ("far", 7), ("far", 8), ("far", 9),
    ("last", 0), ("last", 1), ("last", 2), ("last", 3), ("last", 4), ("last", 5), ("last", 6), ("last", 7), ("last", 8), ("last", 9),
)


def backward(ts, tl, cs, cl, shards, weights, vecs, res, tables):
    shape = Rows(ts.shape[1], tl.shape[1])
    short, long, rows = shape.short, shape.long, shape.total
    widths = (shards[1].shape[0], shards[6].shape[0], shards[13].shape[1])
    S = jax.ShapeDtypeStruct
    V = pltpu.VMEM
    w_in, w_out, w_gate, w_up, w_down = weights
    n1t, proj, spec, carr, longc, mixedt, hid, n2t, pd, ga, ap, ge = res[:12]
    ins = [pd, w_gate, w_up, w_down, w_out, w_in, ts.reshape(short, D), tl.reshape(long, D), cs.reshape(short, D),
           cl.reshape(long, D), vecs[0], vecs[1], n1t, proj, spec, carr, longc, mixedt, hid, n2t, ga, ap, ge]
    ins += list(tables) + list(res[12:])
    any_ = pl.BlockSpec(memory_space=pl.ANY)
    vm = pl.BlockSpec(memory_space=pltpu.VMEM)
    in_specs = [any_] * 10 + [vm] * 2 + [any_] * 18
    shard = [shards[i].shape for i in LARGE]
    outs = [S((short, D), bf16), S((long, D), bf16), S((short, D), f32), S((long, D), f32)]
    outs += [S(s, f32) for s in shard] + [S((24, 128), f32)]
    half, span = shard[2][1] // 2, shard[0][1] // 3
    dims = [shard[4]] + [(shard[2][0], half)] * 4 + [shard[1]] + [(shard[0][0], span)] * 3 + [(24, 128)]
    kinds = [bf16] * 9 + [f32]
    scratch = []
    for lead in ((8, 2), (2,), (2,), (4,), (4,), (3,)):
        scratch += [V(lead + d, t) for d, t in zip(dims, kinds)]
    wide = lambda s: (2, 16 * s[0], s[1])
    scratch += [
        V((8, 2) + shard[4], bf16), V((16 * shard[4][0], 2 * shard[4][1]), bf16), V(wide(shard[2]), bf16),
        V(wide(shard[3]), bf16), V(wide(shard[1]), bf16), V(wide(shard[0]), bf16), V((2, 384, 128), f32),
        V((rows, D), bf16), V((D, rows), bf16), V((2, rows, BLK), bf16), V((2, rows, BLK), bf16),
        V((rows, D), f32), V((rows, D), f32), V((rows, D), bf16), V((D, rows), bf16), V((rows, 3 * D), bf16),
        *[V((rows, BLK), bf16)] * 6, V((shape.padded, BLK), f32), V((shape.padded, BLK), f32),
        V((rows, 2 * BLK), bf16), V((rows, BLK), f32),
    ]
    scratch += [V((m, m), bf16) for m in (short, short, long, long)]
    scratch += [V((8, 32 * widths[0]), f32), V((16, 32 * widths[1]), f32), V((8, 32 * widths[2]), f32)]
    sem = pltpu.SemaphoreType.DMA
    scratch += [sem((10, 31)), sem((10, 23)), sem((8, 2)), sem((36,)), sem((2, 2)), sem((6,)), sem((2,))]
    return pl.pallas_call(
        functools.partial(backward_kernel, shape, widths),
        out_shape=outs,
        in_specs=in_specs,
        out_specs=[any_] * 4 + [vm] * 6,
        scratch_shapes=scratch,
        compiler_params=pltpu.CompilerParams(collective_id=1, has_side_effects=True, vmem_limit_bytes=67043328),
    )(*ins)


def finish_kernel(spans, *refs):
    n = 9
    small, bulk = refs[0], refs[1 : 1 + n]
    outs = refs[1 + n : 1 + 2 * n]
    smalls = refs[1 + 2 * n : 1 + 2 * n + len(spans)]
    bufs = refs[1 + 2 * n + len(spans) : 1 + 3 * n + len(spans)]
    sem = refs[-1]
    ins = [pltpu.make_async_copy(a, b, sem.at[0, k]) for k, (a, b) in enumerate(zip(bulk, bufs))]
    for copy in ins:
        copy.start()
    for (first, count, width), ref in zip(spans, smalls):
        ref[...] = small[first : first + count, 0:width]
    back = [pltpu.make_async_copy(a, b, sem.at[1, k]) for k, (a, b) in enumerate(zip(bufs, outs))]
    for one, two in zip(ins, back):
        one.wait()
        two.start()
    for copy in back:
        copy.wait()


def finish(small, bulk, shards):
    spans = []
    first = 0
    for i in SMALL:
        s = shards[i].shape
        count = s[0] if len(s) == 2 else 1
        spans.append((first, count, s[-1]))
        first += count
    S = jax.ShapeDtypeStruct
    any_ = pl.BlockSpec(memory_space=pl.ANY)
    vm = pl.BlockSpec(memory_space=pltpu.VMEM)
    made = pl.pallas_call(
        functools.partial(finish_kernel, spans),
        out_shape=[S(a.shape, a.dtype) for a in bulk] + [S((c, w), f32) for _, c, w in spans],
        in_specs=[vm] + [any_] * len(bulk),
        out_specs=[any_] * len(bulk) + [vm] * len(spans),
        scratch_shapes=[pltpu.VMEM(a.shape, a.dtype) for a in bulk] + [pltpu.SemaphoreType.DMA((2, len(bulk)))],
    )(small, *bulk)
    grads = {i: v.reshape(shards[i].shape) for i, v in zip(SMALL, made[len(bulk) :])}
    return made[: len(bulk)], grads


def ring_step(ts, tl, cs, cl, shards):
    f = forward(ts, tl, cs, cl, shards)
    b = backward(ts, tl, cs, cl, shards, f[0:5], f[5:8], f[8:20] + f[24:27], f[20:24])
    bulk, grads = finish(b[9], b[:9], shards)
    for i, g in zip(LARGE, bulk[4:9]):
        grads[i] = g
    seqs = (ts, tl, ts, tl)
    return tuple(v.reshape(s.shape) for v, s in zip(bulk, seqs)) + tuple(grads[i] for i in range(16))


def table(length):
    half = length // 2
    t = np.arange(length)
    k = np.arange(half)
    ang = 2.0 * np.pi * (np.outer(k, t) % length) / length
    top = np.cos(ang)
    low = -np.sin(ang)
    low[0] = np.where(t % 2 == 0, 1.0, -1.0)
    return (np.concatenate([top, low]) / math.sqrt(length)).astype(np.float32)

def dft(form, tab, v):
    return jnp.einsum(form, jnp.asarray(tab, bf16), v.astype(bf16), preferred_element_type=f32)

def down(v): return jnp.pad(v[:, :-1], ((0,0),(1,0),(0,0)))
def up(v): return jnp.pad(v[:, 1:], ((0,0),(0,1),(0,0)))
def conv(v, k): return k[0]*down(v)+k[1]*v+k[2]*up(v)
def conv_back(g, k): return k[0]*up(g)+k[1]*g+k[2]*down(g)
def conv_kernel(g, v):
    return jnp.stack([jnp.sum(g*down(v),(0,1)), jnp.sum(g*v,(0,1)), jnp.sum(g*up(v),(0,1))])

def weights(length):
    half = length//2
    w = np.full((half,1),2.0,np.float32); w[0]=1.0
    return np.concatenate([w,w])

def mixer_fwd(proj, sk, ck, fg):
    D = ck.shape[1]; L = proj.shape[1]; H=L//2
    tab = table(L); w = weights(L)
    co = conv(proj, sk)
    gl, gr, va = co[:,:,:D], co[:,:,D:2*D], co[:,:,2*D:]
    cond = conv(va, ck)
    spec = dft("kt,btc->bkc", tab, cond)
    carr = dft("kt,btc->bkc", tab, gr*va)
    th = jnp.tanh(spec*fg[0]); filt = th*fg[1]
    first = (lax.broadcasted_iota(jnp.int32,(H,1),0)==0)
    fa, fb, ca, cb = filt[:,:H], filt[:,H:], carr[:,:H], carr[:,H:]
    pa = fa*ca - jnp.where(first,0.0,fb*cb)
    pb = jnp.where(first, fb*cb, fa*cb+fb*ca)
    prod = jnp.concatenate([pa,pb],1)*w
    longc = dft("kt,bkc->btc", tab, prod)
    return gl*longc, (co, spec, th, carr, longc)

def mixer_bwd(dmix, proj, res, sk, ck, fg):
    co, spec, th, carr, longc = res
    D = ck.shape[1]; L = proj.shape[1]; H=L//2
    tab = table(L); w = weights(L)
    gl, gr, va = co[:,:,:D], co[:,:,D:2*D], co[:,:,2*D:]
    dgl = dmix*longc
    dlong = dmix*gl
    dp = dft("kt,btc->bkc", tab, dlong)*w
    filt = th*fg[1]
    first = (lax.broadcasted_iota(jnp.int32,(H,1),0)==0)
    fa, fb, ca, cb = filt[:,:H], filt[:,H:], carr[:,:H], carr[:,H:]
    da, db = dp[:,:H], dp[:,H:]
    dfa = da*ca + jnp.where(first,0.0,db*cb)
    dfb = jnp.where(first, db*cb, db*ca-da*cb)
    dca = da*fa + jnp.where(first,0.0,db*fb)
    dcb = jnp.where(first, db*fb, db*fa-da*fb)
    df = jnp.concatenate([dfa,dfb],1); dc = jnp.concatenate([dca,dcb],1)
    dth = df*fg[1]*(1-th*th)
    dfg = jnp.stack([jnp.sum(dth*spec,(0,1)), jnp.sum(df*th,(0,1))])
    dcond = dft("kt,bkc->btc", tab, dth*fg[0])
    dgv = dft("kt,bkc->btc", tab, dc)
    dck = conv_kernel(dcond, va)
    dva = conv_back(dcond, ck) + dgv*gr
    dgr = dgv*va
    dco = jnp.concatenate([dgl,dgr,dva],2)
    dsk = conv_kernel(dco, proj)
    return conv_back(dco, sk), dsk, dck, dfg

def mm(a,b): return jnp.dot(a,b,preferred_element_type=f32)
def tn(a,b): return lax.dot_general(a,b,(((0,),(0,)),((),())),preferred_element_type=f32)
def nt(a,b): return lax.dot_general(a,b,(((1,),(1,)),((),())),preferred_element_type=f32)

def norm(v):
    m = jnp.mean(v,-1,keepdims=True); d = v-m
    r = lax.rsqrt(jnp.mean(d*d,-1,keepdims=True)+1e-5)
    return d*r, r

def norm_back(e, h, r):
    return r*(e-jnp.mean(e,-1,keepdims=True)-h*jnp.mean(e*h,-1,keepdims=True))

C0=math.sqrt(2/math.pi); C1=0.044715
def gelu_parts(g):
    t = jnp.tanh(C0*(g+C1*g*g*g))
    return 0.5*g*(1+t), 0.5*(1+t)+0.5*g*(1-t*t)*C0*(1+3*C1*g*g)

def local(ts, tl, P, cs, cl):
    (iw, ib, sk, ck, fg, ow, ob, g1, b1, g2, b2, gw, uw, gb, dw, db) = [p if i in (0,5,11,12,14) else p.astype(f32) for i,p in enumerate(P)]
    D = ow.shape[0]
    ns = ts.shape[0]*ts.shape[1]
    x = jnp.concatenate([ts.reshape(-1,D),tl.reshape(-1,D)]).astype(f32)
    c = jnp.concatenate([cs.reshape(-1,D),cl.reshape(-1,D)])
    h1, r1 = norm(x)
    n1 = (h1*g1+b1).astype(bf16)
    proj = mm(n1, iw)+ib
    ps, pl_ = proj[:ns].reshape(ts.shape[0],ts.shape[1],3*D), proj[ns:].reshape(tl.shape[0],tl.shape[1],3*D)
    ms, rs = mixer_fwd(ps, sk, ck, fg); ml, rl = mixer_fwd(pl_, sk, ck, fg)
    mixed = jnp.concatenate([ms.reshape(-1,D),ml.reshape(-1,D)]).astype(bf16)
    hid = x + mm(mixed, ow)+ob
    h2, r2 = norm(hid)
    n2 = (h2*g2+b2).astype(bf16)
    gp = mm(n2,gw)+gb[0]; up_ = mm(n2,uw)+gb[1]
    ge, gd = gelu_parts(gp)
    ga = (ge*up_).astype(bf16)
    out = (hid+mm(ga,dw)+db).astype(bf16)
    cf = c.astype(f32)
    d_db = jnp.sum(cf,0); d_dw = tn(ga,c)
    dg = nt(c,dw)
    dgate = (dg*up_*gd).astype(bf16); dup=(dg*ge).astype(bf16)
    d_gb = jnp.stack([jnp.sum(dgate.astype(f32),0),jnp.sum(dup.astype(f32),0)])
    d_gw = tn(n2,dgate); d_uw = tn(n2,dup)
    dn2 = nt(dgate,gw)+nt(dup,uw)
    d_g2 = jnp.sum(dn2*h2,0); d_b2=jnp.sum(dn2,0)
    dh = cf + norm_back(dn2*g2,h2,r2)
    gm = dh.astype(bf16)
    d_ob = jnp.sum(gm.astype(f32),0); d_ow = tn(mixed,gm)
    dm = nt(gm,ow)
    dps, a1,a2,a3 = mixer_bwd(dm[:ns].reshape(ts.shape), ps, rs, sk, ck, fg)
    dpl, e1,e2,e3 = mixer_bwd(dm[ns:].reshape(tl.shape), pl_, rl, sk, ck, fg)
    gpj = jnp.concatenate([dps.reshape(-1,3*D),dpl.reshape(-1,3*D)]).astype(bf16)
    d_ib = jnp.sum(gpj.astype(f32),0); d_iw = tn(n1,gpj)
    dn1 = nt(gpj,iw)
    d_g1=jnp.sum(dn1*h1,0); d_b1=jnp.sum(dn1,0)
    dx = dh + norm_back(dn1*g1,h1,r1)
    return (out[:ns].reshape(ts.shape), out[ns:].reshape(tl.shape), dx[:ns].reshape(ts.shape), dx[ns:].reshape(tl.shape),
        d_iw,d_ib,a1+e1,a2+e2,a3+e3,d_ow,d_ob,d_g1,d_b1,d_g2,d_b2,d_gw,d_uw,d_gb,d_dw,d_db)


def fetch_plain(shards):
    params = []
    for i, shard in enumerate(shards):
        if i in LARGE:
            wide = lax.all_gather(shard, "narrow", axis=1, tiled=True)
            params.append(lax.all_gather(wide, "wide", axis=0, tiled=True))
        else:
            params.append(
                lax.all_gather(shard, ("wide", "narrow"), axis=shard.ndim - 1, tiled=True)
            )
    return params


def reduce_plain(grads, shards):
    outs = []
    for i, grad in enumerate(grads):
        if i in LARGE:
            block = lax.psum_scatter(grad.astype(bf16), "wide", scatter_dimension=0, tiled=True)
            block = lax.psum_scatter(block, "narrow", scatter_dimension=1, tiled=True)
            outs.append(block.astype(f32))
        else:
            outs.append(
                lax.psum_scatter(
                    grad, ("wide", "narrow"), scatter_dimension=grad.ndim - 1, tiled=True
                )
            )
    return outs


def plain_step(ts, tl, cs, cl, shards):
    results = local(ts, tl, fetch_plain(shards), cs, cl)
    return tuple(results[:4]) + tuple(reduce_plain(results[4:], shards))


def body(ring, ts, tl, *rest):
    step = ring_step if ring and ts.shape[0] == 1 and tl.shape[0] == 1 else plain_step
    return step(ts, tl, rest[16], rest[17], list(rest[:16]))


def solution(mesh):
    ring = mesh.shape["wide"] == 16 and mesh.shape["narrow"] == 2
    seq = P(("wide", "narrow"), None, None)
    mat = P("wide", "narrow")
    vec = P(("wide", "narrow"))
    pair = P(None, ("wide", "narrow"))
    params = (mat, vec, pair, pair, pair, mat, vec, vec, vec, vec, vec, mat, mat, pair, mat, vec)
    return jax.shard_map(
        functools.partial(body, ring),
        mesh=mesh,
        in_specs=(seq, seq) + params + (seq, seq),
        out_specs=(seq, seq, seq, seq) + params,
        check_vma=False,
    )
```
